32 devices in a mesh: rep: 4 (over y, core), fsdp: 8 (over z, x).
Axes of the slice: x: 2, y: 2, z: 4, core: 2. Of those that a mesh axis runs over, the one named last changes fastest.
Arguments:
- visual: bfloat16 [32, 128, 768], P(('rep', 'fsdp')), may hold values from -6 to 6
- text: bfloat16 [32, 1280, 768], P(('rep', 'fsdp')), may hold values from -6 to 6
- visual_valid: int32 [32, 128], P(('rep', 'fsdp')), may hold values from 0 to 1, as said below
- block_owner: int32 [32, 1280], P(('rep', 'fsdp')), may hold values from 0 to 127, as said below
- cross_query: bfloat16 [768, 768], P('fsdp'), may hold values from -0.21875 to 0.21875
- cross_keyval: bfloat16 [768, 1536], P('fsdp'), may hold values from -0.21875 to 0.21875
- cross_output: bfloat16 [768, 768], P('fsdp'), may hold values from -0.625 to 0.625
- gate_weight: bfloat16 [1536, 768], P('fsdp'), may hold values from -0.15625 to 0.15625
- self_qkv: bfloat16 [768, 2304], P('fsdp'), may hold values from -0.21875 to 0.21875
- self_output: bfloat16 [768, 768], P('fsdp'), may hold values from -0.875 to 0.875
- ffn_up: bfloat16 [768, 3072], P('fsdp'), may hold values from -0.21875 to 0.21875
- ffn_down: bfloat16 [3072, 768], P('fsdp'), may hold values from -0.109375 to 0.109375
- norm_gains: float32 [3072], P('fsdp'), may hold values from 0.5 to 1.5
- norm_biases: float32 [3072], P('fsdp'), may hold values from -1.8 to 1.8
- cotangent: bfloat16 [32, 128, 768], P(('rep', 'fsdp')), may hold values from -6 to 6
Outputs:
- layer_out: bfloat16 [32, 128, 768], P(('rep', 'fsdp'))
- grad_visual: float32 [32, 128, 768], P(('rep', 'fsdp'))
- grad_text: float32 [32, 1280, 768], P(('rep', 'fsdp'))
- grad_cross_query: float32 [768, 768], P('fsdp')
- grad_cross_keyval: float32 [768, 1536], P('fsdp')
- grad_cross_output: float32 [768, 768], P('fsdp')
- grad_gate_weight: float32 [1536, 768], P('fsdp')
- grad_self_qkv: float32 [768, 2304], P('fsdp')
- grad_self_output: float32 [768, 768], P('fsdp')
- grad_ffn_up: float32 [768, 3072], P('fsdp')
- grad_ffn_down: float32 [3072, 768], P('fsdp')
- grad_norm_gains: float32 [3072], P('fsdp')
- grad_norm_biases: float32 [3072], P('fsdp')
The draws below stay inside these ranges and needn't reach their ends.
Inputs may be any that keep to these rules, and one draw needn't show every extreme that they name: `visual_valid`: in every page the real visual blocks come first and the padded ones last; each page has at least a quarter of 128 real blocks and at least one padded block. `block_owner`: each visual block of a page owns exactly 10 of that page's text blocks.
All inputs are finite; a program needn't handle non-finite values.
Results may differ from the reference program's by a relative error of at most 0.04.
Values may be sent and summed in bfloat16 or wider, within the bound.
No kernel may reach another device: no remote copies, remote signals or barrier semaphores. Data moves between devices by JAX's collectives and lax.ppermute only.
A program may use at most 192 MiB of HBM per device.

```python
import jax
import jax.numpy as jnp
from jax import lax

D = 768
H = 12
HD = 64
FF = 3072
VIS = 128
TXT_PER = 10
TXT = 1280
PAGES = 32


def draw_visual_valid(key, part):
    counts = jax.random.randint(key, (PAGES, 1), VIS // 4, VIS)
    return (jnp.arange(VIS, dtype=jnp.int32)[None, :] < counts).astype(jnp.int32)


def draw_block_owner(key, part):
    page_keys = jax.random.split(jax.random.fold_in(key, 7), PAGES)
    shuffled = jax.vmap(lambda subkey: jax.random.permutation(subkey, TXT))(page_keys)
    return (shuffled // TXT_PER).astype(jnp.int32)


def steps_of(key, dims, shards, least, largest):
    factor_of, own = 1.0, jax.random.fold_in(key, 6)
    for axis_at, shards_of in shards:
        heights = jnp.exp(jax.random.uniform(jax.random.fold_in(own, axis_at), (shards_of,), jnp.float32, least / len(shards), largest / len(shards)))
        factor_of = factor_of * jnp.repeat(heights, dims[axis_at] // shards_of).reshape([-1 if axis == axis_at else 1 for axis in range(len(dims))])
    return factor_of


def scatter_about(key, dims, deviation, reach, cuts=(), held_as=jnp.bfloat16):
    array = jax.random.normal(key, dims, jnp.float32) * deviation
    if len(cuts) > 0:
        array = steps_of(key, dims, cuts, -0.22, 0.18) * array
    return jnp.clip(array, min=-reach, max=reach).astype(held_as)


def setup_inputs(seed: int = 0) -> dict:
    splits = jax.random.split(jax.random.key(seed), 16)
    visual = scatter_about(splits[0], (PAGES, VIS, D), 1.0, 6.0, ((0, 32),))
    text = scatter_about(splits[1], (PAGES, TXT, D), 1.0, 6.0, ((0, 32),))
    visual_valid = draw_visual_valid(jax.random.fold_in(splits[15], 71), 0)
    block_owner = draw_block_owner(jax.random.fold_in(splits[15], 71), 0)
    cross_query = scatter_about(splits[4], (D, D), D ** -0.5, 0.21875, ((0, 8),))
    cross_keyval = scatter_about(splits[5], (D, 2 * D), D ** -0.5, 0.21875, ((0, 8),))
    cross_output = scatter_about(splits[6], (D, D), (D // 8) ** -0.5, 0.625, ((0, 8),))
    gate_weight = scatter_about(splits[7], (2 * D, D), (2 * D) ** -0.5, 0.15625, ((0, 8),))
    self_qkv = scatter_about(splits[8], (D, 3 * D), D ** -0.5, 0.21875, ((0, 8),))
    self_output = scatter_about(splits[9], (D, D), (D // 16) ** -0.5, 0.875, ((0, 8),))
    ffn_up = scatter_about(splits[10], (D, FF), D ** -0.5, 0.21875, ((0, 8),))
    ffn_down = scatter_about(splits[11], (FF, D), FF ** -0.5, 0.109375, ((0, 8),))
    norm_gains = jnp.clip(1.0 + 0.1 * jax.random.normal(splits[12], (4 * D,), jnp.float32), 0.5, 1.5)
    norm_biases = scatter_about(splits[13], (4 * D,), 0.3, 1.8, ((0, 8),), jnp.float32)
    cotangent = scatter_about(splits[14], (PAGES, VIS, D), 1.0, 6.0, ((0, 32),))
    return {"visual": visual, "text": text, "visual_valid": visual_valid, "block_owner": block_owner, "cross_query": cross_query, "cross_keyval": cross_keyval, "cross_output": cross_output, "gate_weight": gate_weight, "self_qkv": self_qkv, "self_output": self_output, "ffn_up": ffn_up, "ffn_down": ffn_down, "norm_gains": norm_gains, "norm_biases": norm_biases, "cotangent": cotangent}


@jax.custom_vjp
def low(v):
    return lax.optimization_barrier(v.astype(jnp.bfloat16)).astype(jnp.float32)

@jax.custom_vjp
def low_back(v):
    return v

def low_keep(v):
    return (low(v), None)

def low_pass(kept, grad):
    return (grad,)

def back_keep(v):
    return (v, None)

def back_low(kept, grad):
    return (low(grad),)
low.defvjp(low_keep, low_pass)
low_back.defvjp(back_keep, back_low)
epsilon = 1e-05
filtered_logits = -1000000000.0
shared_sheet_reward = 6.0
highest = lax.Precision.HIGHEST

def layer_norm(inputs, gain_row, bias_row):
    row_mean = lax.optimization_barrier(jnp.mean(inputs, -1, keepdims=True))
    centred = inputs - row_mean
    variance = lax.optimization_barrier(jnp.mean(centred * centred, -1, keepdims=True))
    return centred * lax.rsqrt(variance + epsilon) * gain_row + bias_row

def matmul(left, right):
    return jnp.dot(left, right, precision=highest)

def attend(queries, key_rows, value_rows, score_bias):
    query_count = queries.shape[0]
    head_queries = queries.reshape(query_count, H, HD)
    head_keys = key_rows.reshape(key_rows.shape[0], H, HD)
    head_values = value_rows.reshape(value_rows.shape[0], H, HD)
    scores = jnp.einsum('qhe,khe->hqk', head_queries, head_keys, precision=highest) * HD ** (-0.5) + score_bias[None]
    weighting = jax.nn.softmax(scores, axis=-1)
    mixed_rows = jnp.einsum('hqk,khe->qhe', low(weighting), head_values, precision=highest)
    return mixed_rows.reshape(query_count, H * HD)

def forward(visual_rows, text_rows, params, valid_row, parent_sheet_entry):
    cross_query, cross_keyval, cross_output, gate_weight, self_qkv, self_output, ffn_up, ffn_down, norm_gains, norm_biases = params
    gain_rows = norm_gains.reshape(4, D)
    biases = norm_biases.reshape(4, D)
    normed = low(layer_norm(visual_rows, gain_rows[0], biases[0]))
    text_normed = low(layer_norm(text_rows, gain_rows[1], biases[1]))
    queries = low(low_back(matmul(normed, cross_query)))
    keyval = low(low_back(matmul(text_normed, cross_keyval)))
    word_locations = jnp.arange(VIS, dtype=jnp.int32)
    word_unit_present = valid_row[parent_sheet_entry] > 0
    mixed_sense_offset = jnp.where(parent_sheet_entry[None, :] == word_locations[:, None], shared_sheet_reward, 0.0) + jnp.where(word_unit_present, 0.0, filtered_logits)[None, :]
    mixed_rows = low(low_back(attend(queries, keyval[:, :D], keyval[:, D:], mixed_sense_offset)))
    cross_rows = low(low_back(matmul(mixed_rows, cross_output)))
    gate_rows = jax.nn.sigmoid(low_back(matmul(normed, gate_weight[:D]) + matmul(cross_rows, gate_weight[D:])))
    joined_rows = visual_rows + gate_rows * cross_rows
    second = low(layer_norm(joined_rows, gain_rows[2], biases[2]))
    triple = low(low_back(matmul(second, self_qkv)))
    self_bias = jnp.broadcast_to(jnp.where(valid_row > 0, 0.0, filtered_logits)[None, :], (VIS, VIS))
    attended = low(low_back(attend(triple[:, :D], triple[:, D:2 * D], triple[:, 2 * D:], self_bias)))
    carried = joined_rows + low_back(matmul(attended, self_output))
    third_rows = low(layer_norm(carried, gain_rows[3], biases[3]))
    lifted = low_back(matmul(third_rows, ffn_up))
    active = low(jax.nn.gelu(lifted, approximate=True))
    return carried + low_back(matmul(active, ffn_down))

def reference(visual, text, visual_valid, block_owner, cross_query, cross_keyval, cross_output, gate_weight, self_qkv, self_output, ffn_up, ffn_down, norm_gains, norm_biases, cotangent):
    params = tuple((weight.astype(jnp.float32) for weight in (cross_query, cross_keyval, cross_output, gate_weight, self_qkv, self_output, ffn_up, ffn_down, norm_gains, norm_biases)))

    def page_step(totals, page_items):
        visual_page, text_page, valid_row, parent_sheet_entry, cotangent_page = page_items

        def run(visual_rows, text_rows, layer_params):
            return forward(visual_rows, text_rows, layer_params, valid_row, parent_sheet_entry)
        result, pullback = jax.vjp(run, visual_page.astype(jnp.float32), text_page.astype(jnp.float32), params)
        grad_visual, grad_text, grad_params = pullback(cotangent_page.astype(jnp.float32))
        totals = tuple((running + addition for running, addition in zip(totals, grad_params)))
        return (totals, (result.astype(jnp.bfloat16), grad_visual, grad_text))
    starting = tuple((jnp.zeros(tensor.shape, jnp.float32) for tensor in params))
    totals, (layer_out, grad_visual, grad_text) = lax.scan(page_step, starting, (visual, text, visual_valid, block_owner, cotangent))
    return (layer_out, grad_visual, grad_text, totals[0], totals[1], totals[2], totals[3], totals[4], totals[5], totals[6], totals[7], totals[8], totals[9])
```

```python
import jax
import jax.numpy as jnp
from jax import lax
from jax.sharding import PartitionSpec as P

H = 12
HD = 64
D = H * HD
BF = jnp.bfloat16
F32 = jnp.float32

epsilon = 1e-05
filtered_logits = -1000000000.0
shared_sheet_reward = 6.0


class Links:
    def __init__(self, reps, shards):
        self.reps, self.shards = reps, shards
        self.depth = shards // 2
        rank = lax.axis_index("rep")
        shard = lax.axis_index("fsdp")
        self.c, self.t = rank % 2, (rank // 2) % 2
        self.group = self.t * 2 + self.c
        self.x, self.z = shard % 2, shard // 2
        self.shard = shard

    def core(self, a):
        return lax.ppermute(a, "rep", [(r, r ^ 1) for r in range(self.reps)])

    def y(self, a):
        return lax.ppermute(a, "rep", [(r, r ^ 2) for r in range(self.reps)])

    def rep_bit(self, a, bit):
        return lax.ppermute(a, "rep", [(r, r ^ bit) for r in range(self.reps)])

    def across(self, a):
        return lax.ppermute(a, "fsdp", [(s, s ^ 1) for s in range(self.shards)])

    def along(self, a, k):
        return lax.ppermute(a, "fsdp", [(s, s ^ (2 * k)) for s in range(self.shards)])

    def gather(self, part, axis=0):
        pieces = [part] + [self.along(part, k) for k in range(1, self.depth)]
        shape = part.shape[:axis] + (self.depth,) + part.shape[axis:]
        column = jnp.zeros(shape, part.dtype)
        for k, piece in enumerate(pieces):
            column = lax.dynamic_update_index_in_dim(column, piece, self.z ^ k, axis)
        other = self.across(column)
        first = self.x == 0
        both = jnp.stack([jnp.where(first, column, other), jnp.where(first, other, column)], axis + 1)
        return both.reshape(part.shape[:axis] + (self.shards,) + part.shape[axis:])

    def scatter(self, whole, axis=0):
        shape = whole.shape
        split = whole.reshape(shape[:axis] + (self.depth, 2) + shape[axis + 1 :])
        keep = lax.dynamic_index_in_dim(split, self.x, axis + 1, False)
        send = lax.dynamic_index_in_dim(split, 1 - self.x, axis + 1, False)
        column = (keep.astype(F32) + self.across(send).astype(F32)).astype(BF)
        total = lax.dynamic_index_in_dim(column, self.z, axis, False).astype(F32)
        for k in range(1, self.depth):
            piece = lax.dynamic_index_in_dim(column, self.z ^ k, axis, False)
            total = total + self.along(piece, k).astype(F32)
        for bit in range(2, self.reps.bit_length() - 1):
            total = total + self.rep_bit(total.astype(BF), 1 << bit).astype(F32)
        return total.astype(BF)

    def spread(self, quarter):
        other_c = self.core(quarter)
        pair = jnp.stack([jnp.where(self.c == 0, quarter, other_c), jnp.where(self.c == 0, other_c, quarter)])
        other_t = self.y(pair)
        return jnp.concatenate([jnp.where(self.t == 0, pair, other_t), jnp.where(self.t == 0, other_t, pair)])

    def total(self, a):
        for bit in range(self.reps.bit_length() - 1):
            a = a + self.rep_bit(a, 1 << bit)
        a = a + self.across(a)
        for bit in range(self.depth.bit_length() - 1):
            a = a + self.along(a, 1 << bit)
        return a

    def place(self, own, oth_c, oth_t, oth_b):
        c0 = self.c == 0
        t0 = self.t == 0
        a, b = jnp.where(c0, own, oth_c), jnp.where(c0, oth_c, own)
        e, f = jnp.where(c0, oth_t, oth_b), jnp.where(c0, oth_b, oth_t)
        return [jnp.where(t0, a, e), jnp.where(t0, b, f), jnp.where(t0, e, a), jnp.where(t0, f, b)]

    def pick(self, a, axis):
        return [lax.dynamic_index_in_dim(a, self.group ^ k, axis, False) for k in range(4)]


def norm_stats(rows):
    mean = jnp.mean(rows, -1, keepdims=True)
    centred = rows - mean
    factor = lax.rsqrt(jnp.mean(centred * centred, -1, keepdims=True) + epsilon)
    return centred * factor, factor


def norm_back(gradient, normal, factor, gain_row):
    scaled = gradient * gain_row
    centred = scaled - jnp.mean(scaled, -1, keepdims=True) - normal * jnp.mean(scaled * normal, -1, keepdims=True)
    return centred * factor, jnp.sum(gradient * normal, 0), jnp.sum(gradient, 0)


def mm(a, b):
    return jnp.dot(a, b, preferred_element_type=F32)


def mm_nt(a, b):
    return lax.dot_general(a, b, (((1,), (1,)), ((), ())), preferred_element_type=F32)


def mm_tn(a, b):
    return lax.dot_general(a, b, (((0,), (0,)), ((), ())), preferred_element_type=F32)


def attend(q, k, v, bias):
    n, m, h = q.shape[0], k.shape[0], q.shape[1] // HD
    q, k, v = q.reshape(n, h, HD), k.reshape(m, h, HD), v.reshape(m, h, HD)
    scores = jnp.einsum("qhe,khe->hqk", q, k, preferred_element_type=F32) * HD ** (-0.5) + bias[None]
    peak = jnp.max(scores, -1, keepdims=True)
    expo = jnp.exp(scores - peak)
    total = jnp.sum(expo, -1, keepdims=True)
    weight = (expo / total).astype(BF)
    out = jnp.einsum("hqk,khe->qhe", weight, v, preferred_element_type=F32)
    return out.reshape(n, h * HD).astype(BF), peak + jnp.log(total)


def attend_back(do, q, k, v, bias, logs):
    n, m, h = q.shape[0], k.shape[0], q.shape[1] // HD
    q, k, v, do = q.reshape(n, h, HD), k.reshape(m, h, HD), v.reshape(m, h, HD), do.reshape(n, h, HD)
    scale = HD ** (-0.5)
    scores = jnp.einsum("qhe,khe->hqk", q, k, preferred_element_type=F32) * scale + bias[None]
    weight = jnp.exp(scores - logs)
    dv = jnp.einsum("hqk,qhe->khe", weight.astype(BF), do, preferred_element_type=F32)
    dp = jnp.einsum("qhe,khe->hqk", do, v, preferred_element_type=F32)
    ds = (weight * (dp - jnp.sum(weight * dp, -1, keepdims=True))).astype(BF)
    dq = jnp.einsum("hqk,khe->qhe", ds, k, preferred_element_type=F32) * scale
    dk = jnp.einsum("hqk,qhe->khe", ds, q, preferred_element_type=F32) * scale
    return dq.reshape(n, h * HD), dk.reshape(m, h * HD), dv.reshape(m, h * HD)


def local(reps, shards, visual, text, visual_valid, block_owner, cross_query, cross_keyval, cross_output, gate_weight,
          self_qkv, self_output, ffn_up, ffn_down, norm_gains, norm_biases, cotangent):
    ln = Links(reps, shards)
    visual, text, cotangent = visual[0], text[0], cotangent[0]
    visual_valid, block_owner = visual_valid[0], block_owner[0]
    rows = cross_query.shape[0]
    quarter = rows // 4
    own = ln.group

    w3 = D // 4
    at = own * w3
    ckv = lax.dynamic_slice_in_dim(cross_keyval.reshape(rows, 2, D), at, w3, 2).reshape(rows, 2 * w3)
    cq = lax.dynamic_slice_in_dim(cross_query, at, w3, 1)
    gains_hi = norm_gains.astype(BF)
    biases_hi = norm_biases.astype(BF)
    gains_lo = (norm_gains - gains_hi.astype(F32)).astype(BF)
    biases_lo = (norm_biases - biases_hi.astype(F32)).astype(BF)
    norms = jnp.concatenate([gains_hi, gains_lo, biases_hi, biases_lo])
    norms = jnp.pad(norms, (0, rows * 64 - norms.shape[0])).reshape(rows, 64)
    part_a = jnp.concatenate([ckv, cq, norms], 1)
    part_b = jnp.concatenate([
        lax.dynamic_slice_in_dim(cross_output, own * quarter, quarter, 0),
        lax.dynamic_slice_in_dim(gate_weight, own * 2 * quarter, 2 * quarter, 0),
        lax.dynamic_slice_in_dim(self_output, own * quarter, quarter, 0)], 0)
    part_c = lax.dynamic_index_in_dim(self_qkv.reshape(rows, 3, 4, w3), own, 2, False).reshape(rows, 3 * w3)
    part_d = jnp.stack([
        lax.dynamic_index_in_dim(ffn_up.reshape(rows, shards, 4, rows), own, 2, False).reshape(rows, D),
        lax.dynamic_index_in_dim(ffn_down.reshape(4, rows, D), own, 0, False)], 0)

    def all_groups(mine):
        mine_t = ln.y(mine)
        pair = ln.core(jnp.stack([mine, mine_t]))
        return mine, pair[0], mine_t, pair[1]

    full_a = all_groups(ln.gather(part_a).reshape(D, -1))
    full_b = all_groups(ln.gather(part_b))
    full_c = ln.gather(part_c).reshape(D, -1)
    full_c = jnp.stack([full_c, ln.core(full_c)])
    full_d = ln.gather(part_d, 1).reshape(2, D, D)
    full_d = (full_d, ln.core(full_d))

    norm_all = full_a[0][:, 3 * w3 :].reshape(shards, rows * 64)
    size = norm_gains.shape[0]
    norm_all = norm_all[:, : 4 * size].astype(F32).reshape(shards, 4, size)
    gain_rows = (norm_all[:, 0] + norm_all[:, 1]).reshape(4, D)
    biases = (norm_all[:, 2] + norm_all[:, 3]).reshape(4, D)
    kv_w = [w[:, : 2 * w3] for w in full_a]
    q_w = [w[:, 2 * w3 : 3 * w3] for w in full_a]
    placed = jnp.stack(ln.place(*full_b), 1)
    out_w = placed[:, :, :quarter].reshape(D, D)
    gate_w = placed[:, :, quarter : 3 * quarter].reshape(2 * D, D)
    self_out_w = placed[:, :, 3 * quarter :].reshape(D, D)

    def pair_y(a):
        return jnp.stack([a, ln.y(a)])

    cot_pair = pair_y(cotangent)
    bias_pair = pair_y(jnp.where(visual_valid > 0, 0.0, filtered_logits).astype(F32))
    visual_rows = visual.astype(F32)
    normal_one, factor_one = norm_stats(visual_rows)
    normed = (normal_one * gain_rows[0] + biases[0]).astype(BF)
    normal_text, factor_text = norm_stats(text.astype(F32))
    text_normed = (normal_text * gain_rows[1] + biases[1]).astype(BF)
    queries = jnp.concatenate([mm(normed, w) for w in q_w], 1).astype(BF)
    keyvals = [mm(text_normed, w).astype(BF) for w in kv_w]
    keys = jnp.concatenate([a[:, :w3] for a in keyvals], 1)
    values = jnp.concatenate([a[:, w3:] for a in keyvals], 1)
    vis = visual.shape[0]
    parent = block_owner[None, :] == lax.broadcasted_iota(jnp.int32, (vis, 1), 0)
    present = jnp.sum(jnp.where(parent, visual_valid[:, None], 0), axis=0) > 0
    cross_bias = jnp.where(parent, shared_sheet_reward, 0.0) + jnp.where(present, 0.0, filtered_logits)[None, :]
    mixed_rel, cross_log = attend(queries, keys, values, cross_bias)
    mixed = jnp.concatenate(ln.place(*jnp.split(mixed_rel, 4, 1)), 1)
    cross_rows = mm(mixed, out_w).astype(BF)
    cross_full = cross_rows.astype(F32)
    gate = jax.nn.sigmoid(mm(jnp.concatenate([normed, cross_rows], 1), gate_w))
    joined = visual_rows + gate * cross_full
    normal_two, factor_two = norm_stats(joined)
    second = (normal_two * gain_rows[2] + biases[2]).astype(BF)
    second2 = pair_y(second).reshape(2 * vis, D)
    triple = [mm(second2, full_c[i]).astype(BF).reshape(2, vis, 3, w3) for i in range(2)]
    triple = jnp.stack(triple, 3).reshape(2, vis, 3, 2 * w3)
    self_bias = jnp.broadcast_to(bias_pair[:, None, :], (2, vis, vis))
    self_fwd = [attend(triple[p, :, 0], triple[p, :, 1], triple[p, :, 2], self_bias[p]) for p in range(2)]
    att_mine = self_fwd[0][0]
    att_from = ln.y(self_fwd[1][0])
    attended = jnp.concatenate(ln.place(att_mine[:, :w3], att_mine[:, w3:], att_from[:, :w3], att_from[:, w3:]), 1)
    carried = joined + mm(attended, self_out_w)
    normal_three, factor_three = norm_stats(carried)
    third = (normal_three * gain_rows[3] + biases[3]).astype(BF)
    third2 = pair_y(third).reshape(2 * vis, D)
    lifted = [mm(third2, w[0]) for w in full_d]
    acts = [jax.vjp(lambda v: jax.nn.gelu(v, approximate=True), l) for l in lifted]
    active = [a[0].astype(BF) for a in acts]
    down = (mm(active[0], full_d[0][1]) + mm(active[1], full_d[1][1])).reshape(2, vis, D)
    layer_out = (carried + down[0] + ln.y(down[1].astype(BF)).astype(F32)).astype(BF)

    cot2 = cot_pair.reshape(2 * vis, D)
    d_down = [mm_tn(a, cot2).astype(BF) for a in active]
    d_lifted = [acts[i][1](mm_nt(cot2, full_d[i][1]))[0].astype(BF) for i in range(2)]
    d_up = [mm_tn(third2, d).astype(BF) for d in d_lifted]

    def scatter_core(mine, other, axis):
        both = (mine.astype(F32) + ln.core(other).astype(F32)).astype(BF)
        return ln.scatter(both.reshape(both.shape[:axis] + (shards, rows) + both.shape[axis + 1 :]), axis)

    sum_d = scatter_core(jnp.stack([d_up[0], d_down[0]]), jnp.stack([d_up[1], d_down[1]]), 1)
    d_third = (mm_nt(d_lifted[0], full_d[0][0]) + mm_nt(d_lifted[1], full_d[1][0])).reshape(2, vis, D)
    d_third = d_third[0] + ln.y(d_third[1].astype(BF)).astype(F32)
    back_three, gain_three, bias_three = norm_back(d_third, normal_three, factor_three, gain_rows[3])
    d_carried = cotangent.astype(F32) + back_three
    carried_low = d_carried.astype(BF)
    d_self_output = mm_tn(attended, carried_low).astype(BF)
    d_attended = mm_nt(carried_low, self_out_w).astype(BF)
    d_att = ln.pick(d_attended.reshape(vis, 4, w3), 1)
    from_y = ln.y(jnp.concatenate([d_att[2], d_att[3]], 1))
    d_att = [jnp.concatenate([d_att[0], d_att[1]], 1), from_y]
    self_back = [attend_back(d_att[p], triple[p, :, 0], triple[p, :, 1], triple[p, :, 2], self_bias[p], self_fwd[p][1])
                 for p in range(2)]
    d_triple = jnp.stack([jnp.stack([g.reshape(vis, 2, w3) for g in page], 2) for page in self_back])
    d_triple = d_triple.astype(BF).reshape(2 * vis, 2, 3 * w3)
    d_triple = [d_triple[:, 0], d_triple[:, 1]]
    d_qkv = [mm_tn(second2, g).astype(BF) for g in d_triple]
    sum_c = scatter_core(d_qkv[0], d_qkv[1], 0)
    d_second = (mm_nt(d_triple[0], full_c[0]) + mm_nt(d_triple[1], full_c[1])).reshape(2, vis, D)
    d_second = d_second[0] + ln.y(d_second[1].astype(BF)).astype(F32)
    back_two, gain_two, bias_two = norm_back(d_second, normal_two, factor_two, gain_rows[2])
    d_joined = d_carried + back_two
    d_gate_in = (d_joined * cross_full * gate * (1.0 - gate)).astype(BF)
    d_gate_w = jnp.concatenate([mm_tn(normed, d_gate_in), mm_tn(cross_rows, d_gate_in)], 0).astype(BF)
    d_gate_rows = mm_nt(d_gate_in, gate_w)
    d_cross = (d_joined * gate + d_gate_rows[:, D:]).astype(BF)
    d_out_w = mm_tn(mixed, d_cross).astype(BF)
    stacked_b = jnp.concatenate([
        d_out_w.reshape(shards, 4, quarter, D),
        d_gate_w.reshape(shards, 4, 2 * quarter, D),
        d_self_output.reshape(shards, 4, quarter, D)], 2)

    def scatter_groups(groups):
        got = ln.core(jnp.stack([groups[1], groups[3]]))
        first = (groups[0].astype(F32) + got[0].astype(F32)).astype(BF)
        second_ = (groups[2].astype(F32) + got[1].astype(F32)).astype(BF)
        return ln.scatter((first.astype(F32) + ln.y(second_).astype(F32)).astype(BF))

    sum_b = scatter_groups(ln.pick(stacked_b, 1))
    d_mixed = mm_nt(d_cross, out_w).astype(BF)
    d_mixed = jnp.concatenate(ln.pick(d_mixed.reshape(vis, 4, w3), 1), 1)
    d_q, d_k, d_v = attend_back(d_mixed, queries, keys, values, cross_bias, cross_log)
    d_q = jnp.split(d_q.astype(BF), 4, 1)
    d_kv = [jnp.concatenate([k_, v_], 1).astype(BF) for k_, v_ in zip(jnp.split(d_k, 4, 1), jnp.split(d_v, 4, 1))]
    groups_a = [jnp.concatenate([mm_tn(text_normed, d_kv[g]), mm_tn(normed, d_q[g])], 1).astype(BF).reshape(shards, rows, 3 * w3)
                for g in range(4)]
    sum_a = scatter_groups(groups_a)
    d_normed = mm_nt(d_gate_in, gate_w[:D])
    d_text_normed = 0.0
    for g in range(4):
        d_normed = d_normed + mm_nt(d_q[g], q_w[g])
        d_text_normed = d_text_normed + mm_nt(d_kv[g], kv_w[g])
    back_one, gain_one, bias_one = norm_back(d_normed, normal_one, factor_one, gain_rows[0])
    grad_visual = d_joined + back_one
    grad_text, gain_text, bias_text = norm_back(d_text_normed, normal_text, factor_text, gain_rows[1])
    norm_grads = jnp.stack([gain_one, gain_text, gain_two, gain_three, bias_one, bias_text, bias_two, bias_three])
    norm_grads = ln.total(norm_grads).reshape(2, shards, size)
    norm_grads = lax.dynamic_index_in_dim(norm_grads, ln.shard, 1, False)

    all_a = ln.spread(sum_a).astype(F32)
    all_b = ln.spread(sum_b).astype(F32)
    all_c = ln.spread(sum_c).astype(F32)
    all_d = ln.spread(sum_d).astype(F32)
    g_keyval = all_a[:, :, : 2 * w3].reshape(4, rows, 2, w3).transpose(1, 2, 0, 3).reshape(rows, 2 * D)
    g_query = all_a[:, :, 2 * w3 :].transpose(1, 0, 2).reshape(rows, D)
    g_out = all_b[:, :quarter].reshape(rows, D)
    g_gate = all_b[:, quarter : 3 * quarter].reshape(2 * rows, D)
    g_self_out = all_b[:, 3 * quarter :].reshape(rows, D)
    g_qkv = all_c.reshape(4, rows, 3, w3).transpose(1, 2, 0, 3).reshape(rows, 3 * D)
    g_up = all_d[:, 0].reshape(4, rows, shards, rows).transpose(1, 2, 0, 3).reshape(rows, 4 * D)
    g_down = all_d[:, 1].reshape(4 * rows, D)
    return (layer_out[None], grad_visual[None], grad_text[None], g_query, g_keyval, g_out, g_gate, g_qkv, g_self_out,
            g_up, g_down, norm_grads[0], norm_grads[1])


def solution(mesh):
    pages = P(("rep", "fsdp"), None, None)
    flags = P(("rep", "fsdp"), None)
    matrix = P("fsdp", None)
    vector = P("fsdp")
    in_specs = (pages, pages, flags, flags) + (matrix,) * 8 + (vector, vector, pages)
    out_specs = (pages, pages, pages) + (matrix,) * 8 + (vector, vector)
    reps, shards = mesh.shape["rep"], mesh.shape["fsdp"]

    def run(*args):
        return local(reps, shards, *args)

    return jax.shard_map(run, mesh=mesh, in_specs=in_specs, out_specs=out_specs, check_vma=False)
```

```python
import functools

import jax
import jax.numpy as jnp
from jax import lax
from jax.experimental import pallas as pl
from jax.experimental.pallas import tpu as pltpu
from jax.sharding import PartitionSpec as P

H = 12
HD = 64
D = H * HD
HALF = D // 2
QUART = D // 4
BF = jnp.bfloat16
F32 = jnp.float32

epsilon = 1e-05
filtered_logits = -1000000000.0
shared_sheet_reward = 6.0
SCALE = HD ** (-0.5)
VM = pl.BlockSpec(memory_space=pltpu.VMEM)
SM = pl.BlockSpec(memory_space=pltpu.SMEM)


def sds(shape, dtype=BF):
    return jax.ShapeDtypeStruct(tuple(shape), dtype)


def size_of(a):
    n = jnp.dtype(a.dtype).itemsize
    for d in a.shape:
        n *= d
    return n


def run(body, outs, where, *ins, flops=0, name=None, scratch=()):
    moved = sum(size_of(a) for a in ins) + sum(size_of(o) for o in outs)
    held = moved + sum(size_of(s) for s in scratch)
    return pl.pallas_call(
        body,
        out_shape=list(outs),
        in_specs=[SM] + [VM] * len(ins),
        out_specs=[VM] * len(outs),
        scratch_shapes=[pltpu.VMEM(s.shape, s.dtype) for s in scratch],
        compiler_params=pltpu.CompilerParams(vmem_limit_bytes=min(60 << 20, int(1.25 * held) + (10 << 20))),
        cost_estimate=pl.CostEstimate(flops=flops, bytes_accessed=moved, transcendentals=0),
        name=name,
    )(where, *ins)


T, C, X, Z = 0, 1, 2, 3


class Links:
    def __init__(self, reps, shards):
        self.reps, self.shards = reps, shards
        self.depth = shards // 2
        rank = lax.axis_index("rep")
        shard = lax.axis_index("fsdp")
        self.shard = shard
        self.at = jnp.stack([(rank // 2) % 2, rank % 2, shard % 2, shard // 2]).astype(jnp.int32)

    def core(self, a):
        return lax.ppermute(a, "rep", [(r, r ^ 1) for r in range(self.reps)])

    def y(self, a):
        return lax.ppermute(a, "rep", [(r, r ^ 2) for r in range(self.reps)])

    def rep_bit(self, a, bit):
        return lax.ppermute(a, "rep", [(r, r ^ bit) for r in range(self.reps)])

    def across(self, a):
        return lax.ppermute(a, "fsdp", [(s, s ^ 1) for s in range(self.shards)])

    def along(self, a, k):
        return lax.ppermute(a, "fsdp", [(s, s ^ (2 * k)) for s in range(self.shards)])

    def total(self, a):
        for bit in range(self.reps.bit_length() - 1):
            a = a + self.rep_bit(a, 1 << bit)
        a = a + self.across(a)
        for bit in range(self.depth.bit_length() - 1):
            a = a + self.along(a, 1 << bit)
        return a

    def gather(self, part):
        pieces = [part] + [self.along(part, k) for k in range(1, self.depth)]

        def body(at, *refs):
            out = refs[-1]
            for k in range(self.depth):
                out[at[Z] ^ k] = refs[k][...]

        (column,) = run(body, [sds((self.depth,) + part.shape)], self.at, *pieces, name="column")
        return column, self.across(column)

    def scatter(self, pairs):
        rows, n = pairs[0].shape[-2:]
        depth, count = self.depth, len(pairs)
        pairs = [p.reshape(depth, 2, rows, n) for p in pairs]

        def body1(at, *refs):
            keep, send = refs[-2:]
            for side, out in ((at[X], keep), (1 - at[X], send)):
                for z in range(depth):
                    acc = refs[0][z, side].astype(F32)
                    for r in refs[1:count]:
                        acc = acc + r[z, side].astype(F32)
                    out[z] = acc.astype(BF)

        keep, send = run(body1, [sds((depth, rows, n))] * 2, self.at, *pairs, name="reduce_x")
        got = self.across(send)

        def body2(at, keep, got, *outs):
            for k in range(depth):
                outs[k][...] = (keep[at[Z] ^ k].astype(F32) + got[at[Z] ^ k].astype(F32)).astype(BF)

        pieces = run(body2, [sds((rows, n))] * depth, self.at, keep, got, name="reduce_z")
        parts = [pieces[0]] + [self.along(pieces[k], k) for k in range(1, depth)]

        def body3(at, *refs):
            acc = refs[0][...].astype(F32)
            for r in refs[1:depth]:
                acc = acc + r[...].astype(F32)
            refs[-1][...] = acc.astype(BF)

        (total,) = run(body3, [sds((rows, n))], self.at, *parts, name="reduce_sum")
        for bit in range(2, self.reps.bit_length() - 1):
            total = (total.astype(F32) + self.rep_bit(total, 1 << bit).astype(F32)).astype(BF)
        return total


def mm(a, b):
    return jnp.dot(a, b, preferred_element_type=F32)


def nt(a, b):
    return lax.dot_general(a, b, (((1,), (1,)), ((), ())), preferred_element_type=F32)


def tn(a, b):
    return lax.dot_general(a, b, (((0,), (0,)), ((), ())), preferred_element_type=F32)


def stats(rows):
    mean = jnp.mean(rows, -1, keepdims=True)
    centred = rows - mean
    factor = lax.rsqrt(jnp.mean(centred * centred, -1, keepdims=True) + epsilon)
    return centred * factor, factor


def norm_back(grad, normal, factor, gain):
    scaled = grad * gain
    dx = scaled - jnp.mean(scaled, -1, keepdims=True) - normal * jnp.mean(scaled * normal, -1, keepdims=True)
    return dx * factor, jnp.sum(grad * normal, 0, keepdims=True), jnp.sum(grad, 0, keepdims=True)


def gain_of(ref, i):
    return ref[:, i * D : (i + 1) * D]


def half(i):
    return pl.ds(pl.multiple_of(i * HALF, 128), HALF)


def pair_masks(rows):
    lane = lax.broadcasted_iota(jnp.int32, (rows, 128), 1)
    return lane < HD


def two_heads(a):
    first = pair_masks(a.shape[0])
    zero = jnp.zeros_like(a)
    return jnp.concatenate([jnp.where(first, a, zero), jnp.where(first, zero, a)], 0)


def one_pair(a):
    n = a.shape[0] // 2
    return jnp.where(pair_masks(n), a[:n], a[n:])


def softmax(scores):
    peak = jnp.max(scores, -1, keepdims=True)
    expo = jnp.exp(scores - peak)
    total = jnp.sum(expo, -1, keepdims=True)
    return expo / total, peak + jnp.log(total)


def pack_a(at, query, keyval, gains, biases, part):
    rows, size = query.shape[0], gains.shape[1]
    part[:rows, :HALF] = keyval[:, pl.ds(pl.multiple_of(at[T] * D + at[C] * HALF, 128), HALF)]
    part[:rows, HALF:] = query[:, half(at[C])]
    part[rows:, :] = jnp.zeros((16, D), BF)
    g, b = gains[...], biases[...]
    g_hi, b_hi = g.astype(BF), b.astype(BF)
    g_lo, b_lo = (g - g_hi.astype(F32)).astype(BF), (b - b_hi.astype(F32)).astype(BF)
    row = lax.broadcasted_iota(jnp.int32, (16, size), 0)
    out = jnp.zeros((16, size), F32)
    for i, v in enumerate((g_hi, g_lo, b_hi, b_lo)):
        out = jnp.where(row == i, jnp.broadcast_to(v.astype(F32), (16, size)), out)
    part[rows:, :size] = out.astype(BF)


def pack_rest(at, output, gate, qkv, self_out, up, down, part_bc, part_d):
    rows = output.shape[0]
    shards = D // rows
    t0, c0 = at[T] == 0, at[C] == 0
    gate_c, out_c, self_c = gate[:, half(at[C])], output[:, half(at[C])], self_out[:, half(at[C])]
    part_bc[:, :HALF] = jnp.where(t0, gate_c[:rows], gate_c[rows:])
    part_bc[:, HALF:D] = jnp.where(t0, out_c, self_c)
    pieces = []
    for i in range(3):
        v = qkv[:, pl.ds(pl.multiple_of(i * D + at[T] * HALF, 128), HALF)]
        pieces.append(jnp.where(c0, v[:, :QUART], v[:, QUART:]))
    part_bc[:, D:] = jnp.concatenate(pieces, 1)
    pieces = []
    for s in range(shards):
        v = [up[:, (s * 4 + g) * rows : (s * 4 + g + 1) * rows] for g in range(4)]
        pieces.append(jnp.where(t0, jnp.where(c0, v[0], v[1]), jnp.where(c0, v[2], v[3])))
    part_d[:, :D] = jnp.concatenate(pieces, 1)
    v = [down[g * rows : (g + 1) * rows, :] for g in range(4)]
    part_d[:, D:] = jnp.where(t0, jnp.where(c0, v[0], v[1]), jnp.where(c0, v[2], v[3]))


def join_a(rows, size, at, mine, other, kv, q, gains, biases):
    depth = mine.shape[0]
    for src, side in ((mine, at[X]), (other, 1 - at[X])):
        for z in range(depth):
            kv[z, side] = src[z, :rows, :HALF]
            q[z, side] = src[z, :rows, HALF:]
    first = at[X] == 0
    for z in range(depth):
        a, b = mine[z, rows:, :size].astype(F32), other[z, rows:, :size].astype(F32)
        for i, v in enumerate((jnp.where(first, a, b), jnp.where(first, b, a))):
            s = (z * 2 + i) * size
            gains[:, s : s + size] = v[0:1] + v[1:2]
            biases[:, s : s + size] = v[2:3] + v[3:4]


def join_bc(at, mine, other, b, c):
    depth = mine.shape[0]
    for src, side in ((mine, at[X]), (other, 1 - at[X])):
        for z in range(depth):
            b[z, side] = src[z, :, :D]
            c[z, side] = src[z, :, D:]


def join_d(at, mine, other, out):
    for src, side in ((mine, at[X]), (other, 1 - at[X])):
        for z in range(mine.shape[0]):
            out[z, side] = src[z]


def place_b(at, oo, oc, to, tc, cross_out, self_out, gate):
    t, c = at[T], at[C]
    for src, tt, cc in ((oo, t, c), (oc, t, 1 - c), (to, 1 - t, c), (tc, 1 - t, 1 - c)):
        for s in range(src.shape[0]):
            gate[s, tt, :, half(cc)] = src[s, :, :HALF]

        @pl.when(tt == 0)
        def _():
            cross_out[:, :, half(cc)] = src[:, :, HALF:]

        @pl.when(tt == 1)
        def _():
            self_out[:, :, half(cc)] = src[:, :, HALF:]


def keyval_kernel(at, text, visual, gains, biases, oo, oc, to, tc, q_own, q_oth,
                  text_normed, kv, w_kv, w_q, normed, queries):
    t, c = at[T], at[C]

    @pl.when(pl.program_id(0) == 0)
    def _():
        for src, tt, cc in ((oo, t, c), (oc, t, 1 - c), (to, 1 - t, c), (tc, 1 - t, 1 - c)):
            w_kv[:, pl.ds(pl.multiple_of(tt * D + cc * HALF, 128), HALF)] = src[...]
        w_q[:, half(c)] = q_own[...]
        w_q[:, half(1 - c)] = q_oth[...]
        normal, _f = stats(visual[...].astype(F32))
        n = (normal * gain_of(gains, 0) + gain_of(biases, 0)).astype(BF)
        normed[...] = n
        queries[...] = mm(n, w_q[...]).astype(BF)

    normal, _f = stats(text[...].astype(F32))
    n = (normal * gain_of(gains, 1) + gain_of(biases, 1)).astype(BF)
    text_normed[...] = n
    kv[...] = mm(n, w_kv[...]).astype(BF)


def cross_bias(owner, valid):
    n, m = valid.shape[1], owner.shape[1]
    parent = owner[...] == lax.broadcasted_iota(jnp.int32, (n, m), 0)
    ones = jnp.where(parent, 1.0, 0.0).astype(BF)
    real = jnp.broadcast_to(valid[...].astype(F32), (8, n)).astype(BF)
    present = mm(real, ones)[0:1] > 0.5
    return jnp.where(parent, shared_sheet_reward, 0.0) + jnp.where(present, 0.0, filtered_logits)


def cross_fwd(owner, valid, q, k, v, out, logs, bias):
    @pl.when(pl.program_id(0) == 0)
    def _():
        bias[...] = cross_bias(owner, valid)

    b = bias[...]
    scores = nt(two_heads(q[...]), k[...]) * SCALE + jnp.concatenate([b, b], 0)
    weight, log = softmax(scores)
    logs[0] = log
    out[...] = one_pair(mm(weight.astype(BF), v[...])).astype(BF)


def gate_kernel(at, mixed, normed, visual, gains, biases, w_out, w_gate, cross, gate, joined, second):
    rows = mm(mixed[...], w_out[...]).astype(BF)
    cross[...] = rows
    g = jax.nn.sigmoid(mm(normed[...], w_gate[:D]) + mm(rows, w_gate[D:]))
    gate[...] = g
    j = visual[...].astype(F32) + g * rows.astype(F32)
    joined[...] = j
    normal, _f = stats(j)
    second[...] = (normal * gain_of(gains, 2) + gain_of(biases, 2)).astype(BF)


def head_order(at, a):
    return jnp.where(at[C] == 0, a, jnp.concatenate([a[:, QUART:], a[:, :QUART]], 1))


def self_bias(valid):
    return jnp.where(valid > 0.5, 0.0, filtered_logits)


def self_fwd(at, second0, second1, valid0, valid1, w_own, w_oth, triple, att0, att1):
    n = second0.shape[0]
    rows = jnp.concatenate([second0[...], second1[...]], 0)
    own, oth = mm(rows, w_own[...]).astype(BF), mm(rows, w_oth[...]).astype(BF)
    for i in range(3):
        triple[:, i * HALF : (i + 1) * HALF] = jnp.concatenate(
            [own[:, i * QUART : (i + 1) * QUART], oth[:, i * QUART : (i + 1) * QUART]], 1)
    for page, (valid, att) in enumerate(((valid0, att0), (valid1, att1))):
        bias = self_bias(valid[...])
        r = slice(page * n, (page + 1) * n)
        outs = []
        for p in range(3):
            q, k, v = [triple[r, i * HALF + p * 128 : i * HALF + (p + 1) * 128] for i in range(3)]
            weight, _l = softmax(nt(two_heads(q), k) * SCALE + bias)
            outs.append(one_pair(mm(weight.astype(BF), v)).astype(BF))
        att[...] = head_order(at, jnp.concatenate(outs, 1))


def carry_kernel(at, mine, came, joined, gains, biases, w, attended, carried, third):
    attended[:, half(at[T])] = mine[...]
    attended[:, half(1 - at[T])] = came[...]
    c = joined[...] + mm(attended[...], w[...])
    carried[...] = c
    normal, _f = stats(c)
    third[...] = (normal * gain_of(gains, 3) + gain_of(biases, 3)).astype(BF)


def ffn_kernel(last, at, third0, third1, cot0, cot1, w, *refs):
    n = third0.shape[0]
    if last:
        y0i, y1i, d0i, d1i, y0, y1, d0, d1, grad = refs
    else:
        y0, y1, d0, d1, grad = refs
    rows = jnp.concatenate([third0[...], third1[...]], 0)
    cot = jnp.concatenate([cot0[...], cot1[...]], 0)
    up, down = w[:, :D], w[:, D:]
    v = mm(rows, up)
    k = (2.0 / 3.141592653589793) ** 0.5
    th = jnp.tanh(k * (v + 0.044715 * (v * v * v)))
    act = (0.5 * v * (1.0 + th)).astype(BF)
    slope = 0.5 * (1.0 + th) + 0.5 * v * (1.0 - th * th) * (k * (1.0 + 3.0 * 0.044715 * (v * v)))
    y = mm(act, down)
    grad[:, D:] = tn(act, cot).astype(BF)
    dl = (nt(cot, down) * slope).astype(BF)
    d = nt(dl, up)
    grad[:, :D] = tn(rows, dl).astype(BF)
    if last:
        y0[...] = y[:n] + y0i[...]
        y1[...] = (y[n:] + y1i[...]).astype(BF)
        d0[...] = d[:n] + d0i[...]
        d1[...] = (d[n:] + d1i[...]).astype(BF)
    else:
        y0[...], y1[...], d0[...], d1[...] = y[:n], y[n:], d[:n], d[n:]


def carry_back(at, d0, came, carried, cot, attended, gains, w, d_carried, mine, send, grad, sums):
    normal, factor = stats(carried[...])
    dx, gain, bias = norm_back(d0[...] + came[...].astype(F32), normal, factor, gain_of(gains, 3))
    dc = cot[...].astype(F32) + dx
    d_carried[...] = dc
    low = dc.astype(BF)
    da = nt(low, w[...]).astype(BF)
    t0 = at[T] == 0
    mine[...] = head_order(at, jnp.where(t0, da[:, :HALF], da[:, HALF:]))
    send[...] = head_order(at, jnp.where(t0, da[:, HALF:], da[:, :HALF]))
    grad[...] = tn(attended[...], low).astype(BF)
    sums[0:1], sums[1:2] = gain, bias


def self_back(at, triple, da0, da1, valid0, valid1, second0, second1, w_own, w_oth, d0, d1, g_own, g_oth, dt):
    n = second0.shape[0]
    for page, (valid, da) in enumerate(((valid0, da0), (valid1, da1))):
        bias = self_bias(valid[...])
        r = slice(page * n, (page + 1) * n)
        for p in range(3):
            q, k, v = [triple[r, i * HALF + p * 128 : i * HALF + (p + 1) * 128] for i in range(3)]
            qq = two_heads(q)
            dd = two_heads(da[:, p * 128 : (p + 1) * 128])
            weight, _l = softmax(nt(qq, k) * SCALE + bias)
            dp = nt(dd, v)
            ds = (weight * (dp - jnp.sum(weight * dp, -1, keepdims=True))).astype(BF)
            grads = (one_pair(mm(ds, k)) * SCALE, tn(ds, qq) * SCALE, tn(weight.astype(BF), dd))
            for i in range(3):
                dt[r, i * HALF + p * 128 : i * HALF + (p + 1) * 128] = grads[i].astype(BF)
    own = jnp.concatenate([dt[:, i * HALF : i * HALF + QUART] for i in range(3)], 1)
    oth = jnp.concatenate([dt[:, i * HALF + QUART : (i + 1) * HALF] for i in range(3)], 1)
    rows = jnp.concatenate([second0[...], second1[...]], 0)
    g_own[...] = tn(rows, own).astype(BF)
    g_oth[...] = tn(rows, oth).astype(BF)
    d = nt(own, w_own[...]) + nt(oth, w_oth[...])
    d0[...] = d[:n]
    d1[...] = d[n:].astype(BF)


def gate_back(at, d_carried, d0, came, joined, normed, cross, gate, mixed, gains, w_gate, w_out, g_self,
              d_joined, d_mixed, d_normed, keep, send, sums):
    t, c = at[T], at[C]
    rows = keep.shape[2]
    normal, factor = stats(joined[...])
    dx, gain, bias = norm_back(d0[...] + came[...].astype(F32), normal, factor, gain_of(gains, 2))
    dj = d_carried[...] + dx
    d_joined[...] = dj
    sums[0:1], sums[1:2] = gain, bias
    g = gate[...]
    dg = (dj * cross[...].astype(F32) * g * (1.0 - g)).astype(BF)
    d_normed[...] = nt(dg, w_gate[:D])
    dc = (dj * g + nt(dg, w_gate[D:])).astype(BF)
    d_mixed[...] = nt(dc, w_out[...]).astype(BF)
    g_gate = jnp.concatenate([tn(normed[...], dg).astype(BF), tn(cross[...], dg).astype(BF)], 0)
    g_gate = g_gate.reshape(D // rows, 2, rows, D)
    g_out = tn(mixed[...], dc).astype(BF).reshape(D // rows, rows, D)
    g_so = g_self[...].reshape(D // rows, rows, D)
    for tt in range(2):
        for cc in range(2):
            lanes = slice(cc * HALF, (cc + 1) * HALF)
            side = g_out if tt == 0 else g_so
            for out, same in ((keep, True), (send, False)):
                @pl.when((c == cc) == same)
                def _():
                    out[t ^ tt, :, :, :HALF] = g_gate[:, tt, :, lanes]
                    out[t ^ tt, :, :, HALF:] = side[:, :, lanes]


def cross_back(owner, valid, q, k, v, dm, logs, dq, dkv, bias):
    @pl.when(pl.program_id(0) == 0)
    def _():
        bias[...] = cross_bias(owner, valid)

    b = bias[...]
    qq, dd = two_heads(q[...]), two_heads(dm[...])
    scores = nt(qq, k[...]) * SCALE + jnp.concatenate([b, b], 0)
    weight = jnp.exp(scores - logs[0])
    dp = nt(dd, v[...])
    ds = (weight * (dp - jnp.sum(weight * dp, -1, keepdims=True))).astype(BF)
    dq[...] = (one_pair(mm(ds, k[...])) * SCALE).astype(BF)
    dkv[0] = (tn(ds, qq) * SCALE).astype(BF)
    dkv[1] = tn(weight.astype(BF), dd).astype(BF)


def cross_weights(at, text_normed, normed, dq, dkv, grad):
    t = at[T]
    x = text_normed[...]
    grad[t] = tn(x, dkv[0]).astype(BF)
    grad[1 - t] = tn(x, dkv[1]).astype(BF)
    grad[2] = tn(normed[...], dq[...]).astype(BF)


def text_back(at, text, gains, w_kv, own, oth, grad, sums):
    c = at[C]
    d = nt(own[0], w_kv[:, half(c)])
    d = d + nt(oth[0], w_kv[:, half(1 - c)])
    d = d + nt(own[1], w_kv[:, pl.ds(pl.multiple_of(D + c * HALF, 128), HALF)])
    d = d + nt(oth[1], w_kv[:, pl.ds(pl.multiple_of(D + (1 - c) * HALF, 128), HALF)])
    normal, factor = stats(text[...].astype(F32))
    dx, gain, bias = norm_back(d, normal, factor, gain_of(gains, 1))
    grad[...] = dx

    @pl.when(pl.program_id(0) == 0)
    def _():
        sums[...] = jnp.zeros_like(sums)

    sums[0:1] += gain
    sums[1:2] += bias


def visual_back(at, d_normed, dq_own, dq_oth, w_q, visual, d_joined, gains, s1, s2, s3, grad, sums):
    c = at[C]
    d = d_normed[...] + nt(dq_own[...], w_q[:, half(c)]) + nt(dq_oth[...], w_q[:, half(1 - c)])
    normal, factor = stats(visual[...].astype(F32))
    dx, gain, bias = norm_back(d, normal, factor, gain_of(gains, 0))
    grad[...] = d_joined[...] + dx
    for i, (g, b) in enumerate(((gain, bias), (s1[0:1], s1[1:2]), (s2[0:1], s2[1:2]), (s3[0:1], s3[1:2]))):
        sums[i : i + 1], sums[i + 4 : i + 5] = g, b


def finish_a(at, r, ry, rc, ryc, g_query, g_keyval):
    t, c = at[T], at[C]
    for a, b, cc in ((r, ry, c), (rc, ryc, 1 - c)):
        g_keyval[:, pl.ds(pl.multiple_of(t * D + cc * HALF, 128), HALF)] = a[:, :HALF].astype(F32)
        g_keyval[:, pl.ds(pl.multiple_of((1 - t) * D + cc * HALF, 128), HALF)] = b[:, :HALF].astype(F32)
        g_query[:, half(cc)] = a[:, HALF:].astype(F32) + b[:, HALF:].astype(F32)


def finish_bcd(at, *refs):
    groups, (g_out, g_gate, g_self, g_qkv, g_up, g_down) = refs[:12], refs[12:]
    t, c = at[T], at[C]
    rows = g_out.shape[0]
    shards = D // rows
    t0, c0 = t == 0, c == 0
    b, cq, d = groups[0:4], groups[4:8], groups[8:12]

    def order(g, rs, ls):
        own, y, core, both = [r[rs, ls].astype(F32) for r in g]
        a0, a1 = jnp.where(c0, own, core), jnp.where(c0, core, own)
        b0, b1 = jnp.where(c0, y, both), jnp.where(c0, both, y)
        return jnp.where(t0, a0, b0), jnp.where(t0, a1, b1), jnp.where(t0, b0, a0), jnp.where(t0, b1, a1)

    every = slice(None)
    p = order(b, every, slice(0, HALF))
    for i in range(4):
        g_gate[(i // 2) * rows : (i // 2 + 1) * rows, (i % 2) * HALF : (i % 2 + 1) * HALF] = p[i]
    p = order(b, every, slice(HALF, D))
    g_out[...] = jnp.concatenate(p[:2], 1)
    g_self[...] = jnp.concatenate(p[2:], 1)
    for i in range(3):
        p = order(cq, every, slice(i * QUART, (i + 1) * QUART))
        g_qkv[:, i * D : (i + 1) * D] = jnp.concatenate(p, 1)
    for s in range(shards):
        p = order(d, every, slice(s * rows, (s + 1) * rows))
        g_up[:, s * 4 * rows : (s + 1) * 4 * rows] = jnp.concatenate(p, 1)
    p = order(d, every, slice(D, 2 * D))
    for i in range(4):
        g_down[i * rows : (i + 1) * rows] = p[i]


def local(reps, shards, visual, text, visual_valid, block_owner, cross_query, cross_keyval, cross_output, gate_weight,
          self_qkv, self_output, ffn_up, ffn_down, norm_gains, norm_biases, cotangent):
    ln = Links(reps, shards)
    at = ln.at
    visual, text, cotangent = visual[0], text[0], cotangent[0]
    rows, size = cross_query.shape[0], norm_gains.shape[0]
    vis, txt = visual.shape[0], text.shape[0]
    depth = shards // 2
    split = (depth, 2, rows)

    (part_a,) = run(pack_a, [sds((rows + 16, D))], at, cross_query, cross_keyval,
                    norm_gains.reshape(1, size), norm_biases.reshape(1, size), name="pack_a")
    mine, other = ln.gather(part_a)
    kv_oo, q_own, gains, biases = run(
        functools.partial(join_a, rows, size),
        [sds(split + (HALF,)), sds(split + (HALF,)), sds((1, 4 * D), F32), sds((1, 4 * D), F32)],
        at, mine, other, name="join_a")
    kv_oo, q_own = kv_oo.reshape(D, HALF), q_own.reshape(D, HALF)
    kv_to = ln.y(kv_oo)
    kv_oc, q_oth, kv_tc = ln.core(kv_oo), ln.core(q_own), ln.core(kv_to)

    part_bc, part_d = run(pack_rest, [sds((rows, D + 3 * QUART)), sds((rows, 2 * D))], at,
                          cross_output, gate_weight, self_qkv, self_output, ffn_up, ffn_down, name="pack_rest")
    b_oo, c_own = run(join_bc, [sds(split + (D,)), sds(split + (3 * QUART,))], at, *ln.gather(part_bc), name="join_bc")
    b_oo, c_own = b_oo.reshape(shards, rows, D), c_own.reshape(D, 3 * QUART)
    b_to = ln.y(b_oo)
    b_oc, b_tc, c_oth = ln.core(b_oo), ln.core(b_to), ln.core(c_own)
    w_out, w_self, w_gate = run(
        place_b, [sds((shards, rows, D)), sds((shards, rows, D)), sds((shards, 2, rows, D))],
        at, b_oo, b_oc, b_to, b_tc, name="place_b")
    w_out, w_self, w_gate = w_out.reshape(D, D), w_self.reshape(D, D), w_gate.reshape(2 * D, D)
    (d_own,) = run(join_d, [sds(split + (2 * D,))], at, *ln.gather(part_d), name="join_d")
    d_own = d_own.reshape(D, 2 * D)
    d_oth = ln.core(d_own)

    valid = visual_valid.astype(F32)
    valid_y, cot_y = ln.y(valid), ln.y(cotangent)

    def whole(shape):
        return pl.BlockSpec(shape, lambda *_: (0,) * len(shape))

    def grid_run(body, grid, in_specs, outs, out_specs, *ins, scratch=(), flops=0, name=None, vmem=40):
        return pl.pallas_call(
            body, grid=grid, in_specs=in_specs, out_specs=out_specs, out_shape=outs,
            scratch_shapes=[pltpu.VMEM(s.shape, s.dtype) for s in scratch],
            compiler_params=pltpu.CompilerParams(vmem_limit_bytes=vmem << 20),
            cost_estimate=pl.CostEstimate(flops=flops, transcendentals=0,
                                          bytes_accessed=sum(size_of(a) for a in ins) + sum(size_of(o) for o in outs)),
            name=name)(*ins)

    tile = txt // 5
    row_tile = pl.BlockSpec((tile, D), lambda i: (i, 0))
    text_normed, kv, w_kv, w_q, normed, queries = grid_run(
        keyval_kernel, (5,),
        [SM, row_tile, whole((vis, D)), whole((1, 4 * D)), whole((1, 4 * D))] + [whole((D, HALF))] * 6,
        [sds((txt, D)), sds((txt, 2 * D)), sds((D, 2 * D)), sds((D, D)), sds((vis, D)), sds((vis, D))],
        [row_tile, pl.BlockSpec((tile, 2 * D), lambda i: (i, 0)), whole((D, 2 * D)), whole((D, D)), whole((vis, D)), whole((vis, D))],
        at, text, visual, gains, biases, kv_oo, kv_oc, kv_to, kv_tc, q_own, q_oth,
        flops=2 * (txt * 2 + vis) * D * D, name="keyval")
    pairs = H // 2
    col = lambda n, off=0, k=0: pl.BlockSpec((n, 128), lambda p: (0, p + off))
    mixed, logs = grid_run(
        cross_fwd, (pairs,),
        [whole((1, txt)), whole((1, vis)), col(vis), col(txt), col(txt, pairs)],
        [sds((vis, D)), sds((pairs, 2 * vis, 1), F32)],
        [col(vis), pl.BlockSpec((1, 2 * vis, 1), lambda p: (p, 0, 0))],
        block_owner, visual_valid, queries, kv, kv, scratch=[sds((vis, txt), F32)],
        flops=8 * vis * txt * D, name="cross_fwd")
    cross, gate, joined, second = run(
        gate_kernel, [sds((vis, D)), sds((vis, D), F32), sds((vis, D), F32), sds((vis, D))],
        at, mixed, normed, visual, gains, biases, w_out, w_gate, flops=6 * vis * D * D, name="gate")
    second_y = ln.y(second)
    triple, att_mine, att_send = run(
        self_fwd, [sds((2 * vis, 3 * HALF)), sds((vis, HALF)), sds((vis, HALF))],
        at, second, second_y, valid, valid_y, c_own, c_oth, flops=8 * vis * D * D, name="self_fwd")
    attended, carried, third = run(
        carry_kernel, [sds((vis, D)), sds((vis, D), F32), sds((vis, D))],
        at, att_mine, ln.y(att_send), joined, gains, biases, w_self, flops=2 * vis * D * D, name="carry")
    third_y = ln.y(third)

    page = sds((vis, D), F32)
    y0, y1, d0, d1, grad_d_oth = run(
        functools.partial(ffn_kernel, False), [page] * 4 + [sds((D, 2 * D))],
        at, third, third_y, cotangent, cot_y, d_oth, flops=24 * vis * D * D, name="ffn_first")
    grad_d_came = ln.core(grad_d_oth)
    y0, y1, d0, d1, grad_d = run(
        functools.partial(ffn_kernel, True), [page, sds((vis, D))] * 2 + [sds((D, 2 * D))],
        at, third, third_y, cotangent, cot_y, d_own, y0, y1, d0, d1, flops=24 * vis * D * D, name="ffn_second")
    d1 = ln.y(d1)
    layer_out = (carried + y0 + ln.y(y1).astype(F32)).astype(BF)
    sum_d = ln.scatter([g.reshape(shards, rows, 2 * D) for g in (grad_d, grad_d_came)])

    d_carried, da_mine, da_send, g_self, sums3 = run(
        carry_back, [page, sds((vis, HALF)), sds((vis, HALF)), sds((D, D)), sds((2, D), F32)],
        at, d0, d1, carried, cotangent, attended, gains, w_self, flops=4 * vis * D * D, name="carry_back")
    ds0, ds1, g_c_own, g_c_oth = run(
        self_back, [page, sds((vis, D)), sds((D, 3 * QUART)), sds((D, 3 * QUART))],
        at, triple, da_mine, ln.y(da_send), valid, valid_y, second, second_y, c_own, c_oth,
        scratch=[sds((2 * vis, 3 * HALF))], flops=16 * vis * D * D, name="self_back")
    g_c_came = ln.core(g_c_oth)
    d_joined, d_mixed, d_normed, b_keep, b_send, sums2 = run(
        gate_back, [page, sds((vis, D)), page, sds((2, shards, rows, D)), sds((2, shards, rows, D)), sds((2, D), F32)],
        at, d_carried, ds0, ln.y(ds1), joined, normed, cross, gate, mixed, gains, w_gate, w_out, g_self,
        flops=12 * vis * D * D, name="gate_back")
    sum_c = ln.scatter([g.reshape(shards, rows, 3 * QUART) for g in (g_c_own, g_c_came)])

    def add_core(keep, came):
        def body(at, keep, came, *outs):
            for i, out in enumerate(outs):
                out[...] = (keep[i].astype(F32) + came[i].astype(F32)).astype(BF)

        return run(body, [sds(keep.shape[1:])] * keep.shape[0], at, keep, came, name="add_core")

    own_b, oth_b = add_core(b_keep, ln.core(b_send))
    sum_b = ln.scatter([own_b, ln.y(oth_b)])

    def back_half(index):
        def spec(n, off=0):
            return pl.BlockSpec((n, 128), lambda p, at: (0, (at[C] ^ index) * 3 + p + off))

        fixed = lambda shape: pl.BlockSpec(shape, lambda p, at: (0,) * len(shape))
        ins = (at, block_owner, visual_valid, queries, kv, kv, d_mixed, logs)
        outs = [sds((vis, HALF)), sds((2, txt, HALF))]
        return pl.pallas_call(
            lambda at, *refs: cross_back(*refs),
            grid_spec=pltpu.PrefetchScalarGridSpec(
                num_scalar_prefetch=1, grid=(3,),
                in_specs=[fixed((1, txt)), fixed((1, vis)), spec(vis), spec(txt), spec(txt, pairs), spec(vis),
                          pl.BlockSpec((1, 2 * vis, 1), lambda p, at: ((at[C] ^ index) * 3 + p, 0, 0))],
                out_specs=[pl.BlockSpec((vis, 128), lambda p, at: (0, p)),
                           pl.BlockSpec((2, txt, 128), lambda p, at: (0, 0, p))],
                scratch_shapes=[pltpu.VMEM((vis, txt), F32)]),
            out_shape=outs,
            compiler_params=pltpu.CompilerParams(vmem_limit_bytes=30 << 20),
            cost_estimate=pl.CostEstimate(flops=10 * vis * txt * D, transcendentals=0,
                                          bytes_accessed=sum(size_of(a) for a in ins) + sum(size_of(o) for o in outs)),
            name="cross_back")(*ins)

    def weights_half(dq, dkv):
        (grad,) = run(cross_weights, [sds((3, D, HALF))], at, text_normed, normed, dq, dkv,
                      flops=2 * txt * D * D, name="cross_weights")
        return grad

    dq_oth, dkv_oth = back_half(1)
    a_send = weights_half(dq_oth, dkv_oth)
    a_came = ln.core(a_send)
    dq_own, dkv_own = back_half(0)
    a_keep = weights_half(dq_own, dkv_own)

    def add_a(at, keep, came, own, oth):
        own[:, :HALF] = (keep[0].astype(F32) + came[0].astype(F32)).astype(BF)
        own[:, HALF:] = (keep[2].astype(F32) + came[2].astype(F32)).astype(BF)
        oth[...] = (keep[1].astype(F32) + came[1].astype(F32)).astype(BF)

    own_a, oth_a = run(add_a, [sds((D, D)), sds((D, HALF))], at, a_keep, a_came, name="add_a")
    oth_a = ln.y(oth_a)

    def add_y(at, own, came, out):
        out[:, :HALF] = (own[:, :HALF].astype(F32) + came[...].astype(F32)).astype(BF)
        out[:, HALF:] = own[:, HALF:]

    (own_a,) = run(add_y, [sds((D, D))], at, own_a, oth_a, name="add_y")
    sum_a = ln.scatter([own_a.reshape(shards, rows, D)])

    row3 = pl.BlockSpec((2, tile, HALF), lambda i: (0, i, 0))
    grad_text, sums1 = grid_run(
        text_back, (5,), [SM, row_tile, whole((1, 4 * D)), whole((D, 2 * D)), row3, row3],
        [sds((txt, D), F32), sds((2, D), F32)], [row_tile, whole((2, D))],
        at, text, gains, w_kv, dkv_own, dkv_oth, flops=4 * txt * D * D, name="text_back")
    grad_visual, sums = run(
        visual_back, [page, sds((8, D), F32)],
        at, d_normed, dq_own, dq_oth, w_q, visual, d_joined, gains, sums1, sums2, sums3, flops=2 * vis * D * D, name="visual_back")
    sums = ln.total(sums).reshape(2, shards, size)
    sums = lax.dynamic_index_in_dim(sums, ln.shard, 1, False)

    def groups(r):
        ry = ln.y(r)
        return r, ry, ln.core(r), ln.core(ry)

    out = lambda r, n: sds((r, n), F32)
    g_out, g_gate, g_self_out, g_qkv, g_up, g_down = run(
        finish_bcd,
        [out(rows, D), out(2 * rows, D), out(rows, D), out(rows, 3 * D), out(rows, 4 * D), out(4 * rows, D)],
        at, *groups(sum_b), *groups(sum_c), *groups(sum_d), name="finish_bcd")
    g_query, g_keyval = run(finish_a, [out(rows, D), out(rows, 2 * D)], at, *groups(sum_a), name="finish_a")
    return (layer_out[None], grad_visual[None], grad_text[None], g_query, g_keyval, g_out, g_gate, g_qkv, g_self_out,
            g_up, g_down, sums[0], sums[1])


def solution(mesh):
    pages = P(("rep", "fsdp"), None, None)
    flags = P(("rep", "fsdp"), None)
    matrix = P("fsdp", None)
    vector = P("fsdp")
    in_specs = (pages, pages, flags, flags) + (matrix,) * 8 + (vector, vector, pages)
    out_specs = (pages, pages, pages) + (matrix,) * 8 + (vector, vector)
    reps, shards = mesh.shape["rep"], mesh.shape["fsdp"]

    def program(*args):
        return local(reps, shards, *args)

    return jax.shard_map(program, mesh=mesh, in_specs=in_specs, out_specs=out_specs, check_vma=False)
```

```python
import functools

import jax
import jax.numpy as jnp
from jax import lax
from jax.experimental import pallas as pl
from jax.experimental.pallas import tpu as pltpu
from jax.sharding import PartitionSpec as P

H = 12
HD = 64
D = H * HD
HALF = D // 2
QUART = D // 4
BF = jnp.bfloat16
F32 = jnp.float32

epsilon = 1e-05
filtered_logits = -1000000000.0
shared_sheet_reward = 6.0
SCALE = HD ** (-0.5)
VM = pl.BlockSpec()
SM = pl.BlockSpec(memory_space=pltpu.SMEM)
ANY = pl.BlockSpec(memory_space=pl.ANY)


def sds(shape, dtype=BF):
    return jax.ShapeDtypeStruct(tuple(shape), dtype)


def size_of(a):
    n = jnp.dtype(a.dtype).itemsize
    for d in a.shape:
        n *= d
    return n


class Order:
    def __init__(self):
        self.tokens = []

    def start(self, exchange, a, *args):
        a, *self.tokens = lax.optimization_barrier((a, *self.tokens))
        return exchange(a, *args)

    def wait(self, *arrays):
        self.tokens = self.tokens + list(arrays)

    def run(self, body, outs, where, *ins, name=None, scratch=(), grid=None, in_specs=None, out_specs=None, vmem=None, prefetch=False, far=False):
        moved = sum(size_of(a) for a in ins) + sum(size_of(o) for o in outs)
        held = moved + sum(size_of(s) for s in scratch)
        limit = 66_000_000 if far else vmem << 20 if vmem else min(60 << 20, int(1.25 * held) + (10 << 20))
        ins_specs = ([VM] * len(ins) if in_specs is None else in_specs) + [ANY] * len(self.tokens)
        spec = dict(in_specs=([] if prefetch else [SM]) + ins_specs,
                    out_specs=[VM] * len(outs) if out_specs is None else out_specs,
                    scratch_shapes=[pltpu.VMEM(s.shape, s.dtype) for s in scratch])
        if prefetch:
            spec = dict(grid_spec=pltpu.PrefetchScalarGridSpec(num_scalar_prefetch=1, grid=grid, **spec))
        elif grid is not None:
            spec["grid"] = grid
        kernel, count, late = body, len(ins), len(self.tokens)
        if far:
            spec["in_specs"] = [SM] + [pl.BlockSpec(memory_space=pltpu.HBM)] * count + [ANY] * late
            spec["scratch_shapes"] = [pltpu.VMEM(a.shape, a.dtype) for a in ins] + [pltpu.SemaphoreType.DMA((count,))]

            def kernel(at, *refs):
                held, sems = refs[-1 - count : -1], refs[-1]
                copies = [pltpu.make_async_copy(refs[i], held[i], sems.at[i]) for i in range(count)]
                for one in copies:
                    one.start()
                for one in copies:
                    one.wait()
                body(at, *held, *refs[count : -1 - count])

        got = pl.pallas_call(
            lambda at, *refs: kernel(at, *refs[:count], *refs[count + late :]),
            out_shape=list(outs),
            compiler_params=pltpu.CompilerParams(vmem_limit_bytes=limit),
            cost_estimate=pl.CostEstimate(flops=0, bytes_accessed=1024, transcendentals=0),
            name=name,
            **spec,
        )(where, *ins, *self.tokens)
        self.tokens = [min(got, key=size_of)]
        return got


T, C, X, Z = 0, 1, 2, 3


class Links:
    def __init__(self, reps, shards):
        self.reps, self.shards = reps, shards
        self.depth = shards // 2
        rank = lax.axis_index("rep")
        shard = lax.axis_index("fsdp")
        self.shard = shard
        self.at = jnp.stack([(rank // 2) % 2, rank % 2, shard % 2, shard // 2]).astype(jnp.int32)

    def core(self, a):
        return lax.ppermute(a, "rep", [(r, r ^ 1) for r in range(self.reps)])

    def y(self, a):
        return lax.ppermute(a, "rep", [(r, r ^ 2) for r in range(self.reps)])

    def rep_bit(self, a, bit):
        return lax.ppermute(a, "rep", [(r, r ^ bit) for r in range(self.reps)])

    def across(self, a):
        return lax.ppermute(a, "fsdp", [(s, s ^ 1) for s in range(self.shards)])

    def along(self, a, k):
        return lax.ppermute(a, "fsdp", [(s, s ^ (2 * k)) for s in range(self.shards)])


def mm(a, b):
    return jnp.dot(a, b, preferred_element_type=F32)


def nt(a, b):
    return lax.dot_general(a, b, (((1,), (1,)), ((), ())), preferred_element_type=F32)


def tn(a, b):
    return lax.dot_general(a, b, (((0,), (0,)), ((), ())), preferred_element_type=F32)


def stats(rows):
    mean = jnp.mean(rows, -1, keepdims=True)
    centred = rows - mean
    factor = lax.rsqrt(jnp.mean(centred * centred, -1, keepdims=True) + epsilon)
    return centred * factor, factor


def norm_back(grad, normal, factor, gain):
    scaled = grad * gain
    dx = scaled - jnp.mean(scaled, -1, keepdims=True) - normal * jnp.mean(scaled * normal, -1, keepdims=True)
    return dx * factor, jnp.sum(grad * normal, 0, keepdims=True), jnp.sum(grad, 0, keepdims=True)


def gain_of(ref, i):
    return ref[:, i * D : (i + 1) * D]


def half(i):
    return pl.ds(pl.multiple_of(i * HALF, 128), HALF)


def pair_masks(rows):
    lane = lax.broadcasted_iota(jnp.int32, (rows, 128), 1)
    return lane < HD


def two_heads(a):
    first = pair_masks(a.shape[0])
    zero = jnp.zeros_like(a)
    return jnp.concatenate([jnp.where(first, a, zero), jnp.where(first, zero, a)], 0)


def one_pair(a):
    n = a.shape[0] // 2
    return jnp.where(pair_masks(n), a[:n], a[n:])


def softmax(scores):
    peak = jnp.max(scores, -1, keepdims=True)
    expo = jnp.exp(scores - peak)
    total = jnp.sum(expo, -1, keepdims=True)
    return expo / total, peak + jnp.log(total)


def pack_a(at, query, keyval, gains, biases, part):
    rows, size = query.shape[0], gains.shape[0]
    part[:rows, :HALF] = keyval[:, pl.ds(pl.multiple_of(at[T] * D + at[C] * HALF, 128), HALF)]
    part[:rows, HALF:] = query[:, half(at[C])]
    part[rows:, :] = jnp.zeros((16, D), BF)
    g, b = gains[...].reshape(1, size), biases[...].reshape(1, size)
    g_hi, b_hi = g.astype(BF), b.astype(BF)
    g_lo, b_lo = (g - g_hi.astype(F32)).astype(BF), (b - b_hi.astype(F32)).astype(BF)
    row = lax.broadcasted_iota(jnp.int32, (16, size), 0)
    out = jnp.zeros((16, size), F32)
    for i, v in enumerate((g_hi, g_lo, b_hi, b_lo)):
        out = jnp.where(row == i, jnp.broadcast_to(v.astype(F32), (16, size)), out)
    part[rows:, HALF : HALF + size] = out.astype(BF)


def pack_rest(at, output, gate, qkv, self_out, up, down, part_b, part_c, part_d):
    rows = output.shape[0]
    shards = D // rows
    t0, c0 = at[T] == 0, at[C] == 0
    gate_c, out_c, self_c = gate[:, half(at[C])], output[:, half(at[C])], self_out[:, half(at[C])]
    part_b[:, :HALF] = jnp.where(t0, gate_c[:rows], gate_c[rows:])
    part_b[:, HALF:D] = jnp.where(t0, out_c, self_c)
    pieces = []
    for i in range(3):
        v = qkv[:, pl.ds(pl.multiple_of(i * D + at[T] * HALF, 128), HALF)]
        pieces.append(jnp.where(c0, v[:, :QUART], v[:, QUART:]))
    part_c[...] = jnp.concatenate(pieces, 1)
    pieces = []
    for s in range(shards):
        v = [up[:, (s * 4 + g) * rows : (s * 4 + g + 1) * rows] for g in range(4)]
        pieces.append(jnp.where(t0, jnp.where(c0, v[0], v[1]), jnp.where(c0, v[2], v[3])))
    part_d[:, :D] = jnp.concatenate(pieces, 1)
    v = [down[g * rows : (g + 1) * rows, :] for g in range(4)]
    part_d[:, D:] = jnp.where(t0, jnp.where(c0, v[0], v[1]), jnp.where(c0, v[2], v[3]))


def column(at, *refs):
    for k, piece in enumerate(refs[:-1]):
        refs[-1][at[Z] ^ k] = piece[...]


def column_a(at, *refs):
    kv, qn = refs[-2:]
    rows = kv.shape[1]
    for k, piece in enumerate(refs[:-2]):
        kv[at[Z] ^ k] = piece[:rows, :HALF]
        qn[at[Z] ^ k] = piece[:, HALF:]


def column_rest(at, *refs):
    whole, rest = refs[-2:]
    for k, piece in enumerate(refs[:-2]):
        whole[at[Z] ^ k] = piece[...]
        if k:
            rest[k - 1] = piece[...]


def join_rest(at, mine, other_own, other_rest, out):
    depth = mine.shape[0]
    for z in range(depth):
        out[z, at[X]] = mine[z]
    for k in range(depth):
        out[at[Z] ^ k, 1 - at[X]] = other_own[...] if k == 0 else other_rest[k - 1]


def join(at, mine, other, out):
    for src, side in ((mine, at[X]), (other, 1 - at[X])):
        for z in range(mine.shape[0]):
            out[z, side] = src[z]


def join_b(at, mine, other, y_mine, y_other, out):
    for i, pair in enumerate(((mine, other), (y_mine, y_other))):
        for src, side in zip(pair, (at[X], 1 - at[X])):
            for z in range(src.shape[0]):
                out[i, z, side] = src[z]


def join_a(at, kvm, kvo, kym, kyo, qm, qo, out, gains, biases):
    _three, depth, _two, rows, _n = out.shape
    size = 4 * D // (2 * depth)
    for i, pair in enumerate(((kvm, kvo), (kym, kyo), (qm, qo))):
        for src, side in zip(pair, (at[X], 1 - at[X])):
            for z in range(depth):
                out[i, z, side] = src[z, :rows]
    first = at[X] == 0
    for z in range(depth):
        a, b = qm[z, rows:, :size].astype(F32), qo[z, rows:, :size].astype(F32)
        for i, v in enumerate((jnp.where(first, a, b), jnp.where(first, b, a))):
            s = (z * 2 + i) * size
            gains[:, s : s + size] = v[0:1] + v[1:2]
            biases[:, s : s + size] = v[2:3] + v[3:4]


def place_b(at, own, came, cross_out, self_out, gate):
    t, c = at[T], at[C]
    for src, cc in ((own, c), (came, 1 - c)):
        for i in range(2):
            gate[:, t ^ i, :, half(cc)] = src[i, :, :, :HALF]
        cross_out[:, :, half(cc)] = src[t, :, :, HALF:]
        self_out[:, :, half(cc)] = src[1 - t, :, :, HALF:]


def normed_kernel(at, text, visual, gains, biases, text_normed, normed):
    normal, _f = stats(text[...].astype(F32))
    text_normed[...] = (normal * gain_of(gains, 1) + gain_of(biases, 1)).astype(BF)
    normal, _f = stats(visual[...].astype(F32))
    normed[...] = (normal * gain_of(gains, 0) + gain_of(biases, 0)).astype(BF)


def keyval_kernel(at, text_normed, normed, own, came, kv, w_kv, w_q, queries):
    t, c = at[T], at[C]

    @pl.when(pl.program_id(0) == 0)
    def _():
        for src, cc in ((own, c), (came, 1 - c)):
            for i in range(2):
                w_kv[:, pl.ds(pl.multiple_of((t ^ i) * D + cc * HALF, 128), HALF)] = src[i]
            w_q[:, half(cc)] = src[2]
        queries[...] = mm(normed[...], w_q[...]).astype(BF)

    kv[...] = mm(text_normed[...], w_kv[...]).astype(BF)


def cross_bias(owner, valid):
    n, m = valid.shape[1], owner.shape[1]
    parent = owner[...] == lax.broadcasted_iota(jnp.int32, (n, m), 0)
    ones = jnp.where(parent, 1.0, 0.0).astype(BF)
    real = jnp.broadcast_to(valid[...].astype(F32), (8, n)).astype(BF)
    present = mm(real, ones)[0:1] > 0.5
    return jnp.where(parent, shared_sheet_reward, 0.0) + jnp.where(present, 0.0, filtered_logits)


def cross_fwd(owner, valid, q, k, v, out, logs, bias):
    @pl.when(pl.program_id(0) == 0)
    def _():
        bias[...] = cross_bias(owner, valid)

    b = bias[...]
    scores = nt(two_heads(q[...]), k[...]) * SCALE + jnp.concatenate([b, b], 0)
    weight, log = softmax(scores)
    logs[0] = log
    out[...] = one_pair(mm(weight.astype(BF), v[...])).astype(BF)


def gate_kernel(at, mixed, normed, visual, gains, biases, w_out, w_gate, cross, gate, joined, second):
    rows = mm(mixed[...], w_out[...]).astype(BF)
    cross[...] = rows
    g = jax.nn.sigmoid(mm(normed[...], w_gate[:D]) + mm(rows, w_gate[D:]))
    gate[...] = g
    j = visual[...].astype(F32) + g * rows.astype(F32)
    joined[...] = j
    normal, _f = stats(j)
    second[...] = (normal * gain_of(gains, 2) + gain_of(biases, 2)).astype(BF)


def head_order(at, a):
    return jnp.where(at[C] == 0, a, jnp.concatenate([a[:, QUART:], a[:, :QUART]], 1))


def self_bias(valid):
    return jnp.where(valid > 0.5, 0.0, filtered_logits)


def self_fwd(at, second0, second1, valid0, valid1, w_own, w_oth, triple, att0, att1):
    n = second0.shape[0]
    rows = jnp.concatenate([second0[...], second1[...]], 0)
    own, oth = [mm(rows, w[...]).astype(BF) for w in (w_own, w_oth)]
    for i in range(3):
        triple[:, i * HALF : (i + 1) * HALF] = jnp.concatenate(
            [own[:, i * QUART : (i + 1) * QUART], oth[:, i * QUART : (i + 1) * QUART]], 1)
    for page, (valid, att) in enumerate(((valid0, att0), (valid1, att1))):
        bias = self_bias(valid[...])
        r = slice(page * n, (page + 1) * n)
        outs = []
        for p in range(3):
            q, k, v = [triple[r, i * HALF + p * 128 : i * HALF + (p + 1) * 128] for i in range(3)]
            weight, _l = softmax(nt(two_heads(q), k) * SCALE + bias)
            outs.append(one_pair(mm(weight.astype(BF), v)).astype(BF))
        att[...] = head_order(at, jnp.concatenate(outs, 1))


def carry_kernel(at, mine, came, joined, gains, biases, w, attended, carried, third):
    attended[:, half(at[T])] = mine[...]
    attended[:, half(1 - at[T])] = came[...]
    c = joined[...] + mm(attended[...], w[...])
    carried[...] = c
    normal, _f = stats(c)
    third[...] = (normal * gain_of(gains, 3) + gain_of(biases, 3)).astype(BF)


def ffn_kernel(last, at, third0, third1, cot0, cot1, w, *refs):
    n = third0.shape[0]
    if last:
        y0i, y1i, d0i, d1i, y0, y1, d0, d1, grad = refs
    else:
        y0, y1, d0, d1, grad = refs
    rows = jnp.concatenate([third0[...], third1[...]], 0)
    cot = jnp.concatenate([cot0[...], cot1[...]], 0)
    up, down = w[:, :D], w[:, D:]
    v = mm(rows, up)
    k = (2.0 / 3.141592653589793) ** 0.5
    th = jnp.tanh(k * (v + 0.044715 * (v * v * v)))
    act = (0.5 * v * (1.0 + th)).astype(BF)
    slope = 0.5 * (1.0 + th) + 0.5 * v * (1.0 - th * th) * (k * (1.0 + 3.0 * 0.044715 * (v * v)))
    y = mm(act, down)
    grad[:, D:] = tn(act, cot).astype(BF)
    dl = (nt(cot, down) * slope).astype(BF)
    d = nt(dl, up)
    grad[:, :D] = tn(rows, dl).astype(BF)
    if last:
        y0[...] = y[:n] + y0i[...]
        y1[...] = (y[n:] + y1i[...]).astype(BF)
        d0[...] = d[:n] + d0i[...]
        d1[...] = (d[n:] + d1i[...]).astype(BF)
    else:
        y0[...], y1[...], d0[...], d1[...] = y[:n], y[n:], d[:n], d[n:]


def carry_back(at, d0, came, carried, cot, attended, gains, w, d_carried, mine, send, grad, sums):
    normal, factor = stats(carried[...])
    dx, gain, bias = norm_back(d0[...] + came[...].astype(F32), normal, factor, gain_of(gains, 3))
    dc = cot[...].astype(F32) + dx
    d_carried[...] = dc
    low = dc.astype(BF)
    da = nt(low, w[...]).astype(BF)
    t0 = at[T] == 0
    mine[...] = head_order(at, jnp.where(t0, da[:, :HALF], da[:, HALF:]))
    send[...] = head_order(at, jnp.where(t0, da[:, HALF:], da[:, :HALF]))
    grad[...] = tn(attended[...], low).astype(BF)
    sums[0:1], sums[1:2] = gain, bias


def self_back(at, triple, da0, da1, valid0, valid1, second0, second1, w_own, w_oth, d0, d1, g_own, g_oth, dt):
    n = second0.shape[0]
    for page, (valid, da) in enumerate(((valid0, da0), (valid1, da1))):
        bias = self_bias(valid[...])
        r = slice(page * n, (page + 1) * n)
        for p in range(3):
            q, k, v = [triple[r, i * HALF + p * 128 : i * HALF + (p + 1) * 128] for i in range(3)]
            qq = two_heads(q)
            dd = two_heads(da[:, p * 128 : (p + 1) * 128])
            weight, _l = softmax(nt(qq, k) * SCALE + bias)
            dp = nt(dd, v)
            ds = (weight * (dp - jnp.sum(weight * dp, -1, keepdims=True))).astype(BF)
            grads = (one_pair(mm(ds, k)) * SCALE, tn(ds, qq) * SCALE, tn(weight.astype(BF), dd))
            for i in range(3):
                dt[r, i * HALF + p * 128 : i * HALF + (p + 1) * 128] = grads[i].astype(BF)
    own = jnp.concatenate([dt[:, i * HALF : i * HALF + QUART] for i in range(3)], 1)
    oth = jnp.concatenate([dt[:, i * HALF + QUART : (i + 1) * HALF] for i in range(3)], 1)
    rows = jnp.concatenate([second0[...], second1[...]], 0)
    g_own[...] = tn(rows, own).astype(BF).reshape(g_own.shape)
    g_oth[...] = tn(rows, oth).astype(BF).reshape(g_oth.shape)
    d = nt(own, w_own[...]) + nt(oth, w_oth[...])
    d0[...] = d[:n]
    d1[...] = d[n:].astype(BF)


def gate_back(at, d_carried, d0, came, joined, normed, cross, gate, mixed, gains, w_gate, w_out, g_self,
              d_joined, d_mixed, d_normed, keep, send, sums):
    t, c = at[T], at[C]
    rows = keep.shape[2]
    normal, factor = stats(joined[...])
    dx, gain, bias = norm_back(d0[...] + came[...].astype(F32), normal, factor, gain_of(gains, 2))
    dj = d_carried[...] + dx
    d_joined[...] = dj
    sums[0:1], sums[1:2] = gain, bias
    g = gate[...]
    dg = (dj * cross[...].astype(F32) * g * (1.0 - g)).astype(BF)
    d_normed[...] = nt(dg, w_gate[:D])
    dc = (dj * g + nt(dg, w_gate[D:])).astype(BF)
    d_mixed[...] = nt(dc, w_out[...]).astype(BF)
    g_gate = jnp.concatenate([tn(normed[...], dg).astype(BF), tn(cross[...], dg).astype(BF)], 0)
    g_gate = g_gate.reshape(D // rows, 2, rows, D)
    g_out = tn(mixed[...], dc).astype(BF).reshape(D // rows, rows, D)
    g_so = g_self[...].reshape(D // rows, rows, D)
    for tt in range(2):
        for cc in range(2):
            lanes = slice(cc * HALF, (cc + 1) * HALF)
            side = g_out if tt == 0 else g_so
            for out, same in ((keep, True), (send, False)):
                @pl.when((c == cc) == same)
                def _():
                    out[t ^ tt, :, :, :HALF] = g_gate[:, tt, :, lanes]
                    out[t ^ tt, :, :, HALF:] = side[:, :, lanes]


def cross_back(owner, valid, q, k, v, dm, logs, dq, dkv, bias):
    @pl.when(pl.program_id(0) == 0)
    def _():
        bias[...] = cross_bias(owner, valid)

    b = bias[...]
    qq, dd = two_heads(q[...]), two_heads(dm[...])
    scores = nt(qq, k[...]) * SCALE + jnp.concatenate([b, b], 0)
    weight = jnp.exp(scores - logs[0])
    dp = nt(dd, v[...])
    ds = (weight * (dp - jnp.sum(weight * dp, -1, keepdims=True))).astype(BF)
    dq[...] = (one_pair(mm(ds, k[...])) * SCALE).astype(BF)
    dkv[0] = (tn(ds, qq) * SCALE).astype(BF)
    dkv[1] = tn(weight.astype(BF), dd).astype(BF)


def cross_weights(at, text_normed, normed, dq, dkv, grad):
    t = at[T]
    x = text_normed[...]
    grad[t] = tn(x, dkv[0]).astype(BF)
    grad[1 - t] = tn(x, dkv[1]).astype(BF)
    grad[2] = tn(normed[...], dq[...]).astype(BF)


def text_back(at, text, gains, w_kv, own, oth, grad, sums):
    c = at[C]
    d = nt(own[0], w_kv[:, half(c)])
    d = d + nt(oth[0], w_kv[:, half(1 - c)])
    d = d + nt(own[1], w_kv[:, pl.ds(pl.multiple_of(D + c * HALF, 128), HALF)])
    d = d + nt(oth[1], w_kv[:, pl.ds(pl.multiple_of(D + (1 - c) * HALF, 128), HALF)])
    normal, factor = stats(text[...].astype(F32))
    dx, gain, bias = norm_back(d, normal, factor, gain_of(gains, 1))
    grad[...] = dx

    @pl.when(pl.program_id(0) == 0)
    def _():
        sums[...] = jnp.zeros_like(sums)

    sums[0:1] += gain
    sums[1:2] += bias


def visual_back(at, d_normed, dq_own, dq_oth, w_q, visual, d_joined, gains, s1, s2, s3, grad, norms):
    c = at[C]
    depth = norms.shape[0]
    size = 4 * D // (2 * depth)
    d = d_normed[...] + nt(dq_own[...], w_q[:, half(c)]) + nt(dq_oth[...], w_q[:, half(1 - c)])
    normal, factor = stats(visual[...].astype(F32))
    dx, gain, bias = norm_back(d, normal, factor, gain_of(gains, 0))
    grad[...] = d_joined[...] + dx
    g = jnp.concatenate([gain, s1[0:1], s2[0:1], s3[0:1]], 1)
    b = jnp.concatenate([bias, s1[1:2], s2[1:2], s3[1:2]], 1)
    row = lax.broadcasted_iota(jnp.int32, (16, size), 0)
    norms[...] = jnp.zeros_like(norms)
    for s in range(2 * depth):
        lanes = slice(s * size, (s + 1) * size)
        v = jnp.where(row == 0, jnp.broadcast_to(g[:, lanes], (16, size)), jnp.broadcast_to(b[:, lanes], (16, size)))
        norms[s // 2, s % 2, :, :size] = jnp.where(row < 2, v, 0.0).astype(BF)


def finish_ab(at, r, ry, rc, ryc, g_query, g_keyval, gains, biases):
    t, c = at[T], at[C]
    rows, size = g_query.shape[0], gains.shape[0]
    for a, b, cc in ((r, ry, c), (rc, ryc, 1 - c)):
        g_keyval[:, pl.ds(pl.multiple_of(t * D + cc * HALF, 128), HALF)] = a[:rows, :HALF].astype(F32)
        g_keyval[:, pl.ds(pl.multiple_of((1 - t) * D + cc * HALF, 128), HALF)] = b[:rows, :HALF].astype(F32)
        g_query[:, half(cc)] = a[:rows, HALF:].astype(F32) + b[:rows, HALF:].astype(F32)
    norms = [a[rows:, :size].astype(F32) for a in (r, ry, rc, ryc)]
    norms = norms[0] + norms[1] + norms[2] + norms[3]
    gains[...] = norms[0:1].reshape(size)
    biases[...] = norms[1:2].reshape(size)


def in_order(at, groups, lanes):
    c0, t0 = at[C] == 0, at[T] == 0
    own, y, core, both = [r[:, lanes].astype(F32) for r in groups]
    a0, a1 = jnp.where(c0, own, core), jnp.where(c0, core, own)
    b0, b1 = jnp.where(c0, y, both), jnp.where(c0, both, y)
    return jnp.where(t0, a0, b0), jnp.where(t0, a1, b1), jnp.where(t0, b0, a0), jnp.where(t0, b1, a1)


def finish_cd(at, r, ry, rc, ryc, g_qkv, g_up, g_down):
    groups = (r, ry, rc, ryc)
    rows = g_qkv.shape[0]
    p = in_order(at, groups, slice(0, D))
    for i in range(4):
        g_down[i * rows : (i + 1) * rows] = p[i]
    for s in range(D // rows):
        p = in_order(at, groups, slice(D + s * rows, D + (s + 1) * rows))
        g_up[:, s * 4 * rows : (s + 1) * 4 * rows] = jnp.concatenate(p, 1)
    for i in range(3):
        p = in_order(at, groups, slice(2 * D + i * QUART, 2 * D + (i + 1) * QUART))
        g_qkv[:, i * D : (i + 1) * D] = jnp.concatenate(p, 1)


def finish_b(at, r, ry, rc, ryc, g_out, g_gate, g_self):
    groups = (r, ry, rc, ryc)
    rows = g_out.shape[0]
    p = in_order(at, groups, slice(0, HALF))
    for i in range(4):
        g_gate[(i // 2) * rows : (i // 2 + 1) * rows, (i % 2) * HALF : (i % 2 + 1) * HALF] = p[i]
    p = in_order(at, groups, slice(HALF, D))
    g_out[...] = jnp.concatenate(p[:2], 1)
    g_self[...] = jnp.concatenate(p[2:], 1)


def reduce_x(count, extra, lanes, at, *refs):
    out = refs[-1]
    m = extra[0] if extra else 0
    for z in range(out.shape[0]):
        out[z] = reduced(refs, count, m, lanes, z, 1 - at[X]).astype(BF)


def reduced(refs, count, m, lanes, z, side):
    acc = refs[0][z, side, :, lanes].astype(F32)
    for r in refs[1:count]:
        acc = acc + r[z, side, :, lanes].astype(F32)
    if m:
        y = refs[count]
        y = (y[z, side] if len(y.shape) == 4 else y[z]).astype(F32)
        acc = acc + y if y.shape == acc.shape else jnp.concatenate([acc[:, :m] + y, acc[:, m:]], 1)
    return acc


def reduce_z(count, extra, lanes, at, *refs):
    got, keep, send = refs[-3:]
    m = extra[0] if extra else 0
    for i in range(keep.shape[0]):
        for k, out in ((2 * i, keep), (2 * i + 1, send)):
            z = at[Z] ^ k
            out[i] = (reduced(refs, count, m, lanes, z, at[X]) + got[z].astype(F32)).astype(BF)


def reduce_more(at, keep, got, *outs):
    for i in range(keep.shape[0]):
        v = (keep[i].astype(F32) + got[i].astype(F32)).astype(BF)
        if len(outs) == 1:
            outs[0][...] = v
        else:
            outs[i % 2][i // 2] = v


def reduce_last(count, at, *refs):
    out = refs[-1]
    at_lane = 0
    for keep, got in zip(refs[0 : 2 * count : 2], refs[1 : 2 * count : 2]):
        rows, n = keep.shape[1:]
        out[:rows, at_lane : at_lane + n] = (keep[0].astype(F32) + got[0].astype(F32)).astype(BF)
        at_lane += n
    if len(refs) > 2 * count + 1:
        keep, got = refs[2 * count : 2 * count + 2]
        out[rows:, :] = (keep[0].astype(F32) + got[0].astype(F32)).astype(BF)


def add_core_b(at, keep, came, own, oth_send, oth_keep):
    x = at[X]
    for z in range(own.shape[0]):
        for i in range(2):
            own[z, i] = (keep[0, z, i].astype(F32) + came[0, z, i].astype(F32)).astype(BF)
        oth_send[z] = (keep[1, z, 1 - x].astype(F32) + came[1, z, 1 - x].astype(F32)).astype(BF)
        oth_keep[z] = (keep[1, z, x].astype(F32) + came[1, z, x].astype(F32)).astype(BF)


def add_core_a(at, keep, came, own, oth):
    for z in range(own.shape[0]):
        for i in range(2):
            own[z, i, :, :HALF] = (keep[0, z, i].astype(F32) + came[0, z, i].astype(F32)).astype(BF)
            own[z, i, :, HALF:] = (keep[2, z, i].astype(F32) + came[2, z, i].astype(F32)).astype(BF)
            oth[z, i] = (keep[1, z, i].astype(F32) + came[1, z, i].astype(F32)).astype(BF)


def add_out(at, carried, y0, came, out):
    out[...] = (carried[...] + y0[...] + came[...].astype(F32)).astype(BF)


def local(reps, shards, visual, text, visual_valid, block_owner, cross_query, cross_keyval, cross_output, gate_weight,
          self_qkv, self_output, ffn_up, ffn_down, norm_gains, norm_biases, cotangent):
    ln = Links(reps, shards)
    at = ln.at
    od = Order()
    run = od.run
    visual, text, cotangent = visual[0], text[0], cotangent[0]
    rows, size = cross_query.shape[0], norm_gains.shape[0]
    vis, txt = visual.shape[0], text.shape[0]
    depth = shards // 2
    w3 = 3 * QUART
    whole = lambda shape: pl.BlockSpec(shape, lambda *_: (0,) * len(shape))
    page = sds((vis, D), F32)
    grid4 = lambda n: (depth, 2, rows, n)

    def far_first(part):
        pieces = {0: part}
        for k in range(depth - 1, 0, -1):
            if k & (k - 1) == 0:
                pieces[k] = od.start(ln.along, part, k)
        return pieces

    def passed_on(pieces):
        for k in sorted(range(1, depth), key=lambda k: (bin(k).count("1"), -k)):
            if k not in pieces:
                od.wait(*[pieces[i] for i in sorted(pieces) if i])
                pieces[k] = od.start(ln.along, pieces[k & (k - 1)], k & -k)
        return [pieces[k] for k in range(depth)]

    (part_a,) = run(pack_a, [sds((rows + 16, D))], at, cross_query, cross_keyval, norm_gains, norm_biases, name="pack_a", far=True)
    pieces_a = far_first(part_a)
    valid = visual_valid.astype(F32)
    valid_y = ln.y(valid)
    part_b, part_c, part_d = run(
        pack_rest, [sds((rows, D)), sds((rows, w3)), sds((rows, 2 * D))], at,
        cross_output, gate_weight, self_qkv, self_output, ffn_up, ffn_down, name="pack_rest", far=True)
    d_xo, cot_y = ln.across(part_d), od.start(ln.y, cotangent)
    pieces_a = passed_on(pieces_a)
    od.wait(d_xo, valid_y, cot_y)
    kv_m, qn_m = run(column_a, [sds((depth, rows, HALF)), sds((depth, rows + 16, HALF))], at, *pieces_a, name="column_a")
    kv_o, qn_o, kv_ym = ln.across(kv_m), ln.across(qn_m), ln.y(kv_m)
    pieces_b = passed_on(far_first(part_b))
    od.wait(kv_o)
    kv_yo = ln.y(kv_o)
    pieces_c = far_first(part_c)
    (b_m,) = run(column, [sds((depth, rows, D))], at, *pieces_b, name="column_b")
    joined_a, gains, biases = run(
        join_a, [sds((3,) + grid4(HALF)), sds((1, 4 * D), F32), sds((1, 4 * D), F32)],
        at, kv_m, kv_o, kv_ym, kv_yo, qn_m, qn_o, name="join_a")
    joined_a = joined_a.reshape(3, D, HALF)
    came_a = ln.core(joined_a)
    b_o, b_ym = od.start(ln.across, b_m), od.start(ln.y, b_m)
    tile = txt // 5
    row_tile = pl.BlockSpec((tile, D), lambda i: (i, 0))
    text_normed, normed = run(
        normed_kernel, [sds((txt, D)), sds((vis, D))], at, text, visual, gains, biases,
        grid=(5,), in_specs=[row_tile, whole((vis, D)), whole((1, 4 * D)), whole((1, 4 * D))],
        out_specs=[row_tile, whole((vis, D))], name="normed", vmem=12)
    pieces_c = passed_on(pieces_c)
    od.wait(came_a)

    kv, w_kv, w_q, queries = run(
        keyval_kernel, [sds((txt, 2 * D)), sds((D, 2 * D)), sds((D, D)), sds((vis, D))],
        at, text_normed, normed, joined_a, came_a,
        grid=(5,), in_specs=[row_tile, whole((vis, D)), whole((3, D, HALF)), whole((3, D, HALF))],
        out_specs=[pl.BlockSpec((tile, 2 * D), lambda i: (i, 0)), whole((D, 2 * D)), whole((D, D)), whole((vis, D))],
        name="keyval", vmem=30)
    (c_m,) = run(column, [sds((depth, rows, w3))], at, *pieces_c, name="column_c")
    od.wait(b_o, b_ym)
    c_o, b_yo = od.start(ln.across, c_m), od.start(ln.y, b_o)
    pieces_d = far_first(part_d)
    pairs = H // 2
    col = lambda n, off=0: pl.BlockSpec((n, 128), lambda p: (0, p + off))
    mixed, logs = run(
        lambda at, *refs: cross_fwd(*refs), [sds((vis, D)), sds((pairs, 2 * vis, 1), F32)],
        at, block_owner, visual_valid, queries, kv, kv,
        grid=(pairs,), in_specs=[whole((1, txt)), whole((1, vis)), col(vis), col(txt), col(txt, pairs)],
        out_specs=[col(vis), pl.BlockSpec((1, 2 * vis, 1), lambda p: (p, 0, 0))],
        scratch=[sds((vis, txt), F32)], name="cross_fwd", vmem=16)
    pieces_d = passed_on(pieces_d)
    (wc_own,) = run(join, [sds(grid4(w3))], at, c_m, c_o, name="join_c")
    wc_oth = ln.core(wc_own)
    (joined_b,) = run(join_b, [sds((2,) + grid4(D))], at, b_m, b_o, b_ym, b_yo, name="join_b")
    joined_b = joined_b.reshape(2, shards, rows, D)
    came_b = ln.core(joined_b)
    od.wait(wc_oth)
    d_m, d_rest = run(column_rest, [sds((depth, rows, 2 * D)), sds((depth - 1, rows, 2 * D))], at, *pieces_d, name="column_d")
    d_xr, d_cm, d_cxo = ln.across(d_rest), ln.core(d_m), od.start(ln.core, d_xo)
    wc_own, wc_oth = wc_own.reshape(D, w3), wc_oth.reshape(D, w3)
    w_out, w_self, w_gate = run(
        place_b, [sds((shards, rows, D)), sds((shards, rows, D)), sds((shards, 2, rows, D))], at, joined_b, came_b, name="place_b")
    w_out, w_self, w_gate = w_out.reshape(D, D), w_self.reshape(D, D), w_gate.reshape(2 * D, D)
    cross, gate, joined, second = run(
        gate_kernel, [sds((vis, D)), page, page, sds((vis, D))],
        at, mixed, normed, visual, gains, biases, w_out, w_gate, name="gate")
    second_y = ln.y(second)
    triple, att_mine, att_send = run(
        self_fwd, [sds((2 * vis, 3 * HALF)), sds((vis, HALF)), sds((vis, HALF))],
        at, second, second_y, valid, valid_y, wc_own, wc_oth, name="self_fwd")
    att_came = ln.y(att_send)
    od.wait(d_cm, d_cxo)
    attended, carried, third = run(
        carry_kernel, [sds((vis, D)), page, sds((vis, D))],
        at, att_mine, att_came, joined, gains, biases, w_self, name="carry")
    third_y = ln.y(third)
    od.wait(third_y)
    d_cxr = od.start(ln.core, d_xr)
    (wd_own,) = run(join_rest, [sds(grid4(2 * D))], at, d_m, d_xo, d_xr, name="join_d")
    (wd_oth,) = run(join_rest, [sds(grid4(2 * D))], at, d_cm, d_cxo, d_cxr, name="join_d")
    wd_own, wd_oth = wd_own.reshape(D, 2 * D), wd_oth.reshape(D, 2 * D)

    y0, y1, d0, d1, gd_oth = run(
        functools.partial(ffn_kernel, False), [page] * 4 + [sds((D, 2 * D))],
        at, third, third_y, cotangent, cot_y, wd_oth, name="ffn_first")
    gd_came = ln.core(gd_oth).reshape(grid4(2 * D))
    y0, y1, d0, d1, gd_own = run(
        functools.partial(ffn_kernel, True), [page, sds((vis, D))] * 2 + [sds((D, 2 * D))],
        at, third, third_y, cotangent, cot_y, wd_own, y0, y1, d0, d1, name="ffn_second")
    gd_own = gd_own.reshape(grid4(2 * D))
    d1_came = ln.y(d1)

    class Sum:
        def __init__(self, name, arrays, n, lanes=slice(None), sends=(), keeps=()):
            self.name, self.arrays, self.n, self.lanes, self.keeps = name, arrays, n, lanes, keeps
            self.extra = [a.shape[-1] for a in keeps]
            self.rows = arrays[0].shape[2]
            (self.send,) = run(functools.partial(reduce_x, len(arrays), self.extra, lanes), [sds((depth, self.rows, n))], at,
                               *arrays, *sends, name="reduce_x_" + name)
            self.bit = 0

        def go(self):
            self.got = od.start(ln.across, self.send)
            return self

        def step(self):
            if self.bit == 0:
                outs = [sds((depth // 2, self.rows, self.n))] * 2
                self.keep, send = run(functools.partial(reduce_z, len(self.arrays), self.extra, self.lanes), outs, at,
                                      *self.arrays, *self.keeps, self.got, name="reduce_z_" + self.name)
                self.bit = 1
            elif self.keep.shape[0] > 1:
                outs = [sds((self.keep.shape[0] // 2, self.rows, self.n))] * 2
                self.keep, send = run(reduce_more, outs, at, self.keep, self.got, name="reduce_m_" + self.name)
                self.bit *= 2
            else:
                return False
            self.got = ln.along(send, self.bit)
            return True

    def finish(sums, below=None):
        ins = [a for one in sums + ([below] if below else []) for a in (one.keep, one.got)]
        height = sums[0].rows + (below.rows if below else 0)
        (total,) = run(functools.partial(reduce_last, len(sums)), [sds((height, sum(one.n for one in sums)))], at,
                       *ins, name="reduce_last")
        for bit in range(2, reps.bit_length() - 1):
            total = (total.astype(F32) + ln.rep_bit(total, 1 << bit).astype(F32)).astype(BF)
        ry = ln.y(total)
        return total, ry, ln.core(total), ln.core(ry)

    def back_half(index):
        def spec(n, off=0):
            return pl.BlockSpec((n, 128), lambda p, at: (0, (at[C] ^ index) * 3 + p + off))

        return run(
            lambda at, *refs: cross_back(*refs), [sds((vis, HALF)), sds((2, txt, HALF))],
            at, block_owner, visual_valid, queries, kv, kv, d_mixed, logs, prefetch=True, grid=(3,),
            in_specs=[whole((1, txt)), whole((1, vis)), spec(vis), spec(txt), spec(txt, pairs), spec(vis),
                      pl.BlockSpec((1, 2 * vis, 1), lambda p, at: ((at[C] ^ index) * 3 + p, 0, 0))],
            out_specs=[pl.BlockSpec((vis, 128), lambda p, at: (0, p)), pl.BlockSpec((2, txt, 128), lambda p, at: (0, 0, p))],
            scratch=[sds((vis, txt), F32)], name="cross_back", vmem=20)

    def weights_half(dq, dkv):
        return run(cross_weights, [sds((3, D, HALF))], at, text_normed, normed, dq, dkv, name="cross_weights")[0]

    down = Sum("down", [gd_own, gd_came], D, slice(D, 2 * D)).go()
    d_carried, da_mine, da_send, g_self, sums3 = run(
        carry_back, [page, sds((vis, HALF)), sds((vis, HALF)), sds((D, D)), sds((2, D), F32)],
        at, d0, d1_came, carried, cotangent, attended, gains, w_self, name="carry_back")
    da_came = ln.y(da_send)
    up = Sum("up", [gd_own, gd_came], D, slice(0, D))
    od.wait(da_came)
    down.step()
    up.go()
    ds0, ds1, gc_own, gc_oth = run(
        self_back, [page, sds((vis, D)), sds(grid4(w3)), sds(grid4(w3))],
        at, triple, da_mine, da_came, valid, valid_y, second, second_y, wc_own, wc_oth,
        scratch=[sds((2 * vis, 3 * HALF))], name="self_back")
    ds1_came = ln.y(ds1)
    gc_came = ln.core(gc_oth)
    down.step()
    up.step()
    d_joined, d_mixed, d_normed, b_keep, b_send, sums2 = run(
        gate_back, [page, sds((vis, D)), page, sds((2, shards, rows, D)), sds((2, shards, rows, D)), sds((2, D), F32)],
        at, d_carried, ds0, ds1_came, joined, normed, cross, gate, mixed, gains, w_gate, w_out, g_self, name="gate_back")
    b_came = ln.core(b_send)
    y1_came = od.start(ln.y, y1)
    dq_oth, dkv_oth = back_half(1)
    qkv = Sum("qkv", [gc_own, gc_came], w3).go()
    od.wait(y1_came)
    own_b, b_ys, b_yk = run(
        add_core_b, [sds(grid4(D)), sds((depth, rows, D)), sds((depth, rows, D))], at,
        b_keep.reshape((2,) + grid4(D)), b_came.reshape((2,) + grid4(D)), name="add_core_b")
    b_ys = ln.y(b_ys)
    up.step()
    dq_own, dkv_own = back_half(0)
    od.wait(down.got)
    qkv.step()
    a_send = weights_half(dq_oth, dkv_oth)
    gates = Sum("gate", [own_b], D, sends=[b_ys], keeps=[b_yk]).go()
    gates.keeps = [od.start(ln.y, b_yk)]
    a_came = od.start(ln.core, a_send)
    a_keep = weights_half(dq_own, dkv_own)
    own_a, a_y = run(
        add_core_a, [sds(grid4(D)), sds(grid4(HALF))], at,
        a_keep.reshape((3,) + grid4(HALF)), a_came.reshape((3,) + grid4(HALF)), name="add_core_a")
    a_y = ln.y(a_y)
    od.wait(up.got)
    qkv.step()
    row3 = pl.BlockSpec((2, tile, HALF), lambda i: (0, i, 0))
    grad_text, sums1 = run(
        text_back, [sds((txt, D), F32), sds((2, D), F32)],
        at, text, gains, w_kv, dkv_own, dkv_oth,
        grid=(5,), in_specs=[row_tile, whole((1, 4 * D)), whole((D, 2 * D)), row3, row3],
        out_specs=[row_tile, whole((2, D))], name="text_back", vmem=24)
    gates.step()
    grad_visual, norms = run(
        visual_back, [page, sds((depth, 2, 16, D))],
        at, d_normed, dq_own, dq_oth, w_q, visual, d_joined, gains, sums1, sums2, sums3, name="visual_back")
    proj = Sum("proj", [own_a], D, sends=[a_y], keeps=[a_y]).go()
    norm = Sum("norm", [norms], D).go()
    first = finish([down, up, qkv])
    (layer_out,) = run(add_out, [sds((vis, D))], at, carried, y0, y1_came, name="add_out")
    gates.step()
    od.wait(proj.got, norm.got)
    proj.step()
    norm.step()
    out = lambda r, n: sds((r, n), F32)
    last_b = finish([gates])
    od.wait(proj.got, norm.got)
    proj.step()
    norm.step()
    g_out, g_gate, g_self_out = run(
        finish_b, [out(rows, D), out(2 * rows, D), out(rows, D)], at, *last_b, name="finish_b")
    last_a = finish([proj], norm)
    g_qkv, g_up, g_down = run(
        finish_cd, [out(rows, 3 * D), out(rows, 4 * D), out(4 * rows, D)], at, *first, name="finish_cd")
    g_query, g_keyval, g_gains, g_biases = run(
        finish_ab, [out(rows, D), out(rows, 2 * D), sds((size,), F32), sds((size,), F32)], at, *last_a, name="finish_a")
    return (layer_out[None], grad_visual[None], grad_text[None], g_query, g_keyval, g_out, g_gate, g_qkv, g_self_out,
            g_up, g_down, g_gains, g_biases)


def solution(mesh):
    pages = P(("rep", "fsdp"), None, None)
    flags = P(("rep", "fsdp"), None)
    matrix = P("fsdp", None)
    vector = P("fsdp")
    in_specs = (pages, pages, flags, flags) + (matrix,) * 8 + (vector, vector, pages)
    out_specs = (pages, pages, pages) + (matrix,) * 8 + (vector, vector)
    reps, shards = mesh.shape["rep"], mesh.shape["fsdp"]

    def program(*args):
        return local(reps, shards, *args)

    return jax.shard_map(program, mesh=mesh, in_specs=in_specs, out_specs=out_specs, check_vma=False)
```

```python
import functools

import jax
import jax.numpy as jnp
from jax import lax
from jax.experimental import pallas as pl
from jax.experimental.pallas import tpu as pltpu
from jax.sharding import PartitionSpec as P

H = 12
HD = 64
D = H * HD
HALF = D // 2
QUART = D // 4
BF = jnp.bfloat16
F32 = jnp.float32

epsilon = 1e-05
filtered_logits = -1000000000.0
shared_sheet_reward = 6.0
SCALE = HD ** (-0.5)
VM = pl.BlockSpec()
SM = pl.BlockSpec(memory_space=pltpu.SMEM)
ANY = pl.BlockSpec(memory_space=pl.ANY)


def sds(shape, dtype=BF):
    return jax.ShapeDtypeStruct(tuple(shape), dtype)


def size_of(a):
    n = jnp.dtype(a.dtype).itemsize
    for d in a.shape:
        n *= d
    return n


class Order:
    def __init__(self):
        self.tokens = []

    def start(self, exchange, a, *args):
        a, *self.tokens = lax.optimization_barrier((a, *self.tokens))
        return exchange(a, *args)

    def wait(self, *arrays):
        self.tokens = self.tokens + list(arrays)

    def run(self, body, outs, where, *ins, name=None, scratch=(), grid=None, in_specs=None, out_specs=None, vmem=None, prefetch=False, far=False):
        moved = sum(size_of(a) for a in ins) + sum(size_of(o) for o in outs)
        held = moved + sum(size_of(s) for s in scratch)
        limit = 66_000_000 if far else vmem << 20 if vmem else min(60 << 20, int(1.25 * held) + (10 << 20))
        ins_specs = ([VM] * len(ins) if in_specs is None else in_specs) + [ANY] * len(self.tokens)
        spec = dict(in_specs=([] if prefetch else [SM]) + ins_specs,
                    out_specs=([VM] * len(outs) if out_specs is None else out_specs) + [pl.BlockSpec((8, 128), lambda *_: (0, 0)) if grid else VM],
                    scratch_shapes=[pltpu.VMEM(s.shape, s.dtype) for s in scratch])
        if prefetch:
            spec = dict(grid_spec=pltpu.PrefetchScalarGridSpec(num_scalar_prefetch=1, grid=grid, **spec))
        elif grid is not None:
            spec["grid"] = grid
        kernel, count, late = body, len(ins), len(self.tokens)
        if far:
            spec["in_specs"] = [SM] + [pl.BlockSpec(memory_space=pltpu.HBM)] * count + [ANY] * late
            spec["scratch_shapes"] = [pltpu.VMEM(a.shape, a.dtype) for a in ins] + [pltpu.SemaphoreType.DMA((count,))]

            def kernel(at, *refs):
                held, sems = refs[-1 - count : -1], refs[-1]
                copies = [pltpu.make_async_copy(refs[i], held[i], sems.at[i]) for i in range(count)]
                for one in copies:
                    one.start()
                for one in copies:
                    one.wait()
                body(at, *held, *refs[count : -1 - count])

        ends = count + late + len(outs)

        def marked(at, *refs):
            refs[ends][...] = jnp.zeros((8, 128), F32)
            kernel(at, *refs[:count], *refs[count + late : ends], *refs[ends + 1 :])

        *got, mark = pl.pallas_call(
            marked,
            out_shape=list(outs) + [sds((8, 128), F32)],
            compiler_params=pltpu.CompilerParams(vmem_limit_bytes=limit),
            cost_estimate=pl.CostEstimate(flops=0, bytes_accessed=1024, transcendentals=0),
            name=name,
            **spec,
        )(where, *ins, *self.tokens)
        self.tokens = [mark]
        return got


T, C, X, Z = 0, 1, 2, 3


class Links:
    def __init__(self, reps, shards):
        self.reps, self.shards = reps, shards
        self.depth = shards // 2
        rank = lax.axis_index("rep")
        shard = lax.axis_index("fsdp")
        self.shard = shard
        self.at = jnp.stack([(rank // 2) % 2, rank % 2, shard % 2, shard // 2]).astype(jnp.int32)

    def core(self, a):
        return lax.ppermute(a, "rep", [(r, r ^ 1) for r in range(self.reps)])

    def y(self, a):
        return lax.ppermute(a, "rep", [(r, r ^ 2) for r in range(self.reps)])

    def rep_bit(self, a, bit):
        return lax.ppermute(a, "rep", [(r, r ^ bit) for r in range(self.reps)])

    def across(self, a):
        return lax.ppermute(a, "fsdp", [(s, s ^ 1) for s in range(self.shards)])

    def along(self, a, k):
        return lax.ppermute(a, "fsdp", [(s, s ^ (2 * k)) for s in range(self.shards)])


def mm(a, b):
    return jnp.dot(a, b, preferred_element_type=F32)


def nt(a, b):
    return lax.dot_general(a, b, (((1,), (1,)), ((), ())), preferred_element_type=F32)


def tn(a, b):
    return lax.dot_general(a, b, (((0,), (0,)), ((), ())), preferred_element_type=F32)


def stats(rows):
    mean = jnp.mean(rows, -1, keepdims=True)
    centred = rows - mean
    factor = lax.rsqrt(jnp.mean(centred * centred, -1, keepdims=True) + epsilon)
    return centred * factor, factor


def norm_back(grad, normal, factor, gain):
    scaled = grad * gain
    dx = scaled - jnp.mean(scaled, -1, keepdims=True) - normal * jnp.mean(scaled * normal, -1, keepdims=True)
    return dx * factor, jnp.sum(grad * normal, 0, keepdims=True), jnp.sum(grad, 0, keepdims=True)


def gain_of(ref, i):
    return ref[:, i * D : (i + 1) * D]


def half(i):
    return pl.ds(pl.multiple_of(i * HALF, 128), HALF)


def pair_masks(rows):
    lane = lax.broadcasted_iota(jnp.int32, (rows, 128), 1)
    return lane < HD


def two_heads(a):
    first = pair_masks(a.shape[0])
    zero = jnp.zeros_like(a)
    return jnp.concatenate([jnp.where(first, a, zero), jnp.where(first, zero, a)], 0)


def one_pair(a):
    n = a.shape[0] // 2
    return jnp.where(pair_masks(n), a[:n], a[n:])


def softmax(scores):
    peak = jnp.max(scores, -1, keepdims=True)
    expo = jnp.exp(scores - peak)
    total = jnp.sum(expo, -1, keepdims=True)
    return expo / total, peak + jnp.log(total)


def pack_a(at, query, keyval, gains, biases, part):
    rows, size = query.shape[0], gains.shape[0]
    part[:rows, :HALF] = keyval[:, pl.ds(pl.multiple_of(at[T] * D + at[C] * HALF, 128), HALF)]
    part[:rows, HALF:] = query[:, half(at[C])]
    part[rows:, :] = jnp.zeros((16, D), BF)
    g, b = gains[...].reshape(1, size), biases[...].reshape(1, size)
    g_hi, b_hi = g.astype(BF), b.astype(BF)
    g_lo, b_lo = (g - g_hi.astype(F32)).astype(BF), (b - b_hi.astype(F32)).astype(BF)
    row = lax.broadcasted_iota(jnp.int32, (16, size), 0)
    out = jnp.zeros((16, size), F32)
    for i, v in enumerate((g_hi, g_lo, b_hi, b_lo)):
        out = jnp.where(row == i, jnp.broadcast_to(v.astype(F32), (16, size)), out)
    part[rows:, HALF : HALF + size] = out.astype(BF)


def pack_rest(at, output, gate, qkv, self_out, up, down, cot, valid, part_b, part_c, part_d, page):
    rows = output.shape[0]
    n = cot.shape[0]
    page[:n] = cot[...]
    page[n:, :n] = jnp.broadcast_to(valid[...], (8, n)).astype(F32).astype(BF)
    page[n:, n:] = jnp.zeros((8, D - n), BF)
    shards = D // rows
    t0, c0 = at[T] == 0, at[C] == 0
    gate_c, out_c, self_c = gate[:, half(at[C])], output[:, half(at[C])], self_out[:, half(at[C])]
    part_b[:, :HALF] = jnp.where(t0, gate_c[:rows], gate_c[rows:])
    part_b[:, HALF:D] = jnp.where(t0, out_c, self_c)
    pieces = []
    for i in range(3):
        v = qkv[:, pl.ds(pl.multiple_of(i * D + at[T] * HALF, 128), HALF)]
        pieces.append(jnp.where(c0, v[:, :QUART], v[:, QUART:]))
    part_c[...] = jnp.concatenate(pieces, 1)
    pieces = []
    for s in range(shards):
        v = [up[:, (s * 4 + g) * rows : (s * 4 + g + 1) * rows] for g in range(4)]
        pieces.append(jnp.where(t0, jnp.where(c0, v[0], v[1]), jnp.where(c0, v[2], v[3])))
    part_d[:, :D] = jnp.concatenate(pieces, 1)
    v = [down[g * rows : (g + 1) * rows, :] for g in range(4)]
    part_d[:, D:] = jnp.where(t0, jnp.where(c0, v[0], v[1]), jnp.where(c0, v[2], v[3]))


def column(at, *refs):
    for k, piece in enumerate(refs[:-1]):
        refs[-1][at[Z] ^ k] = piece[...]


def column_a(at, *refs):
    kv, qn = refs[-2:]
    rows = kv.shape[1]
    for k, piece in enumerate(refs[:-2]):
        kv[at[Z] ^ k] = piece[:rows, :HALF]
        qn[at[Z] ^ k] = piece[:, HALF:]


def column_rest(at, *refs):
    whole, rest = refs[-2:]
    for k, piece in enumerate(refs[:-2]):
        whole[at[Z] ^ k] = piece[...]
        if k:
            rest[k - 1] = piece[...]


def join_rest(at, mine, other_own, other_rest, out):
    depth = mine.shape[0]
    for z in range(depth):
        out[z, at[X]] = mine[z]
    for k in range(depth):
        out[at[Z] ^ k, 1 - at[X]] = other_own[...] if k == 0 else other_rest[k - 1]


def join(at, mine, other, out):
    for src, side in ((mine, at[X]), (other, 1 - at[X])):
        for z in range(mine.shape[0]):
            out[z, side] = src[z]


def join_b(at, mine, other, y_mine, y_other, out):
    for i, pair in enumerate(((mine, other), (y_mine, y_other))):
        for src, side in zip(pair, (at[X], 1 - at[X])):
            for z in range(src.shape[0]):
                out[i, z, side] = src[z]


def join_a(at, kvm, kvo, kym, kyo, qm, qo, out, gains, biases):
    _three, depth, _two, rows, _n = out.shape
    size = 4 * D // (2 * depth)
    for i, pair in enumerate(((kvm, kvo), (kym, kyo), (qm, qo))):
        for src, side in zip(pair, (at[X], 1 - at[X])):
            for z in range(depth):
                out[i, z, side] = src[z, :rows]
    first = at[X] == 0
    for z in range(depth):
        a, b = qm[z, rows:, :size].astype(F32), qo[z, rows:, :size].astype(F32)
        for i, v in enumerate((jnp.where(first, a, b), jnp.where(first, b, a))):
            s = (z * 2 + i) * size
            gains[:, s : s + size] = v[0:1] + v[1:2]
            biases[:, s : s + size] = v[2:3] + v[3:4]


def place_b(at, own, came, cross_out, self_out, gate):
    t, c = at[T], at[C]
    for src, cc in ((own, c), (came, 1 - c)):
        for i in range(2):
            gate[:, t ^ i, :, half(cc)] = src[i, :, :, :HALF]
        cross_out[:, :, half(cc)] = src[t, :, :, HALF:]
        self_out[:, :, half(cc)] = src[1 - t, :, :, HALF:]


def normed_kernel(at, text, visual, gains, biases, text_normed, normed):
    normal, _f = stats(text[...].astype(F32))
    text_normed[...] = (normal * gain_of(gains, 1) + gain_of(biases, 1)).astype(BF)
    normal, _f = stats(visual[...].astype(F32))
    normed[...] = (normal * gain_of(gains, 0) + gain_of(biases, 0)).astype(BF)


def keyval_kernel(at, text_normed, normed, own, came, kv, w_kv, w_q, queries):
    t, c = at[T], at[C]

    @pl.when(pl.program_id(0) == 0)
    def _():
        for src, cc in ((own, c), (came, 1 - c)):
            for i in range(2):
                w_kv[:, pl.ds(pl.multiple_of((t ^ i) * D + cc * HALF, 128), HALF)] = src[i]
            w_q[:, half(cc)] = src[2]
        queries[...] = mm(normed[...], w_q[...]).astype(BF)

    kv[...] = mm(text_normed[...], w_kv[...]).astype(BF)


def cross_bias(owner, valid):
    n, m = valid.shape[1], owner.shape[1]
    parent = owner[...] == lax.broadcasted_iota(jnp.int32, (n, m), 0)
    ones = jnp.where(parent, 1.0, 0.0).astype(BF)
    real = jnp.broadcast_to(valid[...].astype(F32), (8, n)).astype(BF)
    present = mm(real, ones)[0:1] > 0.5
    return jnp.where(parent, shared_sheet_reward, 0.0) + jnp.where(present, 0.0, filtered_logits)


def cross_fwd(owner, valid, q, k, v, out, logs, bias):
    @pl.when(pl.program_id(0) == 0)
    def _():
        bias[...] = cross_bias(owner, valid)

    b = bias[...]
    scores = nt(two_heads(q[...]), k[...]) * SCALE + jnp.concatenate([b, b], 0)
    weight, log = softmax(scores)
    logs[0] = log
    out[...] = one_pair(mm(weight.astype(BF), v[...])).astype(BF)


def gate_kernel(at, mixed, normed, visual, gains, biases, w_out, w_gate, cross, gate, joined, second):
    rows = mm(mixed[...], w_out[...]).astype(BF)
    cross[...] = rows
    g = jax.nn.sigmoid(mm(normed[...], w_gate[:D]) + mm(rows, w_gate[D:]))
    gate[...] = g
    j = visual[...].astype(F32) + g * rows.astype(F32)
    joined[...] = j
    normal, _f = stats(j)
    second[...] = (normal * gain_of(gains, 2) + gain_of(biases, 2)).astype(BF)


def head_order(at, a):
    return jnp.where(at[C] == 0, a, jnp.concatenate([a[:, QUART:], a[:, :QUART]], 1))


def self_bias(page):
    n = page.shape[0] - 8
    return jnp.where(page[n : n + 8, :n].astype(F32)[0:1] > 0.5, 0.0, filtered_logits)


def self_fwd(at, second0, second1, valid0, valid1, w_own, w_oth, triple, att0, att1):
    n = second0.shape[0]
    rows = jnp.concatenate([second0[...], second1[...]], 0)
    own, oth = [mm(rows, w[...]).astype(BF) for w in (w_own, w_oth)]
    for i in range(3):
        triple[:, i * HALF : (i + 1) * HALF] = jnp.concatenate(
            [own[:, i * QUART : (i + 1) * QUART], oth[:, i * QUART : (i + 1) * QUART]], 1)
    for page, (valid, att) in enumerate(((valid0, att0), (valid1, att1))):
        bias = self_bias(valid)
        r = slice(page * n, (page + 1) * n)
        outs = []
        for p in range(3):
            q, k, v = [triple[r, i * HALF + p * 128 : i * HALF + (p + 1) * 128] for i in range(3)]
            weight, _l = softmax(nt(two_heads(q), k) * SCALE + bias)
            outs.append(one_pair(mm(weight.astype(BF), v)).astype(BF))
        att[...] = head_order(at, jnp.concatenate(outs, 1))


def carry_kernel(at, mine, came, joined, gains, biases, w, attended, carried, third):
    attended[:, half(at[T])] = mine[...]
    attended[:, half(1 - at[T])] = came[...]
    c = joined[...] + mm(attended[...], w[...])
    carried[...] = c
    normal, _f = stats(c)
    third[...] = (normal * gain_of(gains, 3) + gain_of(biases, 3)).astype(BF)


def ffn_kernel(last, at, third0, third1, cot0, cot1, w, *refs):
    n = third0.shape[0]
    if last:
        y0i, y1i, d0i, d1i, y0, y1, d0, d1, grad = refs
    else:
        y0, y1, d0, d1, grad = refs
    rows = jnp.concatenate([third0[...], third1[...]], 0)
    cot = jnp.concatenate([cot0[:n], cot1[:n]], 0)
    up, down = w[:, :D], w[:, D:]
    v = mm(rows, up)
    k = (2.0 / 3.141592653589793) ** 0.5
    th = jnp.tanh(k * (v + 0.044715 * (v * v * v)))
    act = (0.5 * v * (1.0 + th)).astype(BF)
    slope = 0.5 * (1.0 + th) + 0.5 * v * (1.0 - th * th) * (k * (1.0 + 3.0 * 0.044715 * (v * v)))
    y = mm(act, down)
    grad[:, D:] = tn(act, cot).astype(BF)
    dl = (nt(cot, down) * slope).astype(BF)
    d = nt(dl, up)
    grad[:, :D] = tn(rows, dl).astype(BF)
    if last:
        y0[...] = y[:n] + y0i[...]
        y1[...] = (y[n:] + y1i[...]).astype(BF)
        d0[...] = d[:n] + d0i[...]
        d1[...] = (d[n:] + d1i[...]).astype(BF)
    else:
        y0[...], y1[...], d0[...], d1[...] = y[:n], y[n:], d[:n], d[n:]


def carry_back(at, d0, came, carried, cot, attended, gains, w, d_carried, mine, send, grad, sums):
    normal, factor = stats(carried[...])
    dx, gain, bias = norm_back(d0[...] + came[...].astype(F32), normal, factor, gain_of(gains, 3))
    dc = cot[...].astype(F32) + dx
    d_carried[...] = dc
    low = dc.astype(BF)
    da = nt(low, w[...]).astype(BF)
    t0 = at[T] == 0
    mine[...] = head_order(at, jnp.where(t0, da[:, :HALF], da[:, HALF:]))
    send[...] = head_order(at, jnp.where(t0, da[:, HALF:], da[:, :HALF]))
    grad[...] = tn(attended[...], low).astype(BF)
    sums[0:1], sums[1:2] = gain, bias


def self_back(at, triple, da0, da1, valid0, valid1, second0, second1, w_own, w_oth, d0, d1, g_own, g_oth, dt):
    n = second0.shape[0]

    @pl.loop(0, 3)
    def _(p):
        lanes = [pl.ds(pl.multiple_of(i * HALF + p * 128, 128), 128) for i in range(3)]
        for page, (valid, da) in enumerate(((valid0, da0), (valid1, da1))):
            bias = self_bias(valid)
            r = slice(page * n, (page + 1) * n)
            q, k, v = [triple[r, lane] for lane in lanes]
            qq = two_heads(q)
            dd = two_heads(da[:, lanes[0]])
            weight, _l = softmax(nt(qq, k) * SCALE + bias)
            dp = nt(dd, v)
            ds = (weight * (dp - jnp.sum(weight * dp, -1, keepdims=True))).astype(BF)
            grads = (one_pair(mm(ds, k)) * SCALE, tn(ds, qq) * SCALE, tn(weight.astype(BF), dd))
            for i in range(3):
                dt[r, lanes[i]] = grads[i].astype(BF)

    own = jnp.concatenate([dt[:, i * HALF : i * HALF + QUART] for i in range(3)], 1)
    oth = jnp.concatenate([dt[:, i * HALF + QUART : (i + 1) * HALF] for i in range(3)], 1)
    rows = jnp.concatenate([second0[...], second1[...]], 0)
    g_own[...] = tn(rows, own).astype(BF).reshape(g_own.shape)
    g_oth[...] = tn(rows, oth).astype(BF).reshape(g_oth.shape)
    d = nt(own, w_own[...]) + nt(oth, w_oth[...])
    d0[...] = d[:n]
    d1[...] = d[n:].astype(BF)


def gate_back(at, d_carried, d0, came, joined, normed, cross, gate, mixed, gains, w_gate, w_out, g_self,
              d_joined, d_mixed, d_normed, keep, send, sums):
    t, c = at[T], at[C]
    rows = keep.shape[2]
    normal, factor = stats(joined[...])
    dx, gain, bias = norm_back(d0[...] + came[...].astype(F32), normal, factor, gain_of(gains, 2))
    dj = d_carried[...] + dx
    d_joined[...] = dj
    sums[0:1], sums[1:2] = gain, bias
    g = gate[...]
    dg = (dj * cross[...].astype(F32) * g * (1.0 - g)).astype(BF)
    d_normed[...] = nt(dg, w_gate[:D])
    dc = (dj * g + nt(dg, w_gate[D:])).astype(BF)
    d_mixed[...] = nt(dc, w_out[...]).astype(BF)
    g_gate = jnp.concatenate([tn(normed[...], dg).astype(BF), tn(cross[...], dg).astype(BF)], 0)
    g_gate = g_gate.reshape(D // rows, 2, rows, D)
    g_out = tn(mixed[...], dc).astype(BF).reshape(D // rows, rows, D)
    g_so = g_self[...].reshape(D // rows, rows, D)
    for tt in range(2):
        for cc in range(2):
            lanes = slice(cc * HALF, (cc + 1) * HALF)
            side = g_out if tt == 0 else g_so
            for out, same in ((keep, True), (send, False)):
                @pl.when((c == cc) == same)
                def _():
                    out[t ^ tt, :, :, :HALF] = g_gate[:, tt, :, lanes]
                    out[t ^ tt, :, :, HALF:] = side[:, :, lanes]


def cross_back(owner, valid, q, k, v, dm, logs, dq, dkv, bias):
    @pl.when(pl.program_id(0) == 0)
    def _():
        bias[...] = cross_bias(owner, valid)

    b = bias[...]
    qq, dd = two_heads(q[...]), two_heads(dm[...])
    scores = nt(qq, k[...]) * SCALE + jnp.concatenate([b, b], 0)
    weight = jnp.exp(scores - logs[0])
    dp = nt(dd, v[...])
    ds = (weight * (dp - jnp.sum(weight * dp, -1, keepdims=True))).astype(BF)
    dq[...] = (one_pair(mm(ds, k[...])) * SCALE).astype(BF)
    dkv[0] = (tn(ds, qq) * SCALE).astype(BF)
    dkv[1] = tn(weight.astype(BF), dd).astype(BF)


def cross_weights(at, text_normed, normed, dq, dkv, grad):
    t = at[T]
    x = text_normed[...]
    grad[t] = tn(x, dkv[0]).astype(BF)
    grad[1 - t] = tn(x, dkv[1]).astype(BF)
    grad[2] = tn(normed[...], dq[...]).astype(BF)


def text_back(at, text, gains, w_kv, own, oth, grad, sums):
    c = at[C]
    d = nt(own[0], w_kv[:, half(c)])
    d = d + nt(oth[0], w_kv[:, half(1 - c)])
    d = d + nt(own[1], w_kv[:, pl.ds(pl.multiple_of(D + c * HALF, 128), HALF)])
    d = d + nt(oth[1], w_kv[:, pl.ds(pl.multiple_of(D + (1 - c) * HALF, 128), HALF)])
    normal, factor = stats(text[...].astype(F32))
    dx, gain, bias = norm_back(d, normal, factor, gain_of(gains, 1))
    grad[...] = dx

    @pl.when(pl.program_id(0) == 0)
    def _():
        sums[...] = jnp.zeros_like(sums)

    sums[0:1] += gain
    sums[1:2] += bias


def visual_back(at, d_normed, dq_own, dq_oth, w_q, visual, d_joined, gains, s1, s2, s3, grad, norms):
    c = at[C]
    depth = norms.shape[0]
    size = 4 * D // (2 * depth)
    d = d_normed[...] + nt(dq_own[...], w_q[:, half(c)]) + nt(dq_oth[...], w_q[:, half(1 - c)])
    normal, factor = stats(visual[...].astype(F32))
    dx, gain, bias = norm_back(d, normal, factor, gain_of(gains, 0))
    grad[...] = d_joined[...] + dx
    g = jnp.concatenate([gain, s1[0:1], s2[0:1], s3[0:1]], 1)
    b = jnp.concatenate([bias, s1[1:2], s2[1:2], s3[1:2]], 1)
    row = lax.broadcasted_iota(jnp.int32, (8, size), 0)
    norms[...] = jnp.zeros_like(norms)
    for s in range(2 * depth):
        lanes = slice(s * size, (s + 1) * size)
        v = jnp.where(row == 0, jnp.broadcast_to(g[:, lanes], (8, size)), jnp.broadcast_to(b[:, lanes], (8, size)))
        norms[s // 2, s % 2, :, :size] = jnp.where(row < 2, v, 0.0).astype(BF)


def finish_ab(at, r, ry, rc, ryc, g_query, g_keyval, gains, biases):
    t, c = at[T], at[C]
    rows, size = g_query.shape[0], gains.shape[0]
    for a, b, cc in ((r, ry, c), (rc, ryc, 1 - c)):
        g_keyval[:, pl.ds(pl.multiple_of(t * D + cc * HALF, 128), HALF)] = a[:rows, :HALF].astype(F32)
        g_keyval[:, pl.ds(pl.multiple_of((1 - t) * D + cc * HALF, 128), HALF)] = b[:rows, :HALF].astype(F32)
        g_query[:, half(cc)] = a[:rows, HALF:].astype(F32) + b[:rows, HALF:].astype(F32)
    norms = [a[rows:, :size].astype(F32) for a in (r, ry, rc, ryc)]
    norms = norms[0] + norms[1] + norms[2] + norms[3]
    gains[...] = norms[0:1].reshape(size)
    biases[...] = norms[1:2].reshape(size)


def in_order(at, groups, lanes):
    c0, t0 = at[C] == 0, at[T] == 0
    own, y, core, both = [r[:, lanes].astype(F32) for r in groups]
    a0, a1 = jnp.where(c0, own, core), jnp.where(c0, core, own)
    b0, b1 = jnp.where(c0, y, both), jnp.where(c0, both, y)
    return jnp.where(t0, a0, b0), jnp.where(t0, a1, b1), jnp.where(t0, b0, a0), jnp.where(t0, b1, a1)


def finish_cd(at, r, ry, rc, ryc, g_qkv, g_up, g_down):
    groups = (r, ry, rc, ryc)
    rows = g_qkv.shape[0]
    p = in_order(at, groups, slice(0, D))
    for i in range(4):
        g_down[i * rows : (i + 1) * rows] = p[i]
    for s in range(D // rows):
        p = in_order(at, groups, slice(D + s * rows, D + (s + 1) * rows))
        g_up[:, s * 4 * rows : (s + 1) * 4 * rows] = jnp.concatenate(p, 1)
    for i in range(3):
        p = in_order(at, groups, slice(2 * D + i * QUART, 2 * D + (i + 1) * QUART))
        g_qkv[:, i * D : (i + 1) * D] = jnp.concatenate(p, 1)


def finish_b(at, r, ry, rc, ryc, g_out, g_gate, g_self):
    groups = (r, ry, rc, ryc)
    rows = g_out.shape[0]
    p = in_order(at, groups, slice(0, HALF))
    for i in range(4):
        g_gate[(i // 2) * rows : (i // 2 + 1) * rows, (i % 2) * HALF : (i % 2 + 1) * HALF] = p[i]
    p = in_order(at, groups, slice(HALF, D))
    g_out[...] = jnp.concatenate(p[:2], 1)
    g_self[...] = jnp.concatenate(p[2:], 1)


def reduce_x(count, extra, lanes, at, *refs):
    out = refs[-1]
    m = extra[0] if extra else 0
    for z in range(out.shape[0]):
        out[z] = reduced(refs, count, m, lanes, z, 1 - at[X]).astype(BF)


def reduced(refs, count, m, lanes, z, side):
    acc = refs[0][z, side, :, lanes].astype(F32)
    for r in refs[1:count]:
        acc = acc + r[z, side, :, lanes].astype(F32)
    if m:
        y = refs[count]
        y = (y[z, side] if len(y.shape) == 4 else y[z]).astype(F32)
        acc = acc + y if y.shape == acc.shape else jnp.concatenate([acc[:, :m] + y, acc[:, m:]], 1)
    return acc


def reduce_z(count, extra, lanes, at, *refs):
    got, keep, send = refs[-3:]
    m = extra[0] if extra else 0
    for i in range(keep.shape[0]):
        for k, out in ((2 * i, keep), (2 * i + 1, send)):
            z = at[Z] ^ k
            out[i] = (reduced(refs, count, m, lanes, z, at[X]) + got[z].astype(F32)).astype(BF)


def reduce_x_proj(at, own, oth, norms, out):
    rows = own.shape[2]
    for z in range(out.shape[0]):
        out[z, :rows] = reduced((own, oth), 1, oth.shape[-1], slice(None), z, 1 - at[X]).astype(BF)
        out[z, rows:] = norms[z, 1 - at[X]]


def reduce_z_proj(at, own, oth, norms, got, keep, send):
    rows = own.shape[2]
    for i in range(keep.shape[0]):
        for k, out in ((2 * i, keep), (2 * i + 1, send)):
            z = at[Z] ^ k
            b = got[z].astype(F32)
            out[i, :rows] = (reduced((own, oth), 1, oth.shape[-1], slice(None), z, at[X]) + b[:rows]).astype(BF)
            out[i, rows:] = (norms[z, at[X]].astype(F32) + b[rows:]).astype(BF)


def reduce_more(at, keep, got, *outs):
    for i in range(keep.shape[0]):
        v = (keep[i].astype(F32) + got[i].astype(F32)).astype(BF)
        if len(outs) == 1:
            outs[0][...] = v
        else:
            outs[i % 2][i // 2] = v


def reduce_last(count, at, *refs):
    out = refs[-1]
    at_lane = 0
    for keep, got in zip(refs[0 : 2 * count : 2], refs[1 : 2 * count : 2]):
        rows, n = keep.shape[1:]
        out[:rows, at_lane : at_lane + n] = (keep[0].astype(F32) + got[0].astype(F32)).astype(BF)
        at_lane += n


def add_core_b(at, keep, came, own, oth_send, oth_keep):
    x = at[X]
    for z in range(own.shape[0]):
        for i in range(2):
            own[z, i] = (keep[0, z, i].astype(F32) + came[0, z, i].astype(F32)).astype(BF)
        oth_send[z] = (keep[1, z, 1 - x].astype(F32) + came[1, z, 1 - x].astype(F32)).astype(BF)
        oth_keep[z] = (keep[1, z, x].astype(F32) + came[1, z, x].astype(F32)).astype(BF)


def add_core_a(at, keep, came, own, oth, q):
    for out, i in ((own, 0), (oth, 1), (q, 2)):
        out[...] = (keep[i].astype(F32) + came[i].astype(F32)).astype(BF)


def add_out(at, carried, y0, came, out):
    out[...] = (carried[...] + y0[...] + came[...].astype(F32)).astype(BF)


def local(reps, shards, visual, text, visual_valid, block_owner, cross_query, cross_keyval, cross_output, gate_weight,
          self_qkv, self_output, ffn_up, ffn_down, norm_gains, norm_biases, cotangent):
    ln = Links(reps, shards)
    at = ln.at
    od = Order()
    run = od.run
    visual, text, cotangent = visual[0], text[0], cotangent[0]
    rows, size = cross_query.shape[0], norm_gains.shape[0]
    vis, txt = visual.shape[0], text.shape[0]
    depth = shards // 2
    w3 = 3 * QUART
    whole = lambda shape: pl.BlockSpec(shape, lambda *_: (0,) * len(shape))
    page = sds((vis, D), F32)
    grid4 = lambda n: (depth, 2, rows, n)

    def far_first(part):
        pieces = {0: part}
        for k in range(depth - 1, 0, -1):
            if k & (k - 1) == 0:
                pieces[k] = od.start(ln.along, part, k)
        return pieces

    def passed_on(pieces):
        for k in sorted(range(1, depth), key=lambda k: (bin(k).count("1"), -k)):
            if k not in pieces:
                od.wait(*[pieces[i] for i in sorted(pieces) if i])
                pieces[k] = od.start(ln.along, pieces[k & (k - 1)], k & -k)
        return [pieces[k] for k in range(depth)]

    (part_a,) = run(pack_a, [sds((rows + 16, D))], at, cross_query, cross_keyval, norm_gains, norm_biases, name="pack_a", far=True)
    pieces_a = far_first(part_a)
    part_b, part_c, part_d, cot = run(
        pack_rest, [sds((rows, D)), sds((rows, w3)), sds((rows, 2 * D)), sds((vis + 8, D))], at,
        cross_output, gate_weight, self_qkv, self_output, ffn_up, ffn_down, cotangent, visual_valid,
        name="pack_rest", far=True)
    d_xo, cot_y = ln.across(part_d), ln.y(cot)
    pieces_a = passed_on(pieces_a)
    od.wait(d_xo, cot_y)
    kv_m, qn_m = run(column_a, [sds((depth, rows, HALF)), sds((depth, rows + 16, HALF))], at, *pieces_a, name="column_a")
    kv_o, qn_o, kv_ym = ln.across(kv_m), ln.across(qn_m), ln.y(kv_m)
    pieces_b = passed_on(far_first(part_b))
    od.wait(kv_o)
    kv_yo = ln.y(kv_o)
    pieces_c = far_first(part_c)
    (b_m,) = run(column, [sds((depth, rows, D))], at, *pieces_b, name="column_b")
    joined_a, gains, biases = run(
        join_a, [sds((3,) + grid4(HALF)), sds((1, 4 * D), F32), sds((1, 4 * D), F32)],
        at, kv_m, kv_o, kv_ym, kv_yo, qn_m, qn_o, name="join_a")
    joined_a = joined_a.reshape(3, D, HALF)
    came_a = ln.core(joined_a)
    b_o, b_ym = od.start(ln.across, b_m), od.start(ln.y, b_m)
    tile = txt // 5
    row_tile = pl.BlockSpec((tile, D), lambda i: (i, 0))
    text_normed, normed = run(
        normed_kernel, [sds((txt, D)), sds((vis, D))], at, text, visual, gains, biases,
        grid=(5,), in_specs=[row_tile, whole((vis, D)), whole((1, 4 * D)), whole((1, 4 * D))],
        out_specs=[row_tile, whole((vis, D))], name="normed", vmem=12)
    pieces_c = passed_on(pieces_c)
    od.wait(came_a)
    pieces_d = far_first(part_d)

    kv, w_kv, w_q, queries = run(
        keyval_kernel, [sds((txt, 2 * D)), sds((D, 2 * D)), sds((D, D)), sds((vis, D))],
        at, text_normed, normed, joined_a, came_a,
        grid=(5,), in_specs=[row_tile, whole((vis, D)), whole((3, D, HALF)), whole((3, D, HALF))],
        out_specs=[pl.BlockSpec((tile, 2 * D), lambda i: (i, 0)), whole((D, 2 * D)), whole((D, D)), whole((vis, D))],
        name="keyval", vmem=30)
    (c_m,) = run(column, [sds((depth, rows, w3))], at, *pieces_c, name="column_c")
    od.wait(b_o, b_ym)
    c_o, b_yo = od.start(ln.across, c_m), od.start(ln.y, b_o)
    pairs = H // 2
    col = lambda n, off=0: pl.BlockSpec((n, 128), lambda p: (0, p + off))
    mixed, logs = run(
        lambda at, *refs: cross_fwd(*refs), [sds((vis, D)), sds((pairs, 2 * vis, 1), F32)],
        at, block_owner, visual_valid, queries, kv, kv,
        grid=(pairs,), in_specs=[whole((1, txt)), whole((1, vis)), col(vis), col(txt), col(txt, pairs)],
        out_specs=[col(vis), pl.BlockSpec((1, 2 * vis, 1), lambda p: (p, 0, 0))],
        scratch=[sds((vis, txt), F32)], name="cross_fwd", vmem=16)
    pieces_d = passed_on(pieces_d)
    (wc_own,) = run(join, [sds(grid4(w3))], at, c_m, c_o, name="join_c")
    wc_oth = ln.core(wc_own)
    (joined_b,) = run(join_b, [sds((2,) + grid4(D))], at, b_m, b_o, b_ym, b_yo, name="join_b")
    joined_b = joined_b.reshape(2, shards, rows, D)
    came_b = ln.core(joined_b)
    w_out, w_self, w_gate = run(
        place_b, [sds((shards, rows, D)), sds((shards, rows, D)), sds((shards, 2, rows, D))], at, joined_b, came_b, name="place_b")
    w_out, w_self, w_gate = w_out.reshape(D, D), w_self.reshape(D, D), w_gate.reshape(2 * D, D)
    od.wait(wc_oth)
    wc_own, wc_oth = wc_own.reshape(D, w3), wc_oth.reshape(D, w3)
    cross, gate, joined, second = run(
        gate_kernel, [sds((vis, D)), page, page, sds((vis, D))],
        at, mixed, normed, visual, gains, biases, w_out, w_gate, name="gate")
    second_y = ln.y(second)
    d_m, d_rest = run(column_rest, [sds((depth, rows, 2 * D)), sds((depth - 1, rows, 2 * D))], at, *pieces_d, name="column_d")
    d_xr, d_cm, d_cxo = ln.across(d_rest), ln.core(d_m), od.start(ln.core, d_xo)
    triple, att_mine, att_send = run(
        self_fwd, [sds((2 * vis, 3 * HALF)), sds((vis, HALF)), sds((vis, HALF))],
        at, second, second_y, cot, cot_y, wc_own, wc_oth, name="self_fwd")
    att_came = ln.y(att_send)
    od.wait(d_cm, d_cxo)
    attended, carried, third = run(
        carry_kernel, [sds((vis, D)), page, sds((vis, D))],
        at, att_mine, att_came, joined, gains, biases, w_self, name="carry")
    third_y = ln.y(third)
    od.wait(third_y)
    d_cxr = od.start(ln.core, d_xr)
    (wd_own,) = run(join_rest, [sds(grid4(2 * D))], at, d_m, d_xo, d_xr, name="join_d")
    (wd_oth,) = run(join_rest, [sds(grid4(2 * D))], at, d_cm, d_cxo, d_cxr, name="join_d")
    wd_own, wd_oth = wd_own.reshape(D, 2 * D), wd_oth.reshape(D, 2 * D)

    y0, y1, d0, d1, gd_oth = run(
        functools.partial(ffn_kernel, False), [page] * 4 + [sds((D, 2 * D))],
        at, third, third_y, cot, cot_y, wd_oth, name="ffn_first")
    gd_came = ln.core(gd_oth).reshape(grid4(2 * D))
    y0, y1, d0, d1, gd_own = run(
        functools.partial(ffn_kernel, True), [page, sds((vis, D))] * 2 + [sds((D, 2 * D))],
        at, third, third_y, cot, cot_y, wd_own, y0, y1, d0, d1, name="ffn_second")
    gd_own = gd_own.reshape(grid4(2 * D))
    d1_came = ln.y(d1)

    class Sum:
        def __init__(self, name, arrays, n, lanes=slice(None), sends=(), keeps=(), norms=None):
            self.name, self.n, self.rows = name, n, arrays[0].shape[2]
            extra = [a.shape[-1] for a in keeps]
            first, self.second = [functools.partial(f, len(arrays), extra, lanes) for f in (reduce_x, reduce_z)]
            self.late = list(arrays) + list(keeps)
            early = list(arrays) + list(sends)
            if norms is not None:
                first, self.second, self.rows = reduce_x_proj, reduce_z_proj, self.rows + norms.shape[2]
                self.late, early = self.late + [norms], early + [norms]
            (self.send,) = run(first, [sds((depth, self.rows, n))], at, *early, name="reduce_x_" + name)
            self.bit = 0

        def go(self):
            self.got = od.start(ln.across, self.send)
            return self

        def step(self):
            if self.bit == 0:
                outs = [sds((depth // 2, self.rows, self.n))] * 2
                self.keep, send = run(self.second, outs, at, *self.late, self.got, name="reduce_z_" + self.name)
                self.bit = 1
            elif self.keep.shape[0] > 1:
                outs = [sds((self.keep.shape[0] // 2, self.rows, self.n))] * 2
                self.keep, send = run(reduce_more, outs, at, self.keep, self.got, name="reduce_m_" + self.name)
                self.bit *= 2
            else:
                return False
            self.got = ln.along(send, self.bit)
            return True

    def finish(*sums):
        ins = [a for one in sums for a in (one.keep, one.got)]
        (total,) = run(functools.partial(reduce_last, len(sums)), [sds((sums[0].rows, sum(one.n for one in sums)))], at,
                       *ins, name="reduce_last")
        for bit in range(2, reps.bit_length() - 1):
            total = (total.astype(F32) + ln.rep_bit(total, 1 << bit).astype(F32)).astype(BF)
        ry = ln.y(total)
        return total, ry, ln.core(total), ln.core(ry)

    def back_half(index):
        def spec(n, off=0):
            return pl.BlockSpec((n, 128), lambda p, at: (0, (at[C] ^ index) * 3 + p + off))

        return run(
            lambda at, *refs: cross_back(*refs), [sds((vis, HALF)), sds((2, txt, HALF))],
            at, block_owner, visual_valid, queries, kv, kv, d_mixed, logs, prefetch=True, grid=(3,),
            in_specs=[whole((1, txt)), whole((1, vis)), spec(vis), spec(txt), spec(txt, pairs), spec(vis),
                      pl.BlockSpec((1, 2 * vis, 1), lambda p, at: ((at[C] ^ index) * 3 + p, 0, 0))],
            out_specs=[pl.BlockSpec((vis, 128), lambda p, at: (0, p)), pl.BlockSpec((2, txt, 128), lambda p, at: (0, 0, p))],
            scratch=[sds((vis, txt), F32)], name="cross_back", vmem=20)

    def weights_half(dq, dkv):
        return run(cross_weights, [sds((3, D, HALF))], at, text_normed, normed, dq, dkv, name="cross_weights")[0]

    down = Sum("down", [gd_own, gd_came], D, slice(D, 2 * D)).go()
    d_carried, da_mine, da_send, g_self, sums3 = run(
        carry_back, [page, sds((vis, HALF)), sds((vis, HALF)), sds((D, D)), sds((2, D), F32)],
        at, d0, d1_came, carried, cotangent, attended, gains, w_self, name="carry_back")
    da_came = ln.y(da_send)
    up = Sum("up", [gd_own, gd_came], D, slice(0, D))
    od.wait(da_came)
    down.step()
    up.go()
    ds0, ds1, gc_own, gc_oth = run(
        self_back, [page, sds((vis, D)), sds(grid4(w3)), sds(grid4(w3))],
        at, triple, da_mine, da_came, cot, cot_y, second, second_y, wc_own, wc_oth,
        scratch=[sds((2 * vis, 3 * HALF))], name="self_back")
    ds1_came = ln.y(ds1)
    gc_came = ln.core(gc_oth)
    down.step()
    up.step()
    d_joined, d_mixed, d_normed, b_keep, b_send, sums2 = run(
        gate_back, [page, sds((vis, D)), page, sds((2, shards, rows, D)), sds((2, shards, rows, D)), sds((2, D), F32)],
        at, d_carried, ds0, ds1_came, joined, normed, cross, gate, mixed, gains, w_gate, w_out, g_self, name="gate_back")
    b_came = ln.core(b_send)
    y1_came = od.start(ln.y, y1)
    dq_oth, dkv_oth = back_half(1)
    qkv = Sum("qkv", [gc_own, gc_came], w3).go()
    od.wait(y1_came)
    own_b, b_ys, b_yk = run(
        add_core_b, [sds(grid4(D)), sds((depth, rows, D)), sds((depth, rows, D))], at,
        b_keep.reshape((2,) + grid4(D)), b_came.reshape((2,) + grid4(D)), name="add_core_b")
    b_ys = ln.y(b_ys)
    a_came = ln.core(weights_half(dq_oth, dkv_oth))
    dq_own, dkv_own = back_half(0)
    up.step()
    gates = Sum("gate", [own_b], D, sends=[b_ys], keeps=[b_yk]).go()
    qkv.step()
    a_keep = weights_half(dq_own, dkv_own)
    od.wait(down.got)
    own_a, a_y, own_q = run(
        add_core_a, [sds(grid4(HALF))] * 3, at,
        a_keep.reshape((3,) + grid4(HALF)), a_came.reshape((3,) + grid4(HALF)), name="add_core_a")
    a_y = ln.y(a_y)
    query = Sum("query", [own_q], HALF).go()
    row3 = pl.BlockSpec((2, tile, HALF), lambda i: (0, i, 0))
    grad_text, sums1 = run(
        text_back, [sds((txt, D), F32), sds((2, D), F32)],
        at, text, gains, w_kv, dkv_own, dkv_oth,
        grid=(5,), in_specs=[row_tile, whole((1, 4 * D)), whole((D, 2 * D)), row3, row3],
        out_specs=[row_tile, whole((2, D))], name="text_back", vmem=24)
    od.wait(up.got, gates.got)
    qkv.step()
    query.step()
    grad_visual, norms = run(
        visual_back, [page, sds((depth, 2, 8, HALF))],
        at, d_normed, dq_own, dq_oth, w_q, visual, d_joined, gains, sums1, sums2, sums3, name="visual_back")
    keyval = Sum("keyval", [own_a], HALF, sends=[a_y], keeps=[a_y], norms=norms).go()
    gates.late[1] = od.start(ln.y, b_yk)
    (layer_out,) = run(add_out, [sds((vis, D))], at, carried, y0, y1_came, name="add_out")
    query.step()
    keyval.step()
    first = finish(down, up, qkv)
    od.wait(query.got)
    keyval.step()
    gates.step()
    out = lambda r, n: sds((r, n), F32)
    last_a = finish(keyval, query)
    gates.step()
    g_qkv, g_up, g_down = run(
        finish_cd, [out(rows, 3 * D), out(rows, 4 * D), out(4 * rows, D)], at, *first, name="finish_cd")
    last_b = finish(gates)
    g_query, g_keyval, g_gains, g_biases = run(
        finish_ab, [out(rows, D), out(rows, 2 * D), sds((size,), F32), sds((size,), F32)], at, *last_a, name="finish_a")
    g_out, g_gate, g_self_out = run(
        finish_b, [out(rows, D), out(2 * rows, D), out(rows, D)], at, *last_b, name="finish_b")
    return (layer_out[None], grad_visual[None], grad_text[None], g_query, g_keyval, g_out, g_gate, g_qkv, g_self_out,
            g_up, g_down, g_gains, g_biases)


def solution(mesh):
    pages = P(("rep", "fsdp"), None, None)
    flags = P(("rep", "fsdp"), None)
    matrix = P("fsdp", None)
    vector = P("fsdp")
    in_specs = (pages, pages, flags, flags) + (matrix,) * 8 + (vector, vector, pages)
    out_specs = (pages, pages, pages) + (matrix,) * 8 + (vector, vector)
    reps, shards = mesh.shape["rep"], mesh.shape["fsdp"]

    def program(*args):
        return local(reps, shards, *args)

    return jax.shard_map(program, mesh=mesh, in_specs=in_specs, out_specs=out_specs, check_vma=False)
```

```python
import functools

import jax
import jax.numpy as jnp
from jax import lax
from jax.experimental import pallas as pl
from jax.experimental.pallas import tpu as pltpu
from jax.sharding import PartitionSpec as P

H = 12
HD = 64
D = H * HD
HALF = D // 2
QUART = D // 4
WIDE = -(-3 * QUART // 128) * 128
BF = jnp.bfloat16
F32 = jnp.float32

epsilon = 1e-05
filtered_logits = -1000000000.0
shared_sheet_reward = 6.0
SCALE = HD ** (-0.5)
VM = pl.BlockSpec()
SM = pl.BlockSpec(memory_space=pltpu.SMEM)
ANY = pl.BlockSpec(memory_space=pl.ANY)


def sds(shape, dtype=BF):
    return jax.ShapeDtypeStruct(tuple(shape), dtype)


def size_of(a):
    n = jnp.dtype(a.dtype).itemsize
    for d in a.shape:
        n *= d
    return n


class Order:
    def __init__(self):
        self.tokens = []

    def start(self, exchange, a, *args):
        a, *self.tokens = lax.optimization_barrier((a, *self.tokens))
        return exchange(a, *args)

    def wait(self, *arrays):
        self.tokens = self.tokens + list(arrays)

    def run(self, body, outs, where, *ins, name=None, scratch=(), grid=None, in_specs=None, out_specs=None, vmem=None, prefetch=False, far=False):
        moved = sum(size_of(a) for a in ins) + sum(size_of(o) for o in outs)
        held = moved + sum(size_of(s) for s in scratch)
        limit = 66_000_000 if far else vmem << 20 if vmem else min(60 << 20, int(1.25 * held) + (10 << 20))
        ins_specs = ([VM] * len(ins) if in_specs is None else in_specs) + [ANY] * len(self.tokens)
        spec = dict(in_specs=([] if prefetch else [SM]) + ins_specs,
                    out_specs=([VM] * len(outs) if out_specs is None else out_specs) + [pl.BlockSpec((8, 128), lambda *_: (0, 0)) if grid else VM],
                    scratch_shapes=[pltpu.VMEM(s.shape, s.dtype) for s in scratch])
        if prefetch:
            spec = dict(grid_spec=pltpu.PrefetchScalarGridSpec(num_scalar_prefetch=1, grid=grid, **spec))
        elif grid is not None:
            spec["grid"] = grid
        kernel, count, late = body, len(ins), len(self.tokens)
        if far:
            spec["in_specs"] = [SM] + [pl.BlockSpec(memory_space=pltpu.HBM)] * count + [ANY] * late
            spec["scratch_shapes"] = [pltpu.VMEM(a.shape, a.dtype) for a in ins] + [pltpu.SemaphoreType.DMA((count,))]

            def kernel(at, *refs):
                held, sems = refs[-1 - count : -1], refs[-1]
                copies = [pltpu.make_async_copy(refs[i], held[i], sems.at[i]) for i in range(count)]
                for one in copies:
                    one.start()
                for one in copies:
                    one.wait()
                body(at, *held, *refs[count : -1 - count])

        ends = count + late + len(outs)

        def marked(at, *refs):
            refs[ends][...] = jnp.zeros((8, 128), F32)
            kernel(at, *refs[:count], *refs[count + late : ends], *refs[ends + 1 :])

        *got, mark = pl.pallas_call(
            marked,
            out_shape=list(outs) + [sds((8, 128), F32)],
            compiler_params=pltpu.CompilerParams(vmem_limit_bytes=limit),
            cost_estimate=pl.CostEstimate(flops=0, bytes_accessed=1024, transcendentals=0),
            name=name,
            **spec,
        )(where, *ins, *self.tokens)
        self.tokens = [mark]
        return got


T, C, X, Z = 0, 1, 2, 3


class Links:
    def __init__(self, reps, shards):
        self.reps, self.shards = reps, shards
        self.depth = shards // 2
        rank = lax.axis_index("rep")
        shard = lax.axis_index("fsdp")
        self.shard = shard
        self.at = jnp.stack([(rank // 2) % 2, rank % 2, shard % 2, shard // 2]).astype(jnp.int32)

    def core(self, a):
        return lax.ppermute(a, "rep", [(r, r ^ 1) for r in range(self.reps)])

    def y(self, a):
        return lax.ppermute(a, "rep", [(r, r ^ 2) for r in range(self.reps)])

    def rep_bit(self, a, bit):
        return lax.ppermute(a, "rep", [(r, r ^ bit) for r in range(self.reps)])

    def across(self, a):
        return lax.ppermute(a, "fsdp", [(s, s ^ 1) for s in range(self.shards)])

    def along(self, a, k):
        return lax.ppermute(a, "fsdp", [(s, s ^ (2 * k)) for s in range(self.shards)])


def mm(a, b):
    return jnp.dot(a, b, preferred_element_type=F32)


def nt(a, b):
    return lax.dot_general(a, b, (((1,), (1,)), ((), ())), preferred_element_type=F32)


def tn(a, b):
    return lax.dot_general(a, b, (((0,), (0,)), ((), ())), preferred_element_type=F32)


def stats(rows):
    mean = jnp.mean(rows, -1, keepdims=True)
    centred = rows - mean
    factor = lax.rsqrt(jnp.mean(centred * centred, -1, keepdims=True) + epsilon)
    return centred * factor, factor


def norm_back(grad, normal, factor, gain):
    scaled = grad * gain
    dx = scaled - jnp.mean(scaled, -1, keepdims=True) - normal * jnp.mean(scaled * normal, -1, keepdims=True)
    return dx * factor, jnp.sum(grad * normal, 0, keepdims=True), jnp.sum(grad, 0, keepdims=True)


def gain_of(ref, i):
    return ref[:, i * D : (i + 1) * D]


def half(i):
    return pl.ds(pl.multiple_of(i * HALF, 128), HALF)


def pair_masks(rows):
    lane = lax.broadcasted_iota(jnp.int32, (rows, 128), 1)
    return lane < HD


def two_heads(a):
    first = pair_masks(a.shape[0])
    zero = jnp.zeros_like(a)
    return jnp.concatenate([jnp.where(first, a, zero), jnp.where(first, zero, a)], 0)


def one_pair(a):
    n = a.shape[0] // 2
    return jnp.where(pair_masks(n), a[:n], a[n:])


def softmax(scores):
    peak = jnp.max(scores, -1, keepdims=True)
    expo = jnp.exp(scores - peak)
    total = jnp.sum(expo, -1, keepdims=True)
    return expo / total, peak + jnp.log(total)


def pack_a(at, query, keyval, gains, biases, part):
    rows, size = query.shape[0], gains.shape[0]
    part[:rows, :HALF] = keyval[:, pl.ds(pl.multiple_of(at[T] * D + at[C] * HALF, 128), HALF)]
    part[:rows, HALF:] = query[:, half(at[C])]
    part[rows:, :] = jnp.zeros((16, D), BF)
    g, b = gains[...].reshape(1, size), biases[...].reshape(1, size)
    g_hi, b_hi = g.astype(BF), b.astype(BF)
    g_lo, b_lo = (g - g_hi.astype(F32)).astype(BF), (b - b_hi.astype(F32)).astype(BF)
    row = lax.broadcasted_iota(jnp.int32, (16, size), 0)
    out = jnp.zeros((16, size), F32)
    for i, v in enumerate((g_hi, g_lo, b_hi, b_lo)):
        out = jnp.where(row == i, jnp.broadcast_to(v.astype(F32), (16, size)), out)
    part[rows:, HALF : HALF + size] = out.astype(BF)


def pack_rest(at, output, gate, qkv, self_out, up, down, cot, valid, part_b, part_c, part_d, page):
    rows = output.shape[0]
    n = cot.shape[0]
    page[:n] = cot[...]
    page[n:, :n] = jnp.broadcast_to(valid[...], (8, n)).astype(F32).astype(BF)
    page[n:, n:] = jnp.zeros((8, D - n), BF)
    shards = D // rows
    t0, c0 = at[T] == 0, at[C] == 0
    gate_c, out_c, self_c = gate[:, half(at[C])], output[:, half(at[C])], self_out[:, half(at[C])]
    part_b[:, :HALF] = jnp.where(t0, gate_c[:rows], gate_c[rows:])
    part_b[:, HALF:D] = jnp.where(t0, out_c, self_c)
    pieces = []
    for i in range(3):
        v = qkv[:, pl.ds(pl.multiple_of(i * D + at[T] * HALF, 128), HALF)]
        pieces.append(jnp.where(c0, v[:, :QUART], v[:, QUART:]))
    part_c[...] = jnp.concatenate(pieces + [jnp.zeros((rows, WIDE - 3 * QUART), BF)], 1)
    pieces = []
    for s in range(shards):
        v = [up[:, (s * 4 + g) * rows : (s * 4 + g + 1) * rows] for g in range(4)]
        pieces.append(jnp.where(t0, jnp.where(c0, v[0], v[1]), jnp.where(c0, v[2], v[3])))
    part_d[:, :D] = jnp.concatenate(pieces, 1)
    v = [down[g * rows : (g + 1) * rows, :] for g in range(4)]
    part_d[:, D:] = jnp.where(t0, jnp.where(c0, v[0], v[1]), jnp.where(c0, v[2], v[3]))


def column(at, *refs):
    for k, piece in enumerate(refs[:-1]):
        refs[-1][at[Z] ^ k] = piece[...]


def column_a(at, *refs):
    kv, qn = refs[-2:]
    rows = kv.shape[1]
    for k, piece in enumerate(refs[:-2]):
        kv[at[Z] ^ k] = piece[:rows, :HALF]
        qn[at[Z] ^ k] = piece[:, HALF:]


def column_rest(at, *refs):
    whole, rest = refs[-2:]
    for k, piece in enumerate(refs[:-2]):
        whole[at[Z] ^ k] = piece[...]
        if k:
            rest[k - 1] = piece[...]


def join_rest(at, mine, other_own, other_rest, out):
    depth = mine.shape[0]
    for z in range(depth):
        out[z, at[X]] = mine[z]
    for k in range(depth):
        out[at[Z] ^ k, 1 - at[X]] = other_own[...] if k == 0 else other_rest[k - 1]


def join(at, mine, other, out):
    for src, side in ((mine, at[X]), (other, 1 - at[X])):
        for z in range(mine.shape[0]):
            out[z, side] = src[z]


def join_b(at, mine, other, y_mine, y_other, out):
    for i, pair in enumerate(((mine, other), (y_mine, y_other))):
        for src, side in zip(pair, (at[X], 1 - at[X])):
            for z in range(src.shape[0]):
                out[i, z, side] = src[z]


def join_a(at, kvm, kvo, kym, kyo, qm, qo, out, gains, biases):
    _three, depth, _two, rows, _n = out.shape
    size = 4 * D // (2 * depth)
    for i, pair in enumerate(((kvm, kvo), (kym, kyo), (qm, qo))):
        for src, side in zip(pair, (at[X], 1 - at[X])):
            for z in range(depth):
                out[i, z, side] = src[z, :rows]
    first = at[X] == 0
    for z in range(depth):
        a, b = qm[z, rows:, :size].astype(F32), qo[z, rows:, :size].astype(F32)
        for i, v in enumerate((jnp.where(first, a, b), jnp.where(first, b, a))):
            s = (z * 2 + i) * size
            gains[:, s : s + size] = v[0:1] + v[1:2]
            biases[:, s : s + size] = v[2:3] + v[3:4]


def place_b(at, own, came, cross_out, self_out, gate):
    t, c = at[T], at[C]
    for src, cc in ((own, c), (came, 1 - c)):
        for i in range(2):
            gate[:, t ^ i, :, half(cc)] = src[i, :, :, :HALF]
        cross_out[:, :, half(cc)] = src[t, :, :, HALF:]
        self_out[:, :, half(cc)] = src[1 - t, :, :, HALF:]


def normed_kernel(at, text, visual, gains, biases, text_normed, normed):
    normal, _f = stats(text[...].astype(F32))
    text_normed[...] = (normal * gain_of(gains, 1) + gain_of(biases, 1)).astype(BF)
    normal, _f = stats(visual[...].astype(F32))
    normed[...] = (normal * gain_of(gains, 0) + gain_of(biases, 0)).astype(BF)


def keyval_kernel(at, text_normed, normed, own, came, kv, w_kv, w_q, queries):
    t, c = at[T], at[C]

    @pl.when(pl.program_id(0) == 0)
    def _():
        for src, cc in ((own, c), (came, 1 - c)):
            for i in range(2):
                w_kv[:, pl.ds(pl.multiple_of((t ^ i) * D + cc * HALF, 128), HALF)] = src[i]
            w_q[:, half(cc)] = src[2]
        queries[...] = mm(normed[...], w_q[...]).astype(BF)

    kv[...] = mm(text_normed[...], w_kv[...]).astype(BF)


def cross_bias(owner, valid):
    n, m = valid.shape[1], owner.shape[1]
    parent = owner[...] == lax.broadcasted_iota(jnp.int32, (n, m), 0)
    ones = jnp.where(parent, 1.0, 0.0).astype(BF)
    real = jnp.broadcast_to(valid[...].astype(F32), (8, n)).astype(BF)
    present = mm(real, ones)[0:1] > 0.5
    return jnp.where(parent, shared_sheet_reward, 0.0) + jnp.where(present, 0.0, filtered_logits)


def cross_fwd(owner, valid, q, k, v, out, logs, bias):
    @pl.when(pl.program_id(0) == 0)
    def _():
        bias[...] = cross_bias(owner, valid)

    b = bias[...]
    scores = nt(two_heads(q[...]), k[...]) * SCALE + jnp.concatenate([b, b], 0)
    weight, log = softmax(scores)
    logs[0] = log
    out[...] = one_pair(mm(weight.astype(BF), v[...])).astype(BF)


def gate_kernel(at, mixed, normed, visual, gains, biases, w_out, w_gate, cross, gate, joined, second):
    rows = mm(mixed[...], w_out[...]).astype(BF)
    cross[...] = rows
    g = jax.nn.sigmoid(mm(normed[...], w_gate[:D]) + mm(rows, w_gate[D:]))
    gate[...] = g
    j = visual[...].astype(F32) + g * rows.astype(F32)
    joined[...] = j
    normal, _f = stats(j)
    second[...] = (normal * gain_of(gains, 2) + gain_of(biases, 2)).astype(BF)


def head_order(at, a):
    return jnp.where(at[C] == 0, a, jnp.concatenate([a[:, QUART:], a[:, :QUART]], 1))


def self_bias(page):
    n = page.shape[0] - 8
    return jnp.where(page[n : n + 8, :n].astype(F32)[0:1] > 0.5, 0.0, filtered_logits)


def self_fwd(at, second0, second1, valid0, valid1, w_own, w_oth, triple, att0, att1):
    n = second0.shape[0]
    rows = jnp.concatenate([second0[...], second1[...]], 0)
    own, oth = [mm(rows, w[...]).astype(BF) for w in (w_own, w_oth)]
    for i in range(3):
        triple[:, i * HALF : (i + 1) * HALF] = jnp.concatenate(
            [own[:, i * QUART : (i + 1) * QUART], oth[:, i * QUART : (i + 1) * QUART]], 1)
    for page, (valid, att) in enumerate(((valid0, att0), (valid1, att1))):
        bias = self_bias(valid)
        r = slice(page * n, (page + 1) * n)
        outs = []
        for p in range(3):
            q, k, v = [triple[r, i * HALF + p * 128 : i * HALF + (p + 1) * 128] for i in range(3)]
            weight, _l = softmax(nt(two_heads(q), k) * SCALE + bias)
            outs.append(one_pair(mm(weight.astype(BF), v)).astype(BF))
        att[...] = head_order(at, jnp.concatenate(outs, 1))


def carry_kernel(at, mine, came, joined, gains, biases, w, attended, carried, third):
    attended[:, half(at[T])] = mine[...]
    attended[:, half(1 - at[T])] = came[...]
    c = joined[...] + mm(attended[...], w[...])
    carried[...] = c
    normal, _f = stats(c)
    third[...] = (normal * gain_of(gains, 3) + gain_of(biases, 3)).astype(BF)


def ffn_kernel(last, at, third0, third1, cot0, cot1, w, *refs):
    n = third0.shape[0]
    if last:
        y0i, y1i, d0i, d1i, y0, y1, d0, d1, grad = refs
    else:
        y0, y1, d0, d1, grad = refs
    rows = jnp.concatenate([third0[...], third1[...]], 0)
    cot = jnp.concatenate([cot0[:n], cot1[:n]], 0)
    up, down = w[:, :D], w[:, D:]
    v = mm(rows, up)
    k = (2.0 / 3.141592653589793) ** 0.5
    th = jnp.tanh(k * (v + 0.044715 * (v * v * v)))
    act = (0.5 * v * (1.0 + th)).astype(BF)
    slope = 0.5 * (1.0 + th) + 0.5 * v * (1.0 - th * th) * (k * (1.0 + 3.0 * 0.044715 * (v * v)))
    y = mm(act, down)
    grad[:, D:] = tn(act, cot).astype(BF)
    dl = (nt(cot, down) * slope).astype(BF)
    d = nt(dl, up)
    grad[:, :D] = tn(rows, dl).astype(BF)
    if last:
        y0[...] = y[:n] + y0i[...]
        y1[...] = (y[n:] + y1i[...]).astype(BF)
        d0[...] = d[:n] + d0i[...]
        d1[...] = (d[n:] + d1i[...]).astype(BF)
    else:
        y0[...], y1[...], d0[...], d1[...] = y[:n], y[n:], d[:n], d[n:]


def carry_back(at, d0, came, carried, cot, attended, gains, w, d_carried, mine, send, grad, sums):
    normal, factor = stats(carried[...])
    dx, gain, bias = norm_back(d0[...] + came[...].astype(F32), normal, factor, gain_of(gains, 3))
    dc = cot[...].astype(F32) + dx
    d_carried[...] = dc
    low = dc.astype(BF)
    da = nt(low, w[...]).astype(BF)
    t0 = at[T] == 0
    mine[...] = head_order(at, jnp.where(t0, da[:, :HALF], da[:, HALF:]))
    send[...] = head_order(at, jnp.where(t0, da[:, HALF:], da[:, :HALF]))
    grad[...] = tn(attended[...], low).astype(BF)
    sums[0:1], sums[1:2] = gain, bias


def self_back(at, triple, da0, da1, valid0, valid1, second0, second1, w_own, w_oth, d0, d1, g_own, g_oth, dt):
    n = second0.shape[0]

    @pl.loop(0, 3)
    def _(p):
        lanes = [pl.ds(pl.multiple_of(i * HALF + p * 128, 128), 128) for i in range(3)]
        for page, (valid, da) in enumerate(((valid0, da0), (valid1, da1))):
            bias = self_bias(valid)
            r = slice(page * n, (page + 1) * n)
            q, k, v = [triple[r, lane] for lane in lanes]
            qq = two_heads(q)
            dd = two_heads(da[:, lanes[0]])
            weight, _l = softmax(nt(qq, k) * SCALE + bias)
            dp = nt(dd, v)
            ds = (weight * (dp - jnp.sum(weight * dp, -1, keepdims=True))).astype(BF)
            grads = (one_pair(mm(ds, k)) * SCALE, tn(ds, qq) * SCALE, tn(weight.astype(BF), dd))
            for i in range(3):
                dt[r, lanes[i]] = grads[i].astype(BF)

    none = jnp.zeros((2 * n, WIDE - 3 * QUART), BF)
    own = jnp.concatenate([dt[:, i * HALF : i * HALF + QUART] for i in range(3)] + [none], 1)
    oth = jnp.concatenate([dt[:, i * HALF + QUART : (i + 1) * HALF] for i in range(3)] + [none], 1)
    rows = jnp.concatenate([second0[...], second1[...]], 0)
    g_own[...] = tn(rows, own).astype(BF).reshape(g_own.shape)
    g_oth[...] = tn(rows, oth).astype(BF).reshape(g_oth.shape)
    d = nt(own, w_own[...]) + nt(oth, w_oth[...])
    d0[...] = d[:n]
    d1[...] = d[n:].astype(BF)


def gate_back(at, d_carried, d0, came, joined, normed, cross, gate, mixed, gains, w_gate, w_out, g_self,
              d_joined, d_mixed, d_normed, keep, send, sums):
    t, c = at[T], at[C]
    rows = keep.shape[2]
    normal, factor = stats(joined[...])
    dx, gain, bias = norm_back(d0[...] + came[...].astype(F32), normal, factor, gain_of(gains, 2))
    dj = d_carried[...] + dx
    d_joined[...] = dj
    sums[0:1], sums[1:2] = gain, bias
    g = gate[...]
    dg = (dj * cross[...].astype(F32) * g * (1.0 - g)).astype(BF)
    d_normed[...] = nt(dg, w_gate[:D])
    dc = (dj * g + nt(dg, w_gate[D:])).astype(BF)
    d_mixed[...] = nt(dc, w_out[...]).astype(BF)
    g_gate = jnp.concatenate([tn(normed[...], dg).astype(BF), tn(cross[...], dg).astype(BF)], 0)
    g_gate = g_gate.reshape(D // rows, 2, rows, D)
    g_out = tn(mixed[...], dc).astype(BF).reshape(D // rows, rows, D)
    g_so = g_self[...].reshape(D // rows, rows, D)
    for tt in range(2):
        for cc in range(2):
            lanes = slice(cc * HALF, (cc + 1) * HALF)
            side = g_out if tt == 0 else g_so
            for out, same in ((keep, True), (send, False)):
                @pl.when((c == cc) == same)
                def _():
                    out[t ^ tt, :, :, :HALF] = g_gate[:, tt, :, lanes]
                    out[t ^ tt, :, :, HALF:] = side[:, :, lanes]


def cross_back(owner, valid, q, k, v, dm, logs, dq, dkv, bias):
    @pl.when(pl.program_id(0) == 0)
    def _():
        bias[...] = cross_bias(owner, valid)

    b = bias[...]
    qq, dd = two_heads(q[...]), two_heads(dm[...])
    scores = nt(qq, k[...]) * SCALE + jnp.concatenate([b, b], 0)
    weight = jnp.exp(scores - logs[0])
    dp = nt(dd, v[...])
    ds = (weight * (dp - jnp.sum(weight * dp, -1, keepdims=True))).astype(BF)
    dq[...] = (one_pair(mm(ds, k[...])) * SCALE).astype(BF)
    dkv[0] = (tn(ds, qq) * SCALE).astype(BF)
    dkv[1] = tn(weight.astype(BF), dd).astype(BF)


def cross_weights(at, text_normed, normed, dq, dkv, grad):
    t = at[T]

    @pl.loop(0, 3)
    def _(j):
        lanes = pl.ds(pl.multiple_of(j * 256, 256), 256)
        x = text_normed[:, lanes]
        grad[t, lanes] = tn(x, dkv[0]).astype(BF)
        grad[1 - t, lanes] = tn(x, dkv[1]).astype(BF)
        grad[2, lanes] = tn(normed[:, lanes], dq[...]).astype(BF)


def text_back(at, text, gains, w_kv, own, oth, grad, sums):
    c = at[C]
    d = nt(own[0], w_kv[:, half(c)])
    d = d + nt(oth[0], w_kv[:, half(1 - c)])
    d = d + nt(own[1], w_kv[:, pl.ds(pl.multiple_of(D + c * HALF, 128), HALF)])
    d = d + nt(oth[1], w_kv[:, pl.ds(pl.multiple_of(D + (1 - c) * HALF, 128), HALF)])
    normal, factor = stats(text[...].astype(F32))
    dx, gain, bias = norm_back(d, normal, factor, gain_of(gains, 1))
    grad[...] = dx

    @pl.when(pl.program_id(0) == 0)
    def _():
        sums[...] = jnp.zeros_like(sums)

    sums[0:1] += gain
    sums[1:2] += bias


def visual_back(at, d_normed, dq_own, dq_oth, w_q, visual, d_joined, gains, s1, s2, s3, grad, norms):
    c = at[C]
    depth = norms.shape[0]
    size = 4 * D // (2 * depth)
    d = d_normed[...] + nt(dq_own[...], w_q[:, half(c)]) + nt(dq_oth[...], w_q[:, half(1 - c)])
    normal, factor = stats(visual[...].astype(F32))
    dx, gain, bias = norm_back(d, normal, factor, gain_of(gains, 0))
    grad[...] = d_joined[...] + dx
    g = jnp.concatenate([gain, s1[0:1], s2[0:1], s3[0:1]], 1)
    b = jnp.concatenate([bias, s1[1:2], s2[1:2], s3[1:2]], 1)
    row = lax.broadcasted_iota(jnp.int32, (8, size), 0)
    norms[...] = jnp.zeros_like(norms)
    for s in range(2 * depth):
        lanes = slice(s * size, (s + 1) * size)
        v = jnp.where(row == 0, jnp.broadcast_to(g[:, lanes], (8, size)), jnp.broadcast_to(b[:, lanes], (8, size)))
        norms[s // 2, s % 2, :, :size] = jnp.where(row < 2, v, 0.0).astype(BF)


def finish_ab(at, r, ry, rc, ryc, g_query, g_keyval, gains, biases):
    t, c = at[T], at[C]
    rows, size = g_query.shape[0], gains.shape[0]
    for a, b, cc in ((r, ry, c), (rc, ryc, 1 - c)):
        g_keyval[:, pl.ds(pl.multiple_of(t * D + cc * HALF, 128), HALF)] = a[:rows, :HALF].astype(F32)
        g_keyval[:, pl.ds(pl.multiple_of((1 - t) * D + cc * HALF, 128), HALF)] = b[:rows, :HALF].astype(F32)
        g_query[:, half(cc)] = a[:rows, HALF:].astype(F32) + b[:rows, HALF:].astype(F32)
    norms = [a[rows:, :size].astype(F32) for a in (r, ry, rc, ryc)]
    norms = norms[0] + norms[1] + norms[2] + norms[3]
    gains[...] = norms[0:1].reshape(size)
    biases[...] = norms[1:2].reshape(size)


def in_order(at, groups, lanes):
    c0, t0 = at[C] == 0, at[T] == 0
    own, y, core, both = [r[:, lanes].astype(F32) for r in groups]
    a0, a1 = jnp.where(c0, own, core), jnp.where(c0, core, own)
    b0, b1 = jnp.where(c0, y, both), jnp.where(c0, both, y)
    return jnp.where(t0, a0, b0), jnp.where(t0, a1, b1), jnp.where(t0, b0, a0), jnp.where(t0, b1, a1)


def finish_cd(at, r, ry, rc, ryc, g_qkv, g_up, g_down):
    groups = (r, ry, rc, ryc)
    rows = g_qkv.shape[0]
    p = in_order(at, groups, slice(0, D))
    for i in range(4):
        g_down[i * rows : (i + 1) * rows] = p[i]
    for s in range(D // rows):
        p = in_order(at, groups, slice(D + s * rows, D + (s + 1) * rows))
        g_up[:, s * 4 * rows : (s + 1) * 4 * rows] = jnp.concatenate(p, 1)
    for i in range(3):
        p = in_order(at, groups, slice(2 * D + i * QUART, 2 * D + (i + 1) * QUART))
        g_qkv[:, i * D : (i + 1) * D] = jnp.concatenate(p, 1)


def finish_b(at, r, ry, rc, ryc, g_out, g_gate, g_self):
    groups = (r, ry, rc, ryc)
    rows = g_out.shape[0]
    p = in_order(at, groups, slice(0, HALF))
    for i in range(4):
        g_gate[(i // 2) * rows : (i // 2 + 1) * rows, (i % 2) * HALF : (i % 2 + 1) * HALF] = p[i]
    p = in_order(at, groups, slice(HALF, D))
    g_out[...] = jnp.concatenate(p[:2], 1)
    g_self[...] = jnp.concatenate(p[2:], 1)


def reduce_x(count, extra, lanes, at, *refs):
    out = refs[-1]
    m = extra[0] if extra else 0
    for z in range(out.shape[0]):
        out[z] = reduced(refs, count, m, lanes, z, 1 - at[X]).astype(BF)


def reduced(refs, count, m, lanes, z, side):
    acc = refs[0][z, side, :, lanes].astype(F32)
    for r in refs[1:count]:
        acc = acc + r[z, side, :, lanes].astype(F32)
    if m:
        y = refs[count]
        y = (y[z, side] if len(y.shape) == 4 else y[z]).astype(F32)
        acc = acc + y if y.shape == acc.shape else jnp.concatenate([acc[:, :m] + y, acc[:, m:]], 1)
    return acc


def reduce_z(count, extra, lanes, at, *refs):
    got, keep, send = refs[-3:]
    m = extra[0] if extra else 0
    for i in range(keep.shape[0]):
        for k, out in ((2 * i, keep), (2 * i + 1, send)):
            z = at[Z] ^ k
            out[i] = (reduced(refs, count, m, lanes, z, at[X]) + got[z].astype(F32)).astype(BF)


def reduce_x_proj(at, own, oth, norms, out):
    rows = own.shape[2]
    for z in range(out.shape[0]):
        out[z, :rows] = reduced((own, oth), 1, oth.shape[-1], slice(None), z, 1 - at[X]).astype(BF)
        out[z, rows:] = norms[z, 1 - at[X]]


def reduce_z_proj(at, own, oth, norms, got, keep, send):
    rows = own.shape[2]
    for i in range(keep.shape[0]):
        for k, out in ((2 * i, keep), (2 * i + 1, send)):
            z = at[Z] ^ k
            b = got[z].astype(F32)
            out[i, :rows] = (reduced((own, oth), 1, oth.shape[-1], slice(None), z, at[X]) + b[:rows]).astype(BF)
            out[i, rows:] = (norms[z, at[X]].astype(F32) + b[rows:]).astype(BF)


def reduce_more(at, keep, got, *outs):
    for i in range(keep.shape[0]):
        v = (keep[i].astype(F32) + got[i].astype(F32)).astype(BF)
        if len(outs) == 1:
            outs[0][...] = v
        else:
            outs[i % 2][i // 2] = v


def reduce_last(count, at, *refs):
    out = refs[-1]
    at_lane = 0
    for keep, got in zip(refs[0 : 2 * count : 2], refs[1 : 2 * count : 2]):
        rows, n = keep.shape[1:]
        out[:rows, at_lane : at_lane + n] = (keep[0].astype(F32) + got[0].astype(F32)).astype(BF)
        at_lane += n


def add_core_b(at, keep, came, own, oth_send, oth_keep):
    x = at[X]
    for z in range(own.shape[0]):
        for i in range(2):
            own[z, i] = (keep[0, z, i].astype(F32) + came[0, z, i].astype(F32)).astype(BF)
        oth_send[z] = (keep[1, z, 1 - x].astype(F32) + came[1, z, 1 - x].astype(F32)).astype(BF)
        oth_keep[z] = (keep[1, z, x].astype(F32) + came[1, z, x].astype(F32)).astype(BF)


def add_core_a(at, keep, came, own, oth, q):
    for out, i in ((own, 0), (oth, 1), (q, 2)):
        out[...] = (keep[i].astype(F32) + came[i].astype(F32)).astype(BF)


def add_out(at, carried, y0, came, out):
    out[...] = (carried[...] + y0[...] + came[...].astype(F32)).astype(BF)


def local(reps, shards, visual, text, visual_valid, block_owner, cross_query, cross_keyval, cross_output, gate_weight,
          self_qkv, self_output, ffn_up, ffn_down, norm_gains, norm_biases, cotangent):
    ln = Links(reps, shards)
    at = ln.at
    od = Order()
    run = od.run
    visual, text, cotangent = visual[0], text[0], cotangent[0]
    rows, size = cross_query.shape[0], norm_gains.shape[0]
    vis, txt = visual.shape[0], text.shape[0]
    depth = shards // 2
    w3 = WIDE
    whole = lambda shape: pl.BlockSpec(shape, lambda *_: (0,) * len(shape))
    page = sds((vis, D), F32)
    grid4 = lambda n: (depth, 2, rows, n)

    def far_first(part):
        pieces = {0: part}
        for k in range(depth - 1, 0, -1):
            if k & (k - 1) == 0:
                pieces[k] = od.start(ln.along, part, k)
        return pieces

    def passed_on(pieces):
        for k in sorted(range(1, depth), key=lambda k: (bin(k).count("1"), -k)):
            if k not in pieces:
                od.wait(*[pieces[i] for i in sorted(pieces) if i])
                pieces[k] = od.start(ln.along, pieces[k & (k - 1)], k & -k)
        return [pieces[k] for k in range(depth)]

    (part_a,) = run(pack_a, [sds((rows + 16, D))], at, cross_query, cross_keyval, norm_gains, norm_biases, name="pack_a", far=True)
    pieces_a = far_first(part_a)
    part_b, part_c, part_d, cot = run(
        pack_rest, [sds((rows, D)), sds((rows, w3)), sds((rows, 2 * D)), sds((vis + 8, D))], at,
        cross_output, gate_weight, self_qkv, self_output, ffn_up, ffn_down, cotangent, visual_valid,
        name="pack_rest", far=True)
    d_xo, cot_y = ln.across(part_d), ln.y(cot)
    pieces_a = passed_on(pieces_a)
    od.wait(d_xo, cot_y)
    kv_m, qn_m = run(column_a, [sds((depth, rows, HALF)), sds((depth, rows + 16, HALF))], at, *pieces_a, name="column_a")
    kv_o, qn_o, kv_ym = ln.across(kv_m), ln.across(qn_m), ln.y(kv_m)
    pieces_b = passed_on(far_first(part_b))
    od.wait(kv_o)
    kv_yo = ln.y(kv_o)
    pieces_c = far_first(part_c)
    (b_m,) = run(column, [sds((depth, rows, D))], at, *pieces_b, name="column_b")
    joined_a, gains, biases = run(
        join_a, [sds((3,) + grid4(HALF)), sds((1, 4 * D), F32), sds((1, 4 * D), F32)],
        at, kv_m, kv_o, kv_ym, kv_yo, qn_m, qn_o, name="join_a")
    joined_a = joined_a.reshape(3, D, HALF)
    came_a = ln.core(joined_a)
    b_o, b_ym = od.start(ln.across, b_m), od.start(ln.y, b_m)
    tile = txt // 5
    row_tile = pl.BlockSpec((tile, D), lambda i: (i, 0))
    text_normed, normed = run(
        normed_kernel, [sds((txt, D)), sds((vis, D))], at, text, visual, gains, biases,
        grid=(5,), in_specs=[row_tile, whole((vis, D)), whole((1, 4 * D)), whole((1, 4 * D))],
        out_specs=[row_tile, whole((vis, D))], name="normed", vmem=12)
    pieces_c = passed_on(pieces_c)
    od.wait(came_a)
    pieces_d = far_first(part_d)

    kv, w_kv, w_q, queries = run(
        keyval_kernel, [sds((txt, 2 * D)), sds((D, 2 * D)), sds((D, D)), sds((vis, D))],
        at, text_normed, normed, joined_a, came_a,
        grid=(5,), in_specs=[row_tile, whole((vis, D)), whole((3, D, HALF)), whole((3, D, HALF))],
        out_specs=[pl.BlockSpec((tile, 2 * D), lambda i: (i, 0)), whole((D, 2 * D)), whole((D, D)), whole((vis, D))],
        name="keyval", vmem=30)
    (c_m,) = run(column, [sds((depth, rows, w3))], at, *pieces_c, name="column_c")
    od.wait(b_o, b_ym)
    c_o, b_yo = od.start(ln.across, c_m), od.start(ln.y, b_o)
    pairs = H // 2
    col = lambda n, off=0: pl.BlockSpec((n, 128), lambda p: (0, p + off))
    mixed, logs = run(
        lambda at, *refs: cross_fwd(*refs), [sds((vis, D)), sds((pairs, 2 * vis, 1), F32)],
        at, block_owner, visual_valid, queries, kv, kv,
        grid=(pairs,), in_specs=[whole((1, txt)), whole((1, vis)), col(vis), col(txt), col(txt, pairs)],
        out_specs=[col(vis), pl.BlockSpec((1, 2 * vis, 1), lambda p: (p, 0, 0))],
        scratch=[sds((vis, txt), F32)], name="cross_fwd", vmem=16)
    pieces_d = passed_on(pieces_d)
    (wc_own,) = run(join, [sds(grid4(w3))], at, c_m, c_o, name="join_c")
    wc_oth = ln.core(wc_own)
    (joined_b,) = run(join_b, [sds((2,) + grid4(D))], at, b_m, b_o, b_ym, b_yo, name="join_b")
    joined_b = joined_b.reshape(2, shards, rows, D)
    came_b = ln.core(joined_b)
    w_out, w_self, w_gate = run(
        place_b, [sds((shards, rows, D)), sds((shards, rows, D)), sds((shards, 2, rows, D))], at, joined_b, came_b, name="place_b")
    w_out, w_self, w_gate = w_out.reshape(D, D), w_self.reshape(D, D), w_gate.reshape(2 * D, D)
    od.wait(wc_oth)
    wc_own, wc_oth = wc_own.reshape(D, w3), wc_oth.reshape(D, w3)
    cross, gate, joined, second = run(
        gate_kernel, [sds((vis, D)), page, page, sds((vis, D))],
        at, mixed, normed, visual, gains, biases, w_out, w_gate, name="gate")
    second_y = ln.y(second)
    d_m, d_rest = run(column_rest, [sds((depth, rows, 2 * D)), sds((depth - 1, rows, 2 * D))], at, *pieces_d, name="column_d")
    d_xr, d_cm, d_cxo = ln.across(d_rest), ln.core(d_m), od.start(ln.core, d_xo)
    triple, att_mine, att_send = run(
        self_fwd, [sds((2 * vis, 3 * HALF)), sds((vis, HALF)), sds((vis, HALF))],
        at, second, second_y, cot, cot_y, wc_own, wc_oth, name="self_fwd")
    att_came = ln.y(att_send)
    od.wait(d_cm, d_cxo)
    attended, carried, third = run(
        carry_kernel, [sds((vis, D)), page, sds((vis, D))],
        at, att_mine, att_came, joined, gains, biases, w_self, name="carry")
    third_y = ln.y(third)
    od.wait(third_y)
    d_cxr = od.start(ln.core, d_xr)
    (wd_own,) = run(join_rest, [sds(grid4(2 * D))], at, d_m, d_xo, d_xr, name="join_d")
    (wd_oth,) = run(join_rest, [sds(grid4(2 * D))], at, d_cm, d_cxo, d_cxr, name="join_d")
    wd_own, wd_oth = wd_own.reshape(D, 2 * D), wd_oth.reshape(D, 2 * D)

    y0, y1, d0, d1, gd_oth = run(
        functools.partial(ffn_kernel, False), [page] * 4 + [sds((D, 2 * D))],
        at, third, third_y, cot, cot_y, wd_oth, name="ffn_first")
    gd_came = ln.core(gd_oth).reshape(grid4(2 * D))
    y0, y1, d0, d1, gd_own = run(
        functools.partial(ffn_kernel, True), [page, sds((vis, D))] * 2 + [sds((D, 2 * D))],
        at, third, third_y, cot, cot_y, wd_own, y0, y1, d0, d1, name="ffn_second")
    gd_own = gd_own.reshape(grid4(2 * D))
    d1_came = ln.y(d1)

    class Sum:
        def __init__(self, name, arrays, n, lanes=slice(None), sends=(), keeps=(), norms=None):
            self.name, self.n, self.rows = name, n, arrays[0].shape[2]
            extra = [a.shape[-1] for a in keeps]
            first, self.second = [functools.partial(f, len(arrays), extra, lanes) for f in (reduce_x, reduce_z)]
            self.late = list(arrays) + list(keeps)
            early = list(arrays) + list(sends)
            if norms is not None:
                first, self.second, self.rows = reduce_x_proj, reduce_z_proj, self.rows + norms.shape[2]
                self.late, early = self.late + [norms], early + [norms]
            (self.send,) = run(first, [sds((depth, self.rows, n))], at, *early, name="reduce_x_" + name)
            self.bit = 0

        def go(self):
            self.got = od.start(ln.across, self.send)
            return self

        def step(self):
            if self.bit == 0:
                outs = [sds((depth // 2, self.rows, self.n))] * 2
                self.keep, send = run(self.second, outs, at, *self.late, self.got, name="reduce_z_" + self.name)
                self.bit = 1
            elif self.keep.shape[0] > 1:
                outs = [sds((self.keep.shape[0] // 2, self.rows, self.n))] * 2
                self.keep, send = run(reduce_more, outs, at, self.keep, self.got, name="reduce_m_" + self.name)
                self.bit *= 2
            else:
                return False
            self.got = ln.along(send, self.bit)
            return True

    def finish(*sums):
        ins = [a for one in sums for a in (one.keep, one.got)]
        (total,) = run(functools.partial(reduce_last, len(sums)), [sds((sums[0].rows, sum(one.n for one in sums)))], at,
                       *ins, name="reduce_last")
        for bit in range(2, reps.bit_length() - 1):
            total = (total.astype(F32) + ln.rep_bit(total, 1 << bit).astype(F32)).astype(BF)
        ry = ln.y(total)
        return total, ry, ln.core(total), ln.core(ry)

    def back_half(index):
        def spec(n, off=0):
            return pl.BlockSpec((n, 128), lambda p, at: (0, (at[C] ^ index) * 3 + p + off))

        return run(
            lambda at, *refs: cross_back(*refs), [sds((vis, HALF)), sds((2, txt, HALF))],
            at, block_owner, visual_valid, queries, kv, kv, d_mixed, logs, prefetch=True, grid=(3,),
            in_specs=[whole((1, txt)), whole((1, vis)), spec(vis), spec(txt), spec(txt, pairs), spec(vis),
                      pl.BlockSpec((1, 2 * vis, 1), lambda p, at: ((at[C] ^ index) * 3 + p, 0, 0))],
            out_specs=[pl.BlockSpec((vis, 128), lambda p, at: (0, p)), pl.BlockSpec((2, txt, 128), lambda p, at: (0, 0, p))],
            scratch=[sds((vis, txt), F32)], name="cross_back", vmem=20)

    def weights_half(dq, dkv):
        return run(cross_weights, [sds((3, D, HALF))], at, text_normed, normed, dq, dkv, name="cross_weights")[0]

    down = Sum("down", [gd_own, gd_came], D, slice(D, 2 * D)).go()
    d_carried, da_mine, da_send, g_self, sums3 = run(
        carry_back, [page, sds((vis, HALF)), sds((vis, HALF)), sds((D, D)), sds((2, D), F32)],
        at, d0, d1_came, carried, cotangent, attended, gains, w_self, name="carry_back")
    da_came = ln.y(da_send)
    up = Sum("up", [gd_own, gd_came], D, slice(0, D))
    od.wait(da_came)
    down.step()
    up.go()
    ds0, ds1, gc_own, gc_oth = run(
        self_back, [page, sds((vis, D)), sds(grid4(w3)), sds(grid4(w3))],
        at, triple, da_mine, da_came, cot, cot_y, second, second_y, wc_own, wc_oth,
        scratch=[sds((2 * vis, 3 * HALF))], name="self_back")
    ds1_came = ln.y(ds1)
    gc_came = ln.core(gc_oth)
    down.step()
    up.step()
    d_joined, d_mixed, d_normed, b_keep, b_send, sums2 = run(
        gate_back, [page, sds((vis, D)), page, sds((2, shards, rows, D)), sds((2, shards, rows, D)), sds((2, D), F32)],
        at, d_carried, ds0, ds1_came, joined, normed, cross, gate, mixed, gains, w_gate, w_out, g_self, name="gate_back")
    b_came = ln.core(b_send)
    y1_came = od.start(ln.y, y1)
    dq_oth, dkv_oth = back_half(1)
    qkv = Sum("qkv", [gc_own, gc_came], w3).go()
    od.wait(y1_came)
    own_b, b_ys, b_yk = run(
        add_core_b, [sds(grid4(D)), sds((depth, rows, D)), sds((depth, rows, D))], at,
        b_keep.reshape((2,) + grid4(D)), b_came.reshape((2,) + grid4(D)), name="add_core_b")
    b_ys = ln.y(b_ys)
    a_came = ln.core(weights_half(dq_oth, dkv_oth))
    dq_own, dkv_own = back_half(0)
    up.step()
    gates = Sum("gate", [own_b], D, sends=[b_ys], keeps=[b_yk]).go()
    qkv.step()
    a_keep = weights_half(dq_own, dkv_own)
    od.wait(down.got)
    own_a, a_y, own_q = run(
        add_core_a, [sds(grid4(HALF))] * 3, at,
        a_keep.reshape((3,) + grid4(HALF)), a_came.reshape((3,) + grid4(HALF)), name="add_core_a")
    a_y = ln.y(a_y)
    query = Sum("query", [own_q], HALF).go()
    row3 = pl.BlockSpec((2, tile, HALF), lambda i: (0, i, 0))
    grad_text, sums1 = run(
        text_back, [sds((txt, D), F32), sds((2, D), F32)],
        at, text, gains, w_kv, dkv_own, dkv_oth,
        grid=(5,), in_specs=[row_tile, whole((1, 4 * D)), whole((D, 2 * D)), row3, row3],
        out_specs=[row_tile, whole((2, D))], name="text_back", vmem=24)
    od.wait(up.got, gates.got)
    qkv.step()
    query.step()
    grad_visual, norms = run(
        visual_back, [page, sds((depth, 2, 8, HALF))],
        at, d_normed, dq_own, dq_oth, w_q, visual, d_joined, gains, sums1, sums2, sums3, name="visual_back")
    keyval = Sum("keyval", [own_a], HALF, sends=[a_y], keeps=[a_y], norms=norms).go()
    gates.late[1] = od.start(ln.y, b_yk)
    (layer_out,) = run(add_out, [sds((vis, D))], at, carried, y0, y1_came, name="add_out")
    query.step()
    keyval.step()
    first = finish(down, up, qkv)
    od.wait(query.got)
    keyval.step()
    gates.step()
    out = lambda r, n: sds((r, n), F32)
    last_a = finish(keyval, query)
    gates.step()
    g_qkv, g_up, g_down = run(
        finish_cd, [out(rows, 3 * D), out(rows, 4 * D), out(4 * rows, D)], at, *first, name="finish_cd")
    last_b = finish(gates)
    g_query, g_keyval, g_gains, g_biases = run(
        finish_ab, [out(rows, D), out(rows, 2 * D), sds((size,), F32), sds((size,), F32)], at, *last_a, name="finish_a")
    g_out, g_gate, g_self_out = run(
        finish_b, [out(rows, D), out(2 * rows, D), out(rows, D)], at, *last_b, name="finish_b")
    return (layer_out[None], grad_visual[None], grad_text[None], g_query, g_keyval, g_out, g_gate, g_qkv, g_self_out,
            g_up, g_down, g_gains, g_biases)


def solution(mesh):
    pages = P(("rep", "fsdp"), None, None)
    flags = P(("rep", "fsdp"), None)
    matrix = P("fsdp", None)
    vector = P("fsdp")
    in_specs = (pages, pages, flags, flags) + (matrix,) * 8 + (vector, vector, pages)
    out_specs = (pages, pages, pages) + (matrix,) * 8 + (vector, vector)
    reps, shards = mesh.shape["rep"], mesh.shape["fsdp"]

    def program(*args):
        return local(reps, shards, *args)

    return jax.shard_map(program, mesh=mesh, in_specs=in_specs, out_specs=out_specs, check_vma=False)
```

```python
import functools

import jax
import jax.numpy as jnp
from jax import lax
from jax.experimental import pallas as pl
from jax.experimental.pallas import tpu as pltpu
from jax.sharding import PartitionSpec as P

H = 12
HD = 64
D = H * HD
HALF = D // 2
QUART = D // 4
WIDE = -(-3 * QUART // 128) * 128
BF = jnp.bfloat16
F32 = jnp.float32

epsilon = 1e-05
filtered_logits = -1000000000.0
shared_sheet_reward = 6.0
SCALE = HD ** (-0.5)
VM = pl.BlockSpec()
SM = pl.BlockSpec(memory_space=pltpu.SMEM)
ANY = pl.BlockSpec(memory_space=pl.ANY)
PIN = pl.BlockSpec(memory_space=pltpu.VMEM)


def sds(shape, dtype=BF):
    return jax.ShapeDtypeStruct(tuple(shape), dtype)


def size_of(a):
    n = jnp.dtype(a.dtype).itemsize
    for d in a.shape:
        n *= d
    return n


class Order:
    def __init__(self):
        self.tokens = []

    def start(self, exchange, a, *args):
        a, *self.tokens = lax.optimization_barrier((a, *self.tokens))
        return exchange(a, *args)

    def wait(self, *arrays):
        self.tokens = self.tokens + list(arrays)

    def run(self, body, outs, where, *ins, name=None, scratch=(), grid=None, in_specs=None, out_specs=None, vmem=None, prefetch=False, far=False, cost=0):
        moved = sum(size_of(a) for a in ins) + sum(size_of(o) for o in outs)
        held = moved + sum(size_of(s) for s in scratch)
        limit = 66_000_000 if far else vmem << 20 if vmem else min(60 << 20, int(1.25 * held) + (10 << 20))
        ins_specs = ([VM] * len(ins) if in_specs is None else in_specs) + [ANY] * len(self.tokens)
        spec = dict(in_specs=([] if prefetch else [SM]) + ins_specs,
                    out_specs=([VM] * len(outs) if out_specs is None else out_specs) + [pl.BlockSpec((8, 128), lambda *_: (0, 0)) if grid else VM],
                    scratch_shapes=[pltpu.VMEM(s.shape, s.dtype) for s in scratch])
        if prefetch:
            spec = dict(grid_spec=pltpu.PrefetchScalarGridSpec(num_scalar_prefetch=1, grid=grid, **spec))
        elif grid is not None:
            spec["grid"] = grid
        kernel, count, late = body, len(ins), len(self.tokens)
        if far:
            spec["in_specs"] = [SM] + [pl.BlockSpec(memory_space=pltpu.HBM)] * count + [ANY] * late
            spec["scratch_shapes"] = [pltpu.VMEM(a.shape, a.dtype) for a in ins] + [pltpu.SemaphoreType.DMA((count,))]

            def kernel(at, *refs):
                held, sems = refs[-1 - count : -1], refs[-1]
                copies = [pltpu.make_async_copy(refs[i], held[i], sems.at[i]) for i in range(count)]
                for one in copies:
                    one.start()
                for one in copies:
                    one.wait()
                body(at, *held, *refs[count : -1 - count])

        ends = count + late + len(outs)

        def marked(at, *refs):
            refs[ends][...] = jnp.zeros((8, 128), F32)
            kernel(at, *refs[:count], *refs[count + late : ends], *refs[ends + 1 :])

        *got, mark = pl.pallas_call(
            marked,
            out_shape=list(outs) + [sds((8, 128), F32)],
            compiler_params=pltpu.CompilerParams(vmem_limit_bytes=limit),
            cost_estimate=pl.CostEstimate(flops=cost * 1_150_000_000, bytes_accessed=1024, transcendentals=0),
            name=name,
            **spec,
        )(where, *ins, *self.tokens)
        self.tokens = [mark]
        return got


T, C, X, Z = 0, 1, 2, 3


class Links:
    def __init__(self, reps, shards):
        self.reps, self.shards = reps, shards
        self.depth = shards // 2
        rank = lax.axis_index("rep")
        shard = lax.axis_index("fsdp")
        self.shard = shard
        self.at = jnp.stack([(rank // 2) % 2, rank % 2, shard % 2, shard // 2]).astype(jnp.int32)

    def core(self, a):
        return lax.ppermute(a, "rep", [(r, r ^ 1) for r in range(self.reps)])

    def y(self, a):
        return lax.ppermute(a, "rep", [(r, r ^ 2) for r in range(self.reps)])

    def rep_bit(self, a, bit):
        return lax.ppermute(a, "rep", [(r, r ^ bit) for r in range(self.reps)])

    def across(self, a):
        return lax.ppermute(a, "fsdp", [(s, s ^ 1) for s in range(self.shards)])

    def along(self, a, k):
        return lax.ppermute(a, "fsdp", [(s, s ^ (2 * k)) for s in range(self.shards)])


def mm(a, b):
    return jnp.dot(a, b, preferred_element_type=F32)


def nt(a, b):
    return lax.dot_general(a, b, (((1,), (1,)), ((), ())), preferred_element_type=F32)


def tn(a, b):
    return lax.dot_general(a, b, (((0,), (0,)), ((), ())), preferred_element_type=F32)


def stats(rows):
    mean = jnp.mean(rows, -1, keepdims=True)
    centred = rows - mean
    factor = lax.rsqrt(jnp.mean(centred * centred, -1, keepdims=True) + epsilon)
    return centred * factor, factor


def norm_back(grad, normal, factor, gain):
    scaled = grad * gain
    dx = scaled - jnp.mean(scaled, -1, keepdims=True) - normal * jnp.mean(scaled * normal, -1, keepdims=True)
    return dx * factor, jnp.sum(grad * normal, 0, keepdims=True), jnp.sum(grad, 0, keepdims=True)


def gain_of(ref, i):
    return ref[:, i * D : (i + 1) * D]


def half(i):
    return pl.ds(pl.multiple_of(i * HALF, 128), HALF)


def pair_masks(rows):
    lane = lax.broadcasted_iota(jnp.int32, (rows, 128), 1)
    return lane < HD


def two_heads(a):
    first = pair_masks(a.shape[0])
    zero = jnp.zeros_like(a)
    return jnp.concatenate([jnp.where(first, a, zero), jnp.where(first, zero, a)], 0)


def one_pair(a):
    n = a.shape[0] // 2
    return jnp.where(pair_masks(n), a[:n], a[n:])


def softmax(scores):
    peak = jnp.max(scores, -1, keepdims=True)
    expo = jnp.exp(scores - peak)
    total = jnp.sum(expo, -1, keepdims=True)
    return expo * (1.0 / total), peak + jnp.log(total)


def pack_a(at, query, keyval, gains, biases, part):
    rows, size = query.shape[0], gains.shape[0]
    part[:rows, :HALF] = keyval[:, pl.ds(pl.multiple_of(at[T] * D + at[C] * HALF, 128), HALF)]
    part[:rows, HALF:] = query[:, half(at[C])]
    part[rows:, :] = jnp.zeros((16, D), BF)
    g, b = gains[...].reshape(1, size), biases[...].reshape(1, size)
    g_hi, b_hi = g.astype(BF), b.astype(BF)
    g_lo, b_lo = (g - g_hi.astype(F32)).astype(BF), (b - b_hi.astype(F32)).astype(BF)
    row = lax.broadcasted_iota(jnp.int32, (16, size), 0)
    out = jnp.zeros((16, size), F32)
    for i, v in enumerate((g_hi, g_lo, b_hi, b_lo)):
        out = jnp.where(row == i, jnp.broadcast_to(v.astype(F32), (16, size)), out)
    part[rows:, HALF : HALF + size] = out.astype(BF)


def pack_rest(at, output, gate, qkv, self_out, up, down, cot, valid, part_b, part_c, part_d, page):
    rows = output.shape[0]
    n = cot.shape[0]
    page[:n] = cot[...]
    page[n:, :n] = jnp.broadcast_to(valid[...], (8, n)).astype(F32).astype(BF)
    page[n:, n:] = jnp.zeros((8, D - n), BF)
    shards = D // rows
    t0, c0 = at[T] == 0, at[C] == 0
    gate_c, out_c, self_c = gate[:, half(at[C])], output[:, half(at[C])], self_out[:, half(at[C])]
    part_b[:, :HALF] = jnp.where(t0, gate_c[:rows], gate_c[rows:])
    part_b[:, HALF:D] = jnp.where(t0, out_c, self_c)
    pieces = []
    for i in range(3):
        v = qkv[:, pl.ds(pl.multiple_of(i * D + at[T] * HALF, 128), HALF)]
        pieces.append(jnp.where(c0, v[:, :QUART], v[:, QUART:]))
    part_c[...] = jnp.concatenate(pieces + [jnp.zeros((rows, WIDE - 3 * QUART), BF)], 1)
    pieces = []
    for s in range(shards):
        v = [up[:, (s * 4 + g) * rows : (s * 4 + g + 1) * rows] for g in range(4)]
        pieces.append(jnp.where(t0, jnp.where(c0, v[0], v[1]), jnp.where(c0, v[2], v[3])))
    part_d[:, :D] = jnp.concatenate(pieces, 1)
    v = [down[g * rows : (g + 1) * rows, :] for g in range(4)]
    part_d[:, D:] = jnp.where(t0, jnp.where(c0, v[0], v[1]), jnp.where(c0, v[2], v[3]))


def column(at, *refs):
    for k, piece in enumerate(refs[:-1]):
        refs[-1][at[Z] ^ k] = piece[...]


def column_a(at, *refs):
    kv, qn = refs[-2:]
    rows = kv.shape[1]
    for k, piece in enumerate(refs[:-2]):
        kv[at[Z] ^ k] = piece[:rows, :HALF]
        qn[at[Z] ^ k] = piece[:, HALF:]


def column_halves(at, *refs):
    up, down = refs[-2:]
    for k, piece in enumerate(refs[:-2]):
        up[at[Z] ^ k] = piece[:, :D]
        down[at[Z] ^ k] = piece[:, D:]


def join_pieces(at, up, down, *refs):
    out = refs[-1]
    for z in range(up.shape[0]):
        out[z, at[X], :, :D] = up[z]
        out[z, at[X], :, D:] = down[z]
    for k, piece in enumerate(refs[:-1]):
        out[at[Z] ^ k, 1 - at[X]] = piece[...]


def join(at, mine, other, out):
    for src, side in ((mine, at[X]), (other, 1 - at[X])):
        for z in range(mine.shape[0]):
            out[z, side] = src[z]


def join_b(at, mine, other, y_mine, y_other, out):
    for i, pair in enumerate(((mine, other), (y_mine, y_other))):
        for src, side in zip(pair, (at[X], 1 - at[X])):
            for z in range(src.shape[0]):
                out[i, z, side] = src[z]


def join_a(at, kvm, kvo, kym, kyo, qm, qo, out, gains, biases):
    _three, depth, _two, rows, _n = out.shape
    size = 4 * D // (2 * depth)
    for i, pair in enumerate(((kvm, kvo), (kym, kyo), (qm, qo))):
        for src, side in zip(pair, (at[X], 1 - at[X])):
            for z in range(depth):
                out[i, z, side] = src[z, :rows]
    first = at[X] == 0
    for z in range(depth):
        a, b = qm[z, rows:, :size].astype(F32), qo[z, rows:, :size].astype(F32)
        for i, v in enumerate((jnp.where(first, a, b), jnp.where(first, b, a))):
            s = (z * 2 + i) * size
            gains[:, s : s + size] = v[0:1] + v[1:2]
            biases[:, s : s + size] = v[2:3] + v[3:4]


def place_b(at, own, came, cross_out, self_out, gate):
    t, c = at[T], at[C]
    for src, cc in ((own, c), (came, 1 - c)):
        for i in range(2):
            gate[:, t ^ i, :, half(cc)] = src[i, :, :, :HALF]
        cross_out[:, :, half(cc)] = src[t, :, :, HALF:]
        self_out[:, :, half(cc)] = src[1 - t, :, :, HALF:]


def normed_kernel(at, text, visual, gains, biases, text_normed, normed):
    normal, _f = stats(text[...].astype(F32))
    text_normed[...] = (normal * gain_of(gains, 1) + gain_of(biases, 1)).astype(BF)
    normal, _f = stats(visual[...].astype(F32))
    normed[...] = (normal * gain_of(gains, 0) + gain_of(biases, 0)).astype(BF)


def keyval_kernel(at, text_normed, normed, own, came, kv, w_kv, w_q, queries):
    t, c = at[T], at[C]

    @pl.when(pl.program_id(0) == 0)
    def _():
        for src, cc in ((own, c), (came, 1 - c)):
            for i in range(2):
                w_kv[:, pl.ds(pl.multiple_of((t ^ i) * D + cc * HALF, 128), HALF)] = src[i]
            w_q[:, half(cc)] = src[2]
        queries[...] = mm(normed[...], w_q[...]).astype(BF)

    kv[...] = mm(text_normed[...], w_kv[...]).astype(BF)


def cross_bias(owner, valid):
    n, m = valid.shape[1], owner.shape[1]
    parent = owner[...] == lax.broadcasted_iota(jnp.int32, (n, m), 0)
    ones = jnp.where(parent, 1.0, 0.0).astype(BF)
    real = jnp.broadcast_to(valid[...].astype(F32), (8, n)).astype(BF)
    present = mm(real, ones)[0:1] > 0.5
    return jnp.where(parent, shared_sheet_reward, 0.0) + jnp.where(present, 0.0, filtered_logits)


def lanes_at(i):
    return pl.ds(pl.multiple_of(i * 128, 128), 128)


def cross_fwd(at, owner, valid, q, kv, out, logs, bias):
    bias[...] = cross_bias(owner, valid)
    pairs = q.shape[1] // 128

    @pl.loop(0, pairs)
    def _(p):
        b = bias[...]
        k, v = kv[:, lanes_at(p)], kv[:, lanes_at(pairs + p)]
        scores = nt(two_heads(q[:, lanes_at(p)] * SCALE), k) + jnp.concatenate([b, b], 0)
        weight, log = softmax(scores)
        logs[p] = log
        out[:, lanes_at(p)] = one_pair(mm(weight.astype(BF), v)).astype(BF)


def gate_kernel(at, mixed, normed, visual, gains, biases, w_out, w_gate, cross, gate, joined, second):
    rows = mm(mixed[...], w_out[...]).astype(BF)
    cross[...] = rows
    g = jax.nn.sigmoid(mm(normed[...], w_gate[:D]) + mm(rows, w_gate[D:]))
    gate[...] = g
    j = visual[...].astype(F32) + g * rows.astype(F32)
    joined[...] = j
    normal, _f = stats(j)
    second[...] = (normal * gain_of(gains, 2) + gain_of(biases, 2)).astype(BF)


def head_order(at, a):
    return jnp.where(at[C] == 0, a, jnp.concatenate([a[:, QUART:], a[:, :QUART]], 1))


def self_bias(page):
    n = page.shape[0] - 8
    return jnp.where(page[n : n + 8, :n].astype(F32)[0:1] > 0.5, 0.0, filtered_logits)


def self_fwd(at, second0, second1, valid0, valid1, w_own, w_oth, triple, att0, att1):
    n = second0.shape[0]
    rows = jnp.concatenate([second0[...], second1[...]], 0)
    own, oth = [mm(rows, w[...]).astype(BF) for w in (w_own, w_oth)]
    for i in range(3):
        triple[:, i * HALF : (i + 1) * HALF] = jnp.concatenate(
            [own[:, i * QUART : (i + 1) * QUART], oth[:, i * QUART : (i + 1) * QUART]], 1)
    for page, (valid, att) in enumerate(((valid0, att0), (valid1, att1))):
        bias = self_bias(valid)
        r = slice(page * n, (page + 1) * n)
        outs = []
        for p in range(3):
            q, k, v = [triple[r, i * HALF + p * 128 : i * HALF + (p + 1) * 128] for i in range(3)]
            weight, _l = softmax(nt(two_heads(q), k) * SCALE + bias)
            outs.append(one_pair(mm(weight.astype(BF), v)).astype(BF))
        att[...] = head_order(at, jnp.concatenate(outs, 1))


def carry_kernel(at, mine, came, joined, gains, biases, w, attended, carried, third):
    attended[:, half(at[T])] = mine[...]
    attended[:, half(1 - at[T])] = came[...]
    c = joined[...] + mm(attended[...], w[...])
    carried[...] = c
    normal, _f = stats(c)
    third[...] = (normal * gain_of(gains, 3) + gain_of(biases, 3)).astype(BF)


def ffn_kernel(last, at, third0, third1, cot0, cot1, w, *refs):
    n = third0.shape[0]
    if last:
        y0i, y1i, d0i, d1i, y0, y1, d0, d1, g_up, g_down = refs
    else:
        y0, y1, d0, d1, g_up, g_down = refs
    rows = jnp.concatenate([third0[...], third1[...]], 0)
    cot = jnp.concatenate([cot0[:n], cot1[:n]], 0)
    up, down = w[:, :D], w[:, D:]
    v = mm(rows, up)
    k = (2.0 / 3.141592653589793) ** 0.5
    th = jnp.tanh(k * (v + 0.044715 * (v * v * v)))
    act = (0.5 * v * (1.0 + th)).astype(BF)
    slope = 0.5 * (1.0 + th) + 0.5 * v * (1.0 - th * th) * (k * (1.0 + 3.0 * 0.044715 * (v * v)))
    y = mm(act, down)
    g_down[...] = tn(act, cot).astype(BF)
    dl = (nt(cot, down) * slope).astype(BF)
    d = nt(dl, up)
    g_up[...] = tn(rows, dl).astype(BF)
    if last:
        y0[...] = y[:n] + y0i[...]
        y1[...] = (y[n:] + y1i[...]).astype(BF)
        d0[...] = d[:n] + d0i[...]
        d1[...] = (d[n:] + d1i[...]).astype(BF)
    else:
        y0[...], y1[...], d0[...], d1[...] = y[:n], y[n:], d[:n], d[n:]


def carry_back(at, d0, came, carried, cot, attended, gains, w, d_carried, mine, send, grad, sums):
    normal, factor = stats(carried[...])
    dx, gain, bias = norm_back(d0[...] + came[...].astype(F32), normal, factor, gain_of(gains, 3))
    dc = cot[...].astype(F32) + dx
    d_carried[...] = dc
    low = dc.astype(BF)
    da = nt(low, w[...]).astype(BF)
    t0 = at[T] == 0
    mine[...] = head_order(at, jnp.where(t0, da[:, :HALF], da[:, HALF:]))
    send[...] = head_order(at, jnp.where(t0, da[:, HALF:], da[:, :HALF]))
    grad[...] = tn(attended[...], low).astype(BF)
    sums[0:1], sums[1:2] = gain, bias


def self_back(at, triple, da0, da1, valid0, valid1, second0, second1, w_own, w_oth, d0, d1, g_own, g_oth, dt):
    n = second0.shape[0]

    @pl.loop(0, 3)
    def _(p):
        lanes = [pl.ds(pl.multiple_of(i * HALF + p * 128, 128), 128) for i in range(3)]
        for page, (valid, da) in enumerate(((valid0, da0), (valid1, da1))):
            bias = self_bias(valid)
            r = slice(page * n, (page + 1) * n)
            q, k, v = [triple[r, lane] for lane in lanes]
            qq = two_heads(q)
            dd = two_heads(da[:, lanes[0]])
            weight, _l = softmax(nt(qq, k) * SCALE + bias)
            dp = nt(dd, v)
            ds = (weight * (dp - jnp.sum(weight * dp, -1, keepdims=True))).astype(BF)
            grads = (one_pair(mm(ds, k)) * SCALE, tn(ds, qq) * SCALE, tn(weight.astype(BF), dd))
            for i in range(3):
                dt[r, lanes[i]] = grads[i].astype(BF)

    none = jnp.zeros((2 * n, WIDE - 3 * QUART), BF)
    own = jnp.concatenate([dt[:, i * HALF : i * HALF + QUART] for i in range(3)] + [none], 1)
    oth = jnp.concatenate([dt[:, i * HALF + QUART : (i + 1) * HALF] for i in range(3)] + [none], 1)
    rows = jnp.concatenate([second0[...], second1[...]], 0)
    g_own[...] = tn(rows, own).astype(BF).reshape(g_own.shape)
    g_oth[...] = tn(rows, oth).astype(BF).reshape(g_oth.shape)
    d = nt(own, w_own[...]) + nt(oth, w_oth[...])
    d0[...] = d[:n]
    d1[...] = d[n:].astype(BF)


def gate_back(at, d_carried, d0, came, joined, normed, cross, gate, mixed, gains, w_gate, w_out, g_self,
              d_joined, d_mixed, d_normed, keep, send, sums):
    t, c = at[T], at[C]
    rows = keep.shape[2]
    normal, factor = stats(joined[...])
    dx, gain, bias = norm_back(d0[...] + came[...].astype(F32), normal, factor, gain_of(gains, 2))
    dj = d_carried[...] + dx
    d_joined[...] = dj
    sums[0:1], sums[1:2] = gain, bias
    g = gate[...]
    dg = (dj * cross[...].astype(F32) * g * (1.0 - g)).astype(BF)
    d_normed[...] = nt(dg, w_gate[:D])
    dc = (dj * g + nt(dg, w_gate[D:])).astype(BF)
    d_mixed[...] = nt(dc, w_out[...]).astype(BF)
    g_gate = jnp.concatenate([tn(normed[...], dg).astype(BF), tn(cross[...], dg).astype(BF)], 0)
    g_gate = g_gate.reshape(D // rows, 2, rows, D)
    g_out = tn(mixed[...], dc).astype(BF).reshape(D // rows, rows, D)
    g_so = g_self[...].reshape(D // rows, rows, D)
    for tt in range(2):
        for cc in range(2):
            lanes = slice(cc * HALF, (cc + 1) * HALF)
            side = g_out if tt == 0 else g_so
            for out, same in ((keep, True), (send, False)):
                @pl.when((c == cc) == same)
                def _():
                    out[t ^ tt, :, :, :HALF] = g_gate[:, tt, :, lanes]
                    out[t ^ tt, :, :, HALF:] = side[:, :, lanes]


def cross_back(index, at, owner, valid, q, kv, dm, logs, dq, dkv, bias):
    bias[...] = cross_bias(owner, valid)
    pairs = q.shape[1] // 128
    first = (at[C] ^ index) * (pairs // 2)

    @pl.loop(0, pairs // 2)
    def _(i):
        p = first + i
        b = bias[...]
        k, v = kv[:, lanes_at(p)], kv[:, lanes_at(pairs + p)]
        qq, dd = two_heads(q[:, lanes_at(p)]), two_heads(dm[:, lanes_at(p)])
        scores = nt(qq * SCALE, k) + jnp.concatenate([b, b], 0)
        weight = jnp.exp(scores - logs[p])
        dp = nt(dd, v)
        ds = (weight * (dp - jnp.sum(weight * dp, -1, keepdims=True))).astype(BF)
        dq[:, lanes_at(i)] = (one_pair(mm(ds, k)) * SCALE).astype(BF)
        dkv[0, :, lanes_at(i)] = (tn(ds, qq) * SCALE).astype(BF)
        dkv[1, :, lanes_at(i)] = tn(weight.astype(BF), dd).astype(BF)


def cross_weights(at, text_normed, normed, dq, dkv, own, oth, q):
    t0 = at[T] == 0

    @pl.loop(0, 3)
    def _(j):
        lanes = pl.ds(pl.multiple_of(j * 256, 256), 256)
        x = text_normed[:, lanes]
        k, v = tn(x, dkv[0]).astype(BF), tn(x, dkv[1]).astype(BF)
        own[lanes] = jnp.where(t0, k, v)
        oth[lanes] = jnp.where(t0, v, k)
        q[lanes] = tn(normed[:, lanes], dq[...]).astype(BF)


def text_back(at, text, gains, w_kv, own, oth, grad, sums):
    c = at[C]
    d = nt(own[0], w_kv[:, half(c)])
    d = d + nt(oth[0], w_kv[:, half(1 - c)])
    d = d + nt(own[1], w_kv[:, pl.ds(pl.multiple_of(D + c * HALF, 128), HALF)])
    d = d + nt(oth[1], w_kv[:, pl.ds(pl.multiple_of(D + (1 - c) * HALF, 128), HALF)])
    normal, factor = stats(text[...].astype(F32))
    dx, gain, bias = norm_back(d, normal, factor, gain_of(gains, 1))
    grad[...] = dx

    @pl.when(pl.program_id(0) == 0)
    def _():
        sums[...] = jnp.zeros_like(sums)

    sums[0:1] += gain
    sums[1:2] += bias


def visual_back(at, d_normed, dq_own, dq_oth, w_q, visual, d_joined, gains, s1, s2, s3, grad, norms):
    c = at[C]
    depth = norms.shape[0]
    size = 4 * D // (2 * depth)
    d = d_normed[...] + nt(dq_own[...], w_q[:, half(c)]) + nt(dq_oth[...], w_q[:, half(1 - c)])
    normal, factor = stats(visual[...].astype(F32))
    dx, gain, bias = norm_back(d, normal, factor, gain_of(gains, 0))
    grad[...] = d_joined[...] + dx
    g = jnp.concatenate([gain, s1[0:1], s2[0:1], s3[0:1]], 1)
    b = jnp.concatenate([bias, s1[1:2], s2[1:2], s3[1:2]], 1)
    row = lax.broadcasted_iota(jnp.int32, (8, size), 0)
    norms[...] = jnp.zeros_like(norms)
    for s in range(2 * depth):
        lanes = slice(s * size, (s + 1) * size)
        v = jnp.where(row == 0, jnp.broadcast_to(g[:, lanes], (8, size)), jnp.broadcast_to(b[:, lanes], (8, size)))
        norms[s // 2, s % 2, :, :size] = jnp.where(row < 2, v, 0.0).astype(BF)


def finish_ab(at, r, ry, rc, ryc, g_query, g_keyval, gains, biases):
    t, c = at[T], at[C]
    rows, size = g_query.shape[0], gains.shape[0]
    for a, b, cc in ((r, ry, c), (rc, ryc, 1 - c)):
        g_keyval[:, pl.ds(pl.multiple_of(t * D + cc * HALF, 128), HALF)] = a[:rows, :HALF].astype(F32)
        g_keyval[:, pl.ds(pl.multiple_of((1 - t) * D + cc * HALF, 128), HALF)] = b[:rows, :HALF].astype(F32)
        g_query[:, half(cc)] = a[:rows, HALF:].astype(F32) + b[:rows, HALF:].astype(F32)
    norms = [a[rows:, :size].astype(F32) for a in (r, ry, rc, ryc)]
    norms = norms[0] + norms[1] + norms[2] + norms[3]
    gains[...] = norms[0:1].reshape(size)
    biases[...] = norms[1:2].reshape(size)


def in_order(at, groups, lanes):
    c0, t0 = at[C] == 0, at[T] == 0
    own, y, core, both = [r[:, lanes].astype(F32) for r in groups]
    a0, a1 = jnp.where(c0, own, core), jnp.where(c0, core, own)
    b0, b1 = jnp.where(c0, y, both), jnp.where(c0, both, y)
    return jnp.where(t0, a0, b0), jnp.where(t0, a1, b1), jnp.where(t0, b0, a0), jnp.where(t0, b1, a1)


def finish_cd(at, r, ry, rc, ryc, g_qkv, g_up, g_down):
    groups = (r, ry, rc, ryc)
    rows = g_qkv.shape[0]
    p = in_order(at, groups, slice(0, D))
    for i in range(4):
        g_down[i * rows : (i + 1) * rows] = p[i]
    for s in range(D // rows):
        p = in_order(at, groups, slice(D + s * rows, D + (s + 1) * rows))
        g_up[:, s * 4 * rows : (s + 1) * 4 * rows] = jnp.concatenate(p, 1)
    for i in range(3):
        p = in_order(at, groups, slice(2 * D + i * QUART, 2 * D + (i + 1) * QUART))
        g_qkv[:, i * D : (i + 1) * D] = jnp.concatenate(p, 1)


def finish_b(at, r, ry, rc, ryc, g_out, g_gate, g_self):
    groups = (r, ry, rc, ryc)
    rows = g_out.shape[0]
    p = in_order(at, groups, slice(0, HALF))
    for i in range(4):
        g_gate[(i // 2) * rows : (i // 2 + 1) * rows, (i % 2) * HALF : (i % 2 + 1) * HALF] = p[i]
    p = in_order(at, groups, slice(HALF, D))
    g_out[...] = jnp.concatenate(p[:2], 1)
    g_self[...] = jnp.concatenate(p[2:], 1)


def reduce_x(count, extra, lanes, at, *refs):
    out = refs[-1]
    m = extra[0] if extra else 0
    for z in range(out.shape[0]):
        out[z] = reduced(refs, count, m, lanes, z, 1 - at[X]).astype(BF)


def reduced(refs, count, m, lanes, z, side):
    acc = refs[0][z, side, :, lanes].astype(F32)
    for r in refs[1:count]:
        acc = acc + r[z, side, :, lanes].astype(F32)
    if m:
        y = refs[count]
        y = (y[z, side] if len(y.shape) == 4 else y[z]).astype(F32)
        acc = acc + y if y.shape == acc.shape else jnp.concatenate([acc[:, :m] + y, acc[:, m:]], 1)
    return acc


def reduce_z(count, extra, lanes, at, *refs):
    got, keep, send = refs[-3:]
    m = extra[0] if extra else 0
    for i in range(keep.shape[0]):
        for k, out in ((2 * i, keep), (2 * i + 1, send)):
            z = at[Z] ^ k
            out[i] = (reduced(refs, count, m, lanes, z, at[X]) + got[z].astype(F32)).astype(BF)


def reduce_x_proj(at, own, oth, norms, out):
    rows = own.shape[2]
    for z in range(out.shape[0]):
        out[z, :rows] = reduced((own, oth), 1, oth.shape[-1], slice(None), z, 1 - at[X]).astype(BF)
        out[z, rows:] = norms[z, 1 - at[X]]


def reduce_z_proj(at, own, oth, norms, got, keep, send):
    rows = own.shape[2]
    for i in range(keep.shape[0]):
        for k, out in ((2 * i, keep), (2 * i + 1, send)):
            z = at[Z] ^ k
            b = got[z].astype(F32)
            out[i, :rows] = (reduced((own, oth), 1, oth.shape[-1], slice(None), z, at[X]) + b[:rows]).astype(BF)
            out[i, rows:] = (norms[z, at[X]].astype(F32) + b[rows:]).astype(BF)


def reduce_more(at, keep, got, *outs):
    for i in range(keep.shape[0]):
        v = (keep[i].astype(F32) + got[i].astype(F32)).astype(BF)
        if len(outs) == 1:
            outs[0][...] = v
        else:
            outs[i % 2][i // 2] = v


def reduce_last(count, at, *refs):
    out = refs[-1]
    at_lane = 0
    for keep, got in zip(refs[0 : 2 * count : 2], refs[1 : 2 * count : 2]):
        rows, n = keep.shape[1:]
        out[:rows, at_lane : at_lane + n] = (keep[0].astype(F32) + got[0].astype(F32)).astype(BF)
        at_lane += n


def add_core_b(at, keep, came, own, oth_send, oth_keep):
    x = at[X]
    for z in range(own.shape[0]):
        for i in range(2):
            own[z, i] = (keep[0, z, i].astype(F32) + came[0, z, i].astype(F32)).astype(BF)
        oth_send[z] = (keep[1, z, 1 - x].astype(F32) + came[1, z, 1 - x].astype(F32)).astype(BF)
        oth_keep[z] = (keep[1, z, x].astype(F32) + came[1, z, x].astype(F32)).astype(BF)


def add_core_a(at, *refs):
    for keep, came, out in zip(refs[:3], refs[3:6], refs[6:]):
        out[...] = (keep[...].astype(F32) + came[...].astype(F32)).astype(BF)


def add_out(at, carried, y0, came, out):
    out[...] = (carried[...] + y0[...] + came[...].astype(F32)).astype(BF)


def local(reps, shards, visual, text, visual_valid, block_owner, cross_query, cross_keyval, cross_output, gate_weight,
          self_qkv, self_output, ffn_up, ffn_down, norm_gains, norm_biases, cotangent):
    ln = Links(reps, shards)
    at = ln.at
    od = Order()
    run = od.run
    visual, text, cotangent = visual[0], text[0], cotangent[0]
    rows, size = cross_query.shape[0], norm_gains.shape[0]
    vis, txt = visual.shape[0], text.shape[0]
    depth = shards // 2
    w3 = WIDE
    whole = lambda shape: pl.BlockSpec(shape, lambda *_: (0,) * len(shape))
    page = sds((vis, D), F32)
    grid4 = lambda n: (depth, 2, rows, n)

    def far_first(part):
        pieces = {0: part}
        for k in range(depth - 1, 0, -1):
            if k & (k - 1) == 0:
                pieces[k] = od.start(ln.along, part, k)
        return pieces

    def passed_on(pieces):
        for k in sorted(range(1, depth), key=lambda k: (bin(k).count("1"), -k)):
            if k not in pieces:
                od.wait(*[pieces[i] for i in sorted(pieces) if i])
                pieces[k] = od.start(ln.along, pieces[k & (k - 1)], k & -k)
        return [pieces[k] for k in range(depth)]

    (part_a,) = run(pack_a, [sds((rows + 16, D))], at, cross_query, cross_keyval, norm_gains, norm_biases, name="pack_a", far=True)
    pieces_a = far_first(part_a)
    part_b, part_c, part_d, cot = run(
        pack_rest, [sds((rows, D)), sds((rows, w3)), sds((rows, 2 * D)), sds((vis + 8, D))], at,
        cross_output, gate_weight, self_qkv, self_output, ffn_up, ffn_down, cotangent, visual_valid,
        name="pack_rest", far=True)
    d_xo, cot_y = ln.across(part_d), ln.y(cot)
    pieces_a = passed_on(pieces_a)
    od.wait(d_xo, cot_y)
    kv_m, qn_m = run(column_a, [sds((depth, rows, HALF)), sds((depth, rows + 16, HALF))], at, *pieces_a, name="column_a")
    kv_o, qn_o, kv_ym = ln.across(kv_m), ln.across(qn_m), ln.y(kv_m)
    pieces_b = passed_on(far_first(part_b))
    od.wait(kv_o)
    kv_yo = ln.y(kv_o)
    pieces_c = far_first(part_c)
    (b_m,) = run(column, [sds((depth, rows, D))], at, *pieces_b, name="column_b")
    joined_a, gains, biases = run(
        join_a, [sds((3,) + grid4(HALF)), sds((1, 4 * D), F32), sds((1, 4 * D), F32)],
        at, kv_m, kv_o, kv_ym, kv_yo, qn_m, qn_o, name="join_a")
    joined_a = joined_a.reshape(3, D, HALF)
    came_a = ln.core(joined_a)
    b_o, b_ym = od.start(ln.across, b_m), od.start(ln.y, b_m)
    tile = txt // 5
    row_tile = pl.BlockSpec((tile, D), lambda i: (i, 0))
    text_normed, normed = run(
        normed_kernel, [sds((txt, D)), sds((vis, D))], at, text, visual, gains, biases,
        grid=(5,), in_specs=[row_tile, whole((vis, D)), whole((1, 4 * D)), whole((1, 4 * D))],
        out_specs=[row_tile, whole((vis, D))], name="normed", vmem=12)
    pieces_c = passed_on(pieces_c)
    od.wait(came_a)
    pieces_d = far_first(part_d)

    kv, w_kv, w_q, queries = run(
        keyval_kernel, [sds((txt, 2 * D)), sds((D, 2 * D)), sds((D, D)), sds((vis, D))],
        at, text_normed, normed, joined_a, came_a,
        grid=(5,), in_specs=[row_tile, whole((vis, D)), whole((3, D, HALF)), whole((3, D, HALF))],
        out_specs=[pl.BlockSpec((tile, 2 * D), lambda i: (i, 0)), whole((D, 2 * D)), whole((D, D)), whole((vis, D))],
        name="keyval", vmem=30)
    (c_m,) = run(column, [sds((depth, rows, w3))], at, *pieces_c, name="column_c")
    od.wait(b_o, b_ym)
    c_o, b_yo = od.start(ln.across, c_m), od.start(ln.y, b_o)
    pairs = H // 2
    mixed, logs = run(
        cross_fwd, [sds((vis, D)), sds((pairs, 2 * vis, 1), F32)],
        at, block_owner, visual_valid, queries, kv,
        in_specs=[VM, VM, VM, PIN], scratch=[sds((vis, txt), F32)], name="cross_fwd", vmem=16)
    od.wait(*[pieces_d[k] for k in sorted(pieces_d) if k])
    d_x = {0: d_xo}
    for k in sorted(pieces_d):
        if k:
            d_x[k] = od.start(ln.across, pieces_d[k])
    pieces_d = passed_on(pieces_d)
    (wc_own,) = run(join, [sds(grid4(w3))], at, c_m, c_o, name="join_c")
    wc_oth = ln.core(wc_own)
    (joined_b,) = run(join_b, [sds((2,) + grid4(D))], at, b_m, b_o, b_ym, b_yo, name="join_b")
    joined_b = joined_b.reshape(2, shards, rows, D)
    came_b = ln.core(joined_b)
    w_out, w_self, w_gate = run(
        place_b, [sds((shards, rows, D)), sds((shards, rows, D)), sds((shards, 2, rows, D))], at, joined_b, came_b, name="place_b")
    w_out, w_self, w_gate = w_out.reshape(D, D), w_self.reshape(D, D), w_gate.reshape(2 * D, D)
    od.wait(wc_oth)
    wc_own, wc_oth = wc_own.reshape(D, w3), wc_oth.reshape(D, w3)
    cross, gate, joined, second = run(
        gate_kernel, [sds((vis, D)), page, page, sds((vis, D))],
        at, mixed, normed, visual, gains, biases, w_out, w_gate, name="gate")
    second_y = ln.y(second)
    d_u, d_d = run(column_halves, [sds((depth, rows, D))] * 2, at, *pieces_d, name="column_d")
    d_cu, d_cd = ln.core(d_u), ln.core(d_d)
    od.wait(*[d_x[k] for k in d_x])
    triple, att_mine, att_send = run(
        self_fwd, [sds((2 * vis, 3 * HALF)), sds((vis, HALF)), sds((vis, HALF))],
        at, second, second_y, cot, cot_y, wc_own, wc_oth, name="self_fwd", cost=3)
    att_came = ln.y(att_send)
    d_cx = {k: od.start(ln.core, d_x[k]) for k in d_x}
    for k in range(depth):
        if k not in d_x:
            d_x[k] = od.start(ln.across, pieces_d[k])
    od.wait(d_cu, d_cd)
    attended, carried, third = run(
        carry_kernel, [sds((vis, D)), page, sds((vis, D))],
        at, att_mine, att_came, joined, gains, biases, w_self, name="carry", cost=3)
    third_y = ln.y(third)
    (wd_own,) = run(join_pieces, [sds(grid4(2 * D))], at, d_u, d_d, *[d_x[k] for k in range(depth)], name="join_d")
    od.wait(third_y)
    for k in range(depth):
        if k not in d_cx:
            d_cx[k] = od.start(ln.core, d_x[k])
    (wd_oth,) = run(join_pieces, [sds(grid4(2 * D))], at, d_cu, d_cd, *[d_cx[k] for k in range(depth)], name="join_d")
    wd_own, wd_oth = wd_own.reshape(D, 2 * D), wd_oth.reshape(D, 2 * D)

    y0, y1, d0, d1, gu_oth, gd_oth = run(
        functools.partial(ffn_kernel, False), [page] * 4 + [sds((D, D))] * 2,
        at, third, third_y, cot, cot_y, wd_oth, name="ffn_first")
    gd_came, gu_came = [ln.core(g).reshape(grid4(D)) for g in (gd_oth, gu_oth)]
    y0, y1, d0, d1, gu_own, gd_own = run(
        functools.partial(ffn_kernel, True), [page, sds((vis, D))] * 2 + [sds((D, D))] * 2,
        at, third, third_y, cot, cot_y, wd_own, y0, y1, d0, d1, name="ffn_second")
    gd_own, gu_own = gd_own.reshape(grid4(D)), gu_own.reshape(grid4(D))
    d1_came = ln.y(d1)

    class Sum:
        def __init__(self, name, arrays, n, lanes=slice(None), sends=(), keeps=(), norms=None):
            self.name, self.n, self.rows = name, n, arrays[0].shape[2]
            extra = [a.shape[-1] for a in keeps]
            first, self.second = [functools.partial(f, len(arrays), extra, lanes) for f in (reduce_x, reduce_z)]
            self.late = list(arrays) + list(keeps)
            early = list(arrays) + list(sends)
            if norms is not None:
                first, self.second, self.rows = reduce_x_proj, reduce_z_proj, self.rows + norms.shape[2]
                self.late, early = self.late + [norms], early + [norms]
            (self.send,) = run(first, [sds((depth, self.rows, n))], at, *early, name="reduce_x_" + name)
            self.bit = 0

        def go(self):
            self.got = od.start(ln.across, self.send)
            return self

        def step(self):
            if self.bit == 0:
                outs = [sds((depth // 2, self.rows, self.n))] * 2
                self.keep, send = run(self.second, outs, at, *self.late, self.got, name="reduce_z_" + self.name)
                self.bit = 1
            elif self.keep.shape[0] > 1:
                outs = [sds((self.keep.shape[0] // 2, self.rows, self.n))] * 2
                self.keep, send = run(reduce_more, outs, at, self.keep, self.got, name="reduce_m_" + self.name)
                self.bit *= 2
            else:
                return False
            self.got = ln.along(send, self.bit)
            return True

    def finish(*sums):
        for one in sums:
            while one.keep.shape[0] > 1:
                one.step()
        ins = [a for one in sums for a in (one.keep, one.got)]
        (total,) = run(functools.partial(reduce_last, len(sums)), [sds((sums[0].rows, sum(one.n for one in sums)))], at,
                       *ins, name="reduce_last")
        for bit in range(2, reps.bit_length() - 1):
            total = (total.astype(F32) + ln.rep_bit(total, 1 << bit).astype(F32)).astype(BF)
        ry = ln.y(total)
        return total, ry, ln.core(total), ln.core(ry)

    def back_half(index):
        return run(
            functools.partial(cross_back, index), [sds((vis, HALF)), sds((2, txt, HALF))],
            at, block_owner, visual_valid, queries, kv, d_mixed, logs,
            in_specs=[VM, VM, VM, PIN, VM, VM], scratch=[sds((vis, txt), F32)], name="cross_back", vmem=20)

    def weights_half(dq, dkv):
        return run(cross_weights, [sds((D, HALF))] * 3, at, text_normed, normed, dq, dkv, name="cross_weights")

    down = Sum("down", [gd_own, gd_came], D).go()
    d_carried, da_mine, da_send, g_self, sums3 = run(
        carry_back, [page, sds((vis, HALF)), sds((vis, HALF)), sds((D, D)), sds((2, D), F32)],
        at, d0, d1_came, carried, cotangent, attended, gains, w_self, name="carry_back")
    da_came = ln.y(da_send)
    up = Sum("up", [gu_own, gu_came], D)
    od.wait(da_came)
    down.step()
    up.go()
    ds0, ds1, gc_own, gc_oth = run(
        self_back, [page, sds((vis, D)), sds(grid4(w3)), sds(grid4(w3))],
        at, triple, da_mine, da_came, cot, cot_y, second, second_y, wc_own, wc_oth,
        scratch=[sds((2 * vis, 3 * HALF))], name="self_back")
    ds1_came = ln.y(ds1)
    gc_came = ln.core(gc_oth)
    down.step()
    up.step()
    d_joined, d_mixed, d_normed, b_keep, b_send, sums2 = run(
        gate_back, [page, sds((vis, D)), page, sds((2, shards, rows, D)), sds((2, shards, rows, D)), sds((2, D), F32)],
        at, d_carried, ds0, ds1_came, joined, normed, cross, gate, mixed, gains, w_gate, w_out, g_self, name="gate_back")
    b_came = ln.core(b_send)
    y1_came = od.start(ln.y, y1)
    dq_oth, dkv_oth = back_half(1)
    qkv = Sum("qkv", [gc_own, gc_came], w3).go()
    od.wait(y1_came, down.got)
    own_b, b_ys, b_yk = run(
        add_core_b, [sds(grid4(D)), sds((depth, rows, D)), sds((depth, rows, D))], at,
        b_keep.reshape((2,) + grid4(D)), b_came.reshape((2,) + grid4(D)), name="add_core_b")
    b_ys = ln.y(b_ys)
    a_came = [ln.core(a) for a in weights_half(dq_oth, dkv_oth)]
    dq_own, dkv_own = back_half(0)
    up.step()
    gates = Sum("gate", [own_b], D, sends=[b_ys], keeps=[b_yk]).go()
    qkv.step()
    a_keep = weights_half(dq_own, dkv_own)
    own_a, a_y, own_q = run(
        add_core_a, [sds(grid4(HALF))] * 3, at,
        *[a.reshape(grid4(HALF)) for a in (*a_keep, *a_came)], name="add_core_a")
    a_y = ln.y(a_y)
    query = Sum("query", [own_q], HALF).go()
    row3 = pl.BlockSpec((2, tile, HALF), lambda i: (0, i, 0))
    grad_text, sums1 = run(
        text_back, [sds((txt, D), F32), sds((2, D), F32)],
        at, text, gains, w_kv, dkv_own, dkv_oth,
        grid=(5,), in_specs=[row_tile, whole((1, 4 * D)), whole((D, 2 * D)), row3, row3],
        out_specs=[row_tile, whole((2, D))], name="text_back", vmem=24)
    od.wait(up.got, gates.got)
    qkv.step()
    query.step()
    grad_visual, norms = run(
        visual_back, [page, sds((depth, 2, 8, HALF))],
        at, d_normed, dq_own, dq_oth, w_q, visual, d_joined, gains, sums1, sums2, sums3, name="visual_back")
    keyval = Sum("keyval", [own_a], HALF, sends=[a_y], keeps=[a_y], norms=norms).go()
    gates.late[1] = od.start(ln.y, b_yk)
    (layer_out,) = run(add_out, [sds((vis, D))], at, carried, y0, y1_came, name="add_out")
    query.step()
    keyval.step()
    first = finish(down, up, qkv)
    od.wait(query.got)
    keyval.step()
    gates.step()
    out = lambda r, n: sds((r, n), F32)
    last_a = finish(keyval, query)
    gates.step()
    g_qkv, g_up, g_down = run(
        finish_cd, [out(rows, 3 * D), out(rows, 4 * D), out(4 * rows, D)], at, *first, name="finish_cd")
    last_b = finish(gates)
    g_query, g_keyval, g_gains, g_biases = run(
        finish_ab, [out(rows, D), out(rows, 2 * D), sds((size,), F32), sds((size,), F32)], at, *last_a, name="finish_a")
    g_out, g_gate, g_self_out = run(
        finish_b, [out(rows, D), out(2 * rows, D), out(rows, D)], at, *last_b, name="finish_b")
    return (layer_out[None], grad_visual[None], grad_text[None], g_query, g_keyval, g_out, g_gate, g_qkv, g_self_out,
            g_up, g_down, g_gains, g_biases)


def solution(mesh):
    pages = P(("rep", "fsdp"), None, None)
    flags = P(("rep", "fsdp"), None)
    matrix = P("fsdp", None)
    vector = P("fsdp")
    in_specs = (pages, pages, flags, flags) + (matrix,) * 8 + (vector, vector, pages)
    out_specs = (pages, pages, pages) + (matrix,) * 8 + (vector, vector)
    reps, shards = mesh.shape["rep"], mesh.shape["fsdp"]

    def program(*args):
        return local(reps, shards, *args)

    return jax.shard_map(program, mesh=mesh, in_specs=in_specs, out_specs=out_specs, check_vma=False)
```

```python
import functools

import jax
import jax.numpy as jnp
from jax import lax
from jax.experimental import pallas as pl
from jax.experimental.pallas import tpu as pltpu
from jax.sharding import PartitionSpec as P

H = 12
HD = 64
D = H * HD
HALF = D // 2
QUART = D // 4
WIDE = -(-3 * QUART // 128) * 128
BF = jnp.bfloat16
F32 = jnp.float32

epsilon = 1e-05
filtered_logits = -1000000000.0
shared_sheet_reward = 6.0
SCALE = HD ** (-0.5)
VM = pl.BlockSpec()
SM = pl.BlockSpec(memory_space=pltpu.SMEM)
ANY = pl.BlockSpec(memory_space=pl.ANY)
PIN = pl.BlockSpec(memory_space=pltpu.VMEM)


def sds(shape, dtype=BF):
    return jax.ShapeDtypeStruct(tuple(shape), dtype)


def size_of(a):
    n = jnp.dtype(a.dtype).itemsize
    for d in a.shape:
        n *= d
    return n


class Order:
    def __init__(self):
        self.tokens = []

    def start(self, exchange, a, *args):
        a, *self.tokens = lax.optimization_barrier((a, *self.tokens))
        return exchange(a, *args)

    def wait(self, *arrays):
        self.tokens = self.tokens + list(arrays)

    def run(self, body, outs, where, *ins, name=None, scratch=(), grid=None, in_specs=None, out_specs=None, vmem=None, prefetch=False, far=False, cost=0):
        moved = sum(size_of(a) for a in ins) + sum(size_of(o) for o in outs)
        held = moved + sum(size_of(s) for s in scratch)
        limit = 66_000_000 if far else vmem << 20 if vmem else min(60 << 20, int(1.25 * held) + (10 << 20))
        ins_specs = ([VM] * len(ins) if in_specs is None else in_specs) + [ANY] * len(self.tokens)
        spec = dict(in_specs=([] if prefetch else [SM]) + ins_specs,
                    out_specs=([VM] * len(outs) if out_specs is None else out_specs) + [pl.BlockSpec((8, 128), lambda *_: (0, 0)) if grid else VM],
                    scratch_shapes=[pltpu.VMEM(s.shape, s.dtype) for s in scratch])
        if prefetch:
            spec = dict(grid_spec=pltpu.PrefetchScalarGridSpec(num_scalar_prefetch=1, grid=grid, **spec))
        elif grid is not None:
            spec["grid"] = grid
        kernel, count, late = body, len(ins), len(self.tokens)
        if far:
            spec["in_specs"] = [SM] + [pl.BlockSpec(memory_space=pltpu.HBM)] * count + [ANY] * late
            spec["scratch_shapes"] = [pltpu.VMEM(a.shape, a.dtype) for a in ins] + [pltpu.SemaphoreType.DMA((count,))]

            def kernel(at, *refs):
                held, sems = refs[-1 - count : -1], refs[-1]
                copies = [pltpu.make_async_copy(refs[i], held[i], sems.at[i]) for i in range(count)]
                for one in copies:
                    one.start()
                for one in copies:
                    one.wait()
                body(at, *held, *refs[count : -1 - count])

        ends = count + late + len(outs)

        def marked(at, *refs):
            refs[ends][...] = jnp.zeros((8, 128), F32)
            kernel(at, *refs[:count], *refs[count + late : ends], *refs[ends + 1 :])

        *got, mark = pl.pallas_call(
            marked,
            out_shape=list(outs) + [sds((8, 128), F32)],
            compiler_params=pltpu.CompilerParams(vmem_limit_bytes=limit),
            cost_estimate=pl.CostEstimate(flops=cost * 1_150_000_000, bytes_accessed=1024, transcendentals=0),
            name=name,
            **spec,
        )(where, *ins, *self.tokens)
        self.tokens = [mark]
        return got


T, C, X, Z = 0, 1, 2, 3


class Links:
    def __init__(self, reps, shards):
        self.reps, self.shards = reps, shards
        self.depth = shards // 2
        rank = lax.axis_index("rep")
        shard = lax.axis_index("fsdp")
        self.shard = shard
        self.at = jnp.stack([(rank // 2) % 2, rank % 2, shard % 2, shard // 2]).astype(jnp.int32)

    def core(self, a):
        return lax.ppermute(a, "rep", [(r, r ^ 1) for r in range(self.reps)])

    def y(self, a):
        return lax.ppermute(a, "rep", [(r, r ^ 2) for r in range(self.reps)])

    def rep_bit(self, a, bit):
        return lax.ppermute(a, "rep", [(r, r ^ bit) for r in range(self.reps)])

    def across(self, a):
        return lax.ppermute(a, "fsdp", [(s, s ^ 1) for s in range(self.shards)])

    def along(self, a, k):
        return lax.ppermute(a, "fsdp", [(s, s ^ (2 * k)) for s in range(self.shards)])


def mm(a, b):
    return jnp.dot(a, b, preferred_element_type=F32)


def nt(a, b):
    return lax.dot_general(a, b, (((1,), (1,)), ((), ())), preferred_element_type=F32)


def tn(a, b):
    return lax.dot_general(a, b, (((0,), (0,)), ((), ())), preferred_element_type=F32)


def stats(rows):
    mean = jnp.mean(rows, -1, keepdims=True)
    centred = rows - mean
    factor = lax.rsqrt(jnp.mean(centred * centred, -1, keepdims=True) + epsilon)
    return centred * factor, factor


def norm_back(grad, normal, factor, gain):
    scaled = grad * gain
    dx = scaled - jnp.mean(scaled, -1, keepdims=True) - normal * jnp.mean(scaled * normal, -1, keepdims=True)
    return dx * factor, jnp.sum(grad * normal, 0, keepdims=True), jnp.sum(grad, 0, keepdims=True)


def gain_of(ref, i):
    return ref[:, i * D : (i + 1) * D]


def half(i):
    return pl.ds(pl.multiple_of(i * HALF, 128), HALF)


def pair_masks(rows):
    lane = lax.broadcasted_iota(jnp.int32, (rows, 128), 1)
    return lane < HD


def two_heads(a):
    first = pair_masks(a.shape[0])
    zero = jnp.zeros_like(a)
    return jnp.concatenate([jnp.where(first, a, zero), jnp.where(first, zero, a)], 0)


def one_pair(a):
    n = a.shape[0] // 2
    return jnp.where(pair_masks(n), a[:n], a[n:])


def softmax(scores):
    peak = jnp.max(scores, -1, keepdims=True)
    expo = jnp.exp(scores - peak)
    total = jnp.sum(expo, -1, keepdims=True)
    return expo * (1.0 / total), peak + jnp.log(total)


def pack_a(at, query, keyval, gains, biases, part):
    rows, size = query.shape[0], gains.shape[0]
    part[:rows, :HALF] = keyval[:, pl.ds(pl.multiple_of(at[T] * D + at[C] * HALF, 128), HALF)]
    part[:rows, HALF:] = query[:, half(at[C])]
    part[rows:, :] = jnp.zeros((16, D), BF)
    g, b = gains[...].reshape(1, size), biases[...].reshape(1, size)
    g_hi, b_hi = g.astype(BF), b.astype(BF)
    g_lo, b_lo = (g - g_hi.astype(F32)).astype(BF), (b - b_hi.astype(F32)).astype(BF)
    row = lax.broadcasted_iota(jnp.int32, (16, size), 0)
    out = jnp.zeros((16, size), F32)
    for i, v in enumerate((g_hi, g_lo, b_hi, b_lo)):
        out = jnp.where(row == i, jnp.broadcast_to(v.astype(F32), (16, size)), out)
    part[rows:, HALF : HALF + size] = out.astype(BF)


def pack_rest(at, output, gate, qkv, self_out, up, down, cot, valid, part_b, part_c, part_d, page):
    rows = output.shape[0]
    n = cot.shape[0]
    page[:n] = cot[...]
    page[n:, :n] = jnp.broadcast_to(valid[...], (8, n)).astype(F32).astype(BF)
    page[n:, n:] = jnp.zeros((8, D - n), BF)
    shards = D // rows
    t0, c0 = at[T] == 0, at[C] == 0
    gate_c, out_c, self_c = gate[:, half(at[C])], output[:, half(at[C])], self_out[:, half(at[C])]
    part_b[:, :HALF] = jnp.where(t0, gate_c[:rows], gate_c[rows:])
    part_b[:, HALF:D] = jnp.where(t0, out_c, self_c)
    pieces = []
    for i in range(3):
        v = qkv[:, pl.ds(pl.multiple_of(i * D + at[T] * HALF, 128), HALF)]
        pieces.append(jnp.where(c0, v[:, :QUART], v[:, QUART:]))
    part_c[...] = jnp.concatenate(pieces + [jnp.zeros((rows, WIDE - 3 * QUART), BF)], 1)
    pieces = []
    for s in range(shards):
        v = [up[:, (s * 4 + g) * rows : (s * 4 + g + 1) * rows] for g in range(4)]
        pieces.append(jnp.where(t0, jnp.where(c0, v[0], v[1]), jnp.where(c0, v[2], v[3])))
    part_d[:, :D] = jnp.concatenate(pieces, 1)
    v = [down[g * rows : (g + 1) * rows, :] for g in range(4)]
    part_d[:, D:] = jnp.where(t0, jnp.where(c0, v[0], v[1]), jnp.where(c0, v[2], v[3]))


def column(at, *refs):
    for k, piece in enumerate(refs[:-1]):
        refs[-1][at[Z] ^ k] = piece[...]


def column_a(at, *refs):
    kv, qn = refs[-2:]
    rows = kv.shape[1]
    for k, piece in enumerate(refs[:-2]):
        kv[at[Z] ^ k] = piece[:rows, :HALF]
        qn[at[Z] ^ k] = piece[:, HALF:]


def column_halves(at, *refs):
    up, down = refs[-2:]
    for k, piece in enumerate(refs[:-2]):
        up[at[Z] ^ k] = piece[:, :D]
        down[at[Z] ^ k] = piece[:, D:]


def join_pieces(at, up, down, *refs):
    out = refs[-1]
    for z in range(up.shape[0]):
        out[z, at[X], :, :D] = up[z]
        out[z, at[X], :, D:] = down[z]
    for k, piece in enumerate(refs[:-1]):
        out[at[Z] ^ k, 1 - at[X]] = piece[...]


def join(at, mine, other, out):
    for src, side in ((mine, at[X]), (other, 1 - at[X])):
        for z in range(mine.shape[0]):
            out[z, side] = src[z]


def join_b(at, mine, other, y_mine, y_other, out):
    for i, pair in enumerate(((mine, other), (y_mine, y_other))):
        for src, side in zip(pair, (at[X], 1 - at[X])):
            for z in range(src.shape[0]):
                out[i, z, side] = src[z]


def join_a(at, kvm, kvo, kym, kyo, qm, qo, out, gains, biases):
    _three, depth, _two, rows, _n = out.shape
    size = 4 * D // (2 * depth)
    for i, pair in enumerate(((kvm, kvo), (kym, kyo), (qm, qo))):
        for src, side in zip(pair, (at[X], 1 - at[X])):
            for z in range(depth):
                out[i, z, side] = src[z, :rows]
    first = at[X] == 0
    for z in range(depth):
        a, b = qm[z, rows:, :size].astype(F32), qo[z, rows:, :size].astype(F32)
        for i, v in enumerate((jnp.where(first, a, b), jnp.where(first, b, a))):
            s = (z * 2 + i) * size
            gains[:, s : s + size] = v[0:1] + v[1:2]
            biases[:, s : s + size] = v[2:3] + v[3:4]


def place_b(at, own, came, cross_out, self_out, gate):
    t, c = at[T], at[C]
    for src, cc in ((own, c), (came, 1 - c)):
        for i in range(2):
            gate[:, t ^ i, :, half(cc)] = src[i, :, :, :HALF]
        cross_out[:, :, half(cc)] = src[t, :, :, HALF:]
        self_out[:, :, half(cc)] = src[1 - t, :, :, HALF:]


def normed_kernel(at, text, visual, gains, biases, text_normed, normed):
    normal, _f = stats(text[...].astype(F32))
    text_normed[...] = (normal * gain_of(gains, 1) + gain_of(biases, 1)).astype(BF)
    normal, _f = stats(visual[...].astype(F32))
    normed[...] = (normal * gain_of(gains, 0) + gain_of(biases, 0)).astype(BF)


def keyval_kernel(at, text_normed, normed, own, came, kv, w_kv, w_q, queries):
    t, c = at[T], at[C]

    @pl.when(pl.program_id(0) == 0)
    def _():
        for src, cc in ((own, c), (came, 1 - c)):
            for i in range(2):
                w_kv[:, pl.ds(pl.multiple_of((t ^ i) * D + cc * HALF, 128), HALF)] = src[i]
            w_q[:, half(cc)] = src[2]
        queries[...] = mm(normed[...], w_q[...]).astype(BF)

    kv[...] = mm(text_normed[...], w_kv[...]).astype(BF)


def cross_bias(owner, valid):
    n, m = valid.shape[1], owner.shape[1]
    parent = owner[...] == lax.broadcasted_iota(jnp.int32, (n, m), 0)
    ones = jnp.where(parent, 1.0, 0.0).astype(BF)
    real = jnp.broadcast_to(valid[...].astype(F32), (8, n)).astype(BF)
    present = mm(real, ones)[0:1] > 0.5
    return jnp.where(parent, shared_sheet_reward, 0.0) + jnp.where(present, 0.0, filtered_logits)


def lanes_at(i):
    return pl.ds(pl.multiple_of(i * 128, 128), 128)


def cross_fwd(at, owner, valid, q, kv, out, logs, bias):
    bias[...] = cross_bias(owner, valid)
    pairs = q.shape[1] // 128

    @pl.loop(0, pairs)
    def _(p):
        b = bias[...]
        k, v = kv[:, lanes_at(p)], kv[:, lanes_at(pairs + p)]
        scores = nt(two_heads(q[:, lanes_at(p)] * SCALE), k) + jnp.concatenate([b, b], 0)
        weight, log = softmax(scores)
        logs[p] = log
        out[:, lanes_at(p)] = one_pair(mm(weight.astype(BF), v)).astype(BF)


def gate_kernel(at, mixed, normed, visual, gains, biases, w_out, w_gate, cross, gate, joined, second):
    rows = mm(mixed[...], w_out[...]).astype(BF)
    cross[...] = rows
    g = jax.nn.sigmoid(mm(normed[...], w_gate[:D]) + mm(rows, w_gate[D:]))
    gate[...] = g
    j = visual[...].astype(F32) + g * rows.astype(F32)
    joined[...] = j
    normal, _f = stats(j)
    second[...] = (normal * gain_of(gains, 2) + gain_of(biases, 2)).astype(BF)


def head_order(at, a):
    return jnp.where(at[C] == 0, a, jnp.concatenate([a[:, QUART:], a[:, :QUART]], 1))


def self_bias(page):
    n = page.shape[0] - 8
    return jnp.where(page[n : n + 8, :n].astype(F32)[0:1] > 0.5, 0.0, filtered_logits)


def self_fwd(at, second0, second1, valid0, valid1, w_own, w_oth, triple, att0, att1):
    n = second0.shape[0]
    rows = jnp.concatenate([second0[...], second1[...]], 0)
    own, oth = [mm(rows, w[...]).astype(BF) for w in (w_own, w_oth)]
    for i in range(3):
        triple[:, i * HALF : (i + 1) * HALF] = jnp.concatenate(
            [own[:, i * QUART : (i + 1) * QUART], oth[:, i * QUART : (i + 1) * QUART]], 1)
    for page, (valid, att) in enumerate(((valid0, att0), (valid1, att1))):
        bias = self_bias(valid)
        r = slice(page * n, (page + 1) * n)
        outs = []
        for p in range(3):
            q, k, v = [triple[r, i * HALF + p * 128 : i * HALF + (p + 1) * 128] for i in range(3)]
            weight, _l = softmax(nt(two_heads(q), k) * SCALE + bias)
            outs.append(one_pair(mm(weight.astype(BF), v)).astype(BF))
        att[...] = head_order(at, jnp.concatenate(outs, 1))


def carry_kernel(at, mine, came, joined, gains, biases, w, attended, carried, third):
    attended[:, half(at[T])] = mine[...]
    attended[:, half(1 - at[T])] = came[...]
    c = joined[...] + mm(attended[...], w[...])
    carried[...] = c
    normal, _f = stats(c)
    third[...] = (normal * gain_of(gains, 3) + gain_of(biases, 3)).astype(BF)


def ffn_kernel(last, at, third0, third1, cot0, cot1, w, *refs):
    n = third0.shape[0]
    if last:
        y0i, y1i, d0i, d1i, y0, y1, d0, d1, g_up, g_down = refs
    else:
        y0, y1, d0, d1, g_up, g_down = refs
    rows = jnp.concatenate([third0[...], third1[...]], 0)
    cot = jnp.concatenate([cot0[:n], cot1[:n]], 0)
    up, down = w[:, :D], w[:, D:]
    v = mm(rows, up)
    k = (2.0 / 3.141592653589793) ** 0.5
    th = jnp.tanh(k * (v + 0.044715 * (v * v * v)))
    act = (0.5 * v * (1.0 + th)).astype(BF)
    slope = 0.5 * (1.0 + th) + 0.5 * v * (1.0 - th * th) * (k * (1.0 + 3.0 * 0.044715 * (v * v)))
    y = mm(act, down)
    g_down[...] = tn(act, cot).astype(BF)
    dl = (nt(cot, down) * slope).astype(BF)
    d = nt(dl, up)
    g_up[...] = tn(rows, dl).astype(BF)
    if last:
        y0[...] = y[:n] + y0i[...]
        y1[...] = (y[n:] + y1i[...]).astype(BF)
        d0[...] = d[:n] + d0i[...]
        d1[...] = (d[n:] + d1i[...]).astype(BF)
    else:
        y0[...], y1[...], d0[...], d1[...] = y[:n], y[n:], d[:n], d[n:]


def carry_back(at, d0, came, carried, cot, attended, gains, w, d_carried, mine, send, grad, sums):
    normal, factor = stats(carried[...])
    dx, gain, bias = norm_back(d0[...] + came[...].astype(F32), normal, factor, gain_of(gains, 3))
    dc = cot[...].astype(F32) + dx
    d_carried[...] = dc
    low = dc.astype(BF)
    da = nt(low, w[...]).astype(BF)
    t0 = at[T] == 0
    mine[...] = head_order(at, jnp.where(t0, da[:, :HALF], da[:, HALF:]))
    send[...] = head_order(at, jnp.where(t0, da[:, HALF:], da[:, :HALF]))
    grad[...] = tn(attended[...], low).astype(BF)
    sums[0:1], sums[1:2] = gain, bias


def self_back(at, triple, da0, da1, valid0, valid1, second0, second1, w_own, w_oth, d0, d1, g_own, g_oth, dt):
    n = second0.shape[0]

    @pl.loop(0, 3)
    def _(p):
        lanes = [pl.ds(pl.multiple_of(i * HALF + p * 128, 128), 128) for i in range(3)]
        for page, (valid, da) in enumerate(((valid0, da0), (valid1, da1))):
            bias = self_bias(valid)
            r = slice(page * n, (page + 1) * n)
            q, k, v = [triple[r, lane] for lane in lanes]
            qq = two_heads(q)
            dd = two_heads(da[:, lanes[0]])
            weight, _l = softmax(nt(qq, k) * SCALE + bias)
            dp = nt(dd, v)
            ds = (weight * (dp - jnp.sum(weight * dp, -1, keepdims=True))).astype(BF)
            grads = (one_pair(mm(ds, k)) * SCALE, tn(ds, qq) * SCALE, tn(weight.astype(BF), dd))
            for i in range(3):
                dt[r, lanes[i]] = grads[i].astype(BF)

    none = jnp.zeros((2 * n, WIDE - 3 * QUART), BF)
    own = jnp.concatenate([dt[:, i * HALF : i * HALF + QUART] for i in range(3)] + [none], 1)
    oth = jnp.concatenate([dt[:, i * HALF + QUART : (i + 1) * HALF] for i in range(3)] + [none], 1)
    rows = jnp.concatenate([second0[...], second1[...]], 0)
    g_own[...] = tn(rows, own).astype(BF).reshape(g_own.shape)
    g_oth[...] = tn(rows, oth).astype(BF).reshape(g_oth.shape)
    d = nt(own, w_own[...]) + nt(oth, w_oth[...])
    d0[...] = d[:n]
    d1[...] = d[n:].astype(BF)


def gate_back(at, d_carried, d0, came, joined, normed, cross, gate, mixed, gains, w_gate, w_out, g_self,
              d_joined, d_mixed, d_normed, keep, send, sums):
    t, c = at[T], at[C]
    rows = keep.shape[2]
    normal, factor = stats(joined[...])
    dx, gain, bias = norm_back(d0[...] + came[...].astype(F32), normal, factor, gain_of(gains, 2))
    dj = d_carried[...] + dx
    d_joined[...] = dj
    sums[0:1], sums[1:2] = gain, bias
    g = gate[...]
    dg = (dj * cross[...].astype(F32) * g * (1.0 - g)).astype(BF)
    d_normed[...] = nt(dg, w_gate[:D])
    dc = (dj * g + nt(dg, w_gate[D:])).astype(BF)
    d_mixed[...] = nt(dc, w_out[...]).astype(BF)
    g_gate = jnp.concatenate([tn(normed[...], dg).astype(BF), tn(cross[...], dg).astype(BF)], 0)
    g_gate = g_gate.reshape(D // rows, 2, rows, D)
    g_out = tn(mixed[...], dc).astype(BF).reshape(D // rows, rows, D)
    g_so = g_self[...].reshape(D // rows, rows, D)
    for tt in range(2):
        for cc in range(2):
            lanes = slice(cc * HALF, (cc + 1) * HALF)
            side = g_out if tt == 0 else g_so
            for out, same in ((keep, True), (send, False)):
                @pl.when((c == cc) == same)
                def _():
                    out[t ^ tt, :, :, :HALF] = g_gate[:, tt, :, lanes]
                    out[t ^ tt, :, :, HALF:] = side[:, :, lanes]


def cross_back(index, at, owner, valid, q, kv, dm, logs, dq, dkv, bias):
    bias[...] = cross_bias(owner, valid)
    pairs = q.shape[1] // 128
    first = (at[C] ^ index) * (pairs // 2)

    @pl.loop(0, pairs // 2)
    def _(i):
        p = first + i
        b = bias[...]
        k, v = kv[:, lanes_at(p)], kv[:, lanes_at(pairs + p)]
        qq, dd = two_heads(q[:, lanes_at(p)]), two_heads(dm[:, lanes_at(p)])
        scores = nt(qq * SCALE, k) + jnp.concatenate([b, b], 0)
        weight = jnp.exp(scores - logs[p])
        dp = nt(dd, v)
        ds = (weight * (dp - jnp.sum(weight * dp, -1, keepdims=True))).astype(BF)
        dq[:, lanes_at(i)] = (one_pair(mm(ds, k)) * SCALE).astype(BF)
        dkv[0, :, lanes_at(i)] = (tn(ds, qq) * SCALE).astype(BF)
        dkv[1, :, lanes_at(i)] = tn(weight.astype(BF), dd).astype(BF)


def cross_weights(at, text_normed, normed, dq, dkv, own, oth, q):
    t0 = at[T] == 0

    @pl.loop(0, 3)
    def _(j):
        lanes = pl.ds(pl.multiple_of(j * 256, 256), 256)
        x = text_normed[:, lanes]
        k, v = tn(x, dkv[0]).astype(BF), tn(x, dkv[1]).astype(BF)
        own[lanes] = jnp.where(t0, k, v)
        oth[lanes] = jnp.where(t0, v, k)
        q[lanes] = tn(normed[:, lanes], dq[...]).astype(BF)


def text_back(at, text, gains, w_kv, own, oth, grad, sums):
    c = at[C]
    d = nt(own[0], w_kv[:, half(c)])
    d = d + nt(oth[0], w_kv[:, half(1 - c)])
    d = d + nt(own[1], w_kv[:, pl.ds(pl.multiple_of(D + c * HALF, 128), HALF)])
    d = d + nt(oth[1], w_kv[:, pl.ds(pl.multiple_of(D + (1 - c) * HALF, 128), HALF)])
    normal, factor = stats(text[...].astype(F32))
    dx, gain, bias = norm_back(d, normal, factor, gain_of(gains, 1))
    grad[...] = dx

    @pl.when(pl.program_id(0) == 0)
    def _():
        sums[...] = jnp.zeros_like(sums)

    sums[0:1] += gain
    sums[1:2] += bias


def visual_back(at, d_normed, dq_own, dq_oth, w_q, visual, d_joined, gains, s1, s2, s3, grad, norms):
    c = at[C]
    depth = norms.shape[0]
    size = 4 * D // (2 * depth)
    d = d_normed[...] + nt(dq_own[...], w_q[:, half(c)]) + nt(dq_oth[...], w_q[:, half(1 - c)])
    normal, factor = stats(visual[...].astype(F32))
    dx, gain, bias = norm_back(d, normal, factor, gain_of(gains, 0))
    grad[...] = d_joined[...] + dx
    g = jnp.concatenate([gain, s1[0:1], s2[0:1], s3[0:1]], 1)
    b = jnp.concatenate([bias, s1[1:2], s2[1:2], s3[1:2]], 1)
    row = lax.broadcasted_iota(jnp.int32, (8, size), 0)
    norms[...] = jnp.zeros_like(norms)
    for s in range(2 * depth):
        lanes = slice(s * size, (s + 1) * size)
        v = jnp.where(row == 0, jnp.broadcast_to(g[:, lanes], (8, size)), jnp.broadcast_to(b[:, lanes], (8, size)))
        norms[s // 2, s % 2, :, :size] = jnp.where(row < 2, v, 0.0).astype(BF)


def finish_ab(at, r, ry, rc, ryc, g_query, g_keyval, gains, biases):
    t, c = at[T], at[C]
    rows, size = g_query.shape[0], gains.shape[0]
    for a, b, cc in ((r, ry, c), (rc, ryc, 1 - c)):
        g_keyval[:, pl.ds(pl.multiple_of(t * D + cc * HALF, 128), HALF)] = a[:rows, :HALF].astype(F32)
        g_keyval[:, pl.ds(pl.multiple_of((1 - t) * D + cc * HALF, 128), HALF)] = b[:rows, :HALF].astype(F32)
        g_query[:, half(cc)] = a[:rows, HALF:].astype(F32) + b[:rows, HALF:].astype(F32)
    norms = [a[rows:, :size].astype(F32) for a in (r, ry, rc, ryc)]
    norms = norms[0] + norms[1] + norms[2] + norms[3]
    gains[...] = norms[0:1].reshape(size)
    biases[...] = norms[1:2].reshape(size)


def in_order(at, groups, lanes):
    c0, t0 = at[C] == 0, at[T] == 0
    own, y, core, both = [r[:, lanes].astype(F32) for r in groups]
    a0, a1 = jnp.where(c0, own, core), jnp.where(c0, core, own)
    b0, b1 = jnp.where(c0, y, both), jnp.where(c0, both, y)
    return jnp.where(t0, a0, b0), jnp.where(t0, a1, b1), jnp.where(t0, b0, a0), jnp.where(t0, b1, a1)


def finish_cd(at, r, ry, rc, ryc, g_qkv, g_up, g_down):
    groups = (r, ry, rc, ryc)
    rows = g_qkv.shape[0]
    p = in_order(at, groups, slice(0, D))
    for i in range(4):
        g_down[i * rows : (i + 1) * rows] = p[i]
    for s in range(D // rows):
        p = in_order(at, groups, slice(D + s * rows, D + (s + 1) * rows))
        g_up[:, s * 4 * rows : (s + 1) * 4 * rows] = jnp.concatenate(p, 1)
    for i in range(3):
        p = in_order(at, groups, slice(2 * D + i * QUART, 2 * D + (i + 1) * QUART))
        g_qkv[:, i * D : (i + 1) * D] = jnp.concatenate(p, 1)


def finish_b(at, r, ry, rc, ryc, g_out, g_gate, g_self):
    groups = (r, ry, rc, ryc)
    rows = g_out.shape[0]
    p = in_order(at, groups, slice(0, HALF))
    for i in range(4):
        g_gate[(i // 2) * rows : (i // 2 + 1) * rows, (i % 2) * HALF : (i % 2 + 1) * HALF] = p[i]
    p = in_order(at, groups, slice(HALF, D))
    g_out[...] = jnp.concatenate(p[:2], 1)
    g_self[...] = jnp.concatenate(p[2:], 1)


def reduce_x(count, extra, lanes, at, *refs):
    out = refs[-1]
    m = extra[0] if extra else 0
    for z in range(out.shape[0]):
        out[z] = reduced(refs, count, m, lanes, z, 1 - at[X]).astype(BF)


def reduced(refs, count, m, lanes, z, side):
    acc = refs[0][z, side, :, lanes].astype(F32)
    for r in refs[1:count]:
        acc = acc + r[z, side, :, lanes].astype(F32)
    if m:
        y = refs[count]
        y = (y[z, side] if len(y.shape) == 4 else y[z]).astype(F32)
        acc = acc + y if y.shape == acc.shape else jnp.concatenate([acc[:, :m] + y, acc[:, m:]], 1)
    return acc


def reduce_z(count, extra, lanes, at, *refs):
    got, keep, send = refs[-3:]
    m = extra[0] if extra else 0
    for i in range(keep.shape[0]):
        for k, out in ((2 * i, keep), (2 * i + 1, send)):
            z = at[Z] ^ k
            out[i] = (reduced(refs, count, m, lanes, z, at[X]) + got[z].astype(F32)).astype(BF)


def reduce_x_proj(at, own, oth, norms, out):
    rows = own.shape[2]
    for z in range(out.shape[0]):
        out[z, :rows] = reduced((own, oth), 1, oth.shape[-1], slice(None), z, 1 - at[X]).astype(BF)
        out[z, rows:] = norms[z, 1 - at[X]]


def reduce_z_proj(at, own, oth, norms, got, keep, send):
    rows = own.shape[2]
    for i in range(keep.shape[0]):
        for k, out in ((2 * i, keep), (2 * i + 1, send)):
            z = at[Z] ^ k
            b = got[z].astype(F32)
            out[i, :rows] = (reduced((own, oth), 1, oth.shape[-1], slice(None), z, at[X]) + b[:rows]).astype(BF)
            out[i, rows:] = (norms[z, at[X]].astype(F32) + b[rows:]).astype(BF)


def reduce_more(at, keep, got, *outs):
    for i in range(keep.shape[0]):
        v = (keep[i].astype(F32) + got[i].astype(F32)).astype(BF)
        if len(outs) == 1:
            outs[0][...] = v
        else:
            outs[i % 2][i // 2] = v


def reduce_last(count, at, *refs):
    out = refs[-1]
    at_lane = 0
    for keep, got in zip(refs[0 : 2 * count : 2], refs[1 : 2 * count : 2]):
        rows, n = keep.shape[1:]
        out[:rows, at_lane : at_lane + n] = (keep[0].astype(F32) + got[0].astype(F32)).astype(BF)
        at_lane += n


def add_core_b(at, keep, came, own, oth_send, oth_keep):
    x = at[X]
    for z in range(own.shape[0]):
        for i in range(2):
            own[z, i] = (keep[0, z, i].astype(F32) + came[0, z, i].astype(F32)).astype(BF)
        oth_send[z] = (keep[1, z, 1 - x].astype(F32) + came[1, z, 1 - x].astype(F32)).astype(BF)
        oth_keep[z] = (keep[1, z, x].astype(F32) + came[1, z, x].astype(F32)).astype(BF)


def add_core_a(at, *refs):
    for keep, came, out in zip(refs[:3], refs[3:6], refs[6:]):
        out[...] = (keep[...].astype(F32) + came[...].astype(F32)).astype(BF)


def add_out(at, carried, y0, came, out):
    out[...] = (carried[...] + y0[...] + came[...].astype(F32)).astype(BF)


def local(reps, shards, visual, text, visual_valid, block_owner, cross_query, cross_keyval, cross_output, gate_weight,
          self_qkv, self_output, ffn_up, ffn_down, norm_gains, norm_biases, cotangent):
    ln = Links(reps, shards)
    at = ln.at
    od = Order()
    run = od.run
    visual, text, cotangent = visual[0], text[0], cotangent[0]
    rows, size = cross_query.shape[0], norm_gains.shape[0]
    vis, txt = visual.shape[0], text.shape[0]
    depth = shards // 2
    w3 = WIDE
    whole = lambda shape: pl.BlockSpec(shape, lambda *_: (0,) * len(shape))
    page = sds((vis, D), F32)
    grid4 = lambda n: (depth, 2, rows, n)

    def far_first(part):
        pieces = {0: part}
        for k in range(depth - 1, 0, -1):
            if k & (k - 1) == 0:
                pieces[k] = od.start(ln.along, part, k)
        return pieces

    def passed_on(pieces):
        for k in sorted(range(1, depth), key=lambda k: (bin(k).count("1"), -k)):
            if k not in pieces:
                od.wait(*[pieces[i] for i in sorted(pieces) if i])
                pieces[k] = od.start(ln.along, pieces[k & (k - 1)], k & -k)
        return [pieces[k] for k in range(depth)]

    (part_a,) = run(pack_a, [sds((rows + 16, D))], at, cross_query, cross_keyval, norm_gains, norm_biases, name="pack_a", far=True)
    pieces_a = far_first(part_a)
    part_b, part_c, part_d, cot = run(
        pack_rest, [sds((rows, D)), sds((rows, w3)), sds((rows, 2 * D)), sds((vis + 8, D))], at,
        cross_output, gate_weight, self_qkv, self_output, ffn_up, ffn_down, cotangent, visual_valid,
        name="pack_rest", far=True)
    d_xo, cot_y = ln.across(part_d), ln.y(cot)
    pieces_a = passed_on(pieces_a)
    od.wait(d_xo, cot_y)
    kv_m, qn_m = run(column_a, [sds((depth, rows, HALF)), sds((depth, rows + 16, HALF))], at, *pieces_a, name="column_a")
    kv_o, qn_o, kv_ym = ln.across(kv_m), ln.across(qn_m), ln.y(kv_m)
    pieces_b = passed_on(far_first(part_b))
    od.wait(kv_o)
    kv_yo = ln.y(kv_o)
    pieces_c = far_first(part_c)
    (b_m,) = run(column, [sds((depth, rows, D))], at, *pieces_b, name="column_b")
    joined_a, gains, biases = run(
        join_a, [sds((3,) + grid4(HALF)), sds((1, 4 * D), F32), sds((1, 4 * D), F32)],
        at, kv_m, kv_o, kv_ym, kv_yo, qn_m, qn_o, name="join_a")
    joined_a = joined_a.reshape(3, D, HALF)
    came_a = ln.core(joined_a)
    b_o, b_ym = od.start(ln.across, b_m), od.start(ln.y, b_m)
    tile = txt // 5
    row_tile = pl.BlockSpec((tile, D), lambda i: (i, 0))
    text_normed, normed = run(
        normed_kernel, [sds((txt, D)), sds((vis, D))], at, text, visual, gains, biases,
        grid=(5,), in_specs=[row_tile, whole((vis, D)), whole((1, 4 * D)), whole((1, 4 * D))],
        out_specs=[row_tile, whole((vis, D))], name="normed", vmem=12)
    pieces_c = passed_on(pieces_c)
    od.wait(came_a)
    pieces_d = far_first(part_d)

    kv, w_kv, w_q, queries = run(
        keyval_kernel, [sds((txt, 2 * D)), sds((D, 2 * D)), sds((D, D)), sds((vis, D))],
        at, text_normed, normed, joined_a, came_a,
        grid=(5,), in_specs=[row_tile, whole((vis, D)), whole((3, D, HALF)), whole((3, D, HALF))],
        out_specs=[pl.BlockSpec((tile, 2 * D), lambda i: (i, 0)), whole((D, 2 * D)), whole((D, D)), whole((vis, D))],
        name="keyval", vmem=30)
    (c_m,) = run(column, [sds((depth, rows, w3))], at, *pieces_c, name="column_c")
    od.wait(b_o, b_ym)
    c_o, b_yo = od.start(ln.across, c_m), od.start(ln.y, b_o)
    pairs = H // 2
    mixed, logs = run(
        cross_fwd, [sds((vis, D)), sds((pairs, 2 * vis, 1), F32)],
        at, block_owner, visual_valid, queries, kv,
        in_specs=[VM, VM, VM, PIN], scratch=[sds((vis, txt), F32)], name="cross_fwd", vmem=16)
    od.wait(*[pieces_d[k] for k in sorted(pieces_d) if k])
    d_x = {0: d_xo}
    for k in sorted(pieces_d):
        if k:
            d_x[k] = od.start(ln.across, pieces_d[k])
    pieces_d = passed_on(pieces_d)
    (wc_own,) = run(join, [sds(grid4(w3))], at, c_m, c_o, name="join_c")
    wc_oth = ln.core(wc_own)
    (joined_b,) = run(join_b, [sds((2,) + grid4(D))], at, b_m, b_o, b_ym, b_yo, name="join_b")
    joined_b = joined_b.reshape(2, shards, rows, D)
    came_b = ln.core(joined_b)
    w_out, w_self, w_gate = run(
        place_b, [sds((shards, rows, D)), sds((shards, rows, D)), sds((shards, 2, rows, D))], at, joined_b, came_b, name="place_b")
    w_out, w_self, w_gate = w_out.reshape(D, D), w_self.reshape(D, D), w_gate.reshape(2 * D, D)
    od.wait(wc_oth)
    wc_own, wc_oth = wc_own.reshape(D, w3), wc_oth.reshape(D, w3)
    cross, gate, joined, second = run(
        gate_kernel, [sds((vis, D)), page, page, sds((vis, D))],
        at, mixed, normed, visual, gains, biases, w_out, w_gate, name="gate")
    second_y = ln.y(second)
    d_u, d_d = run(column_halves, [sds((depth, rows, D))] * 2, at, *pieces_d, name="column_d")
    d_cu, d_cd = ln.core(d_u), ln.core(d_d)
    od.wait(*[d_x[k] for k in d_x])
    triple, att_mine, att_send = run(
        self_fwd, [sds((2 * vis, 3 * HALF)), sds((vis, HALF)), sds((vis, HALF))],
        at, second, second_y, cot, cot_y, wc_own, wc_oth, name="self_fwd", cost=3)
    att_came = ln.y(att_send)
    d_cx = {k: od.start(ln.core, d_x[k]) for k in d_x}
    for k in range(depth):
        if k not in d_x:
            d_x[k] = od.start(ln.across, pieces_d[k])
    od.wait(d_cu, d_cd)
    attended, carried, third = run(
        carry_kernel, [sds((vis, D)), page, sds((vis, D))],
        at, att_mine, att_came, joined, gains, biases, w_self, name="carry", cost=3)
    third_y = ln.y(third)
    (wd_own,) = run(join_pieces, [sds(grid4(2 * D))], at, d_u, d_d, *[d_x[k] for k in range(depth)], name="join_d")
    od.wait(third_y)
    for k in range(depth):
        if k not in d_cx:
            d_cx[k] = od.start(ln.core, d_x[k])
    (wd_oth,) = run(join_pieces, [sds(grid4(2 * D))], at, d_cu, d_cd, *[d_cx[k] for k in range(depth)], name="join_d")
    wd_own, wd_oth = wd_own.reshape(D, 2 * D), wd_oth.reshape(D, 2 * D)

    y0, y1, d0, d1, gu_oth, gd_oth = run(
        functools.partial(ffn_kernel, False), [page] * 4 + [sds((D, D))] * 2,
        at, third, third_y, cot, cot_y, wd_oth, name="ffn_first")
    gd_came, gu_came = [ln.core(g).reshape(grid4(D)) for g in (gd_oth, gu_oth)]
    y0, y1, d0, d1, gu_own, gd_own = run(
        functools.partial(ffn_kernel, True), [page, sds((vis, D))] * 2 + [sds((D, D))] * 2,
        at, third, third_y, cot, cot_y, wd_own, y0, y1, d0, d1, name="ffn_second")
    gd_own, gu_own = gd_own.reshape(grid4(D)), gu_own.reshape(grid4(D))
    d1_came = ln.y(d1)

    class Sum:
        def __init__(self, name, arrays, n, lanes=slice(None), sends=(), keeps=(), norms=None):
            self.name, self.n, self.rows = name, n, arrays[0].shape[2]
            extra = [a.shape[-1] for a in keeps]
            first, self.second = [functools.partial(f, len(arrays), extra, lanes) for f in (reduce_x, reduce_z)]
            self.late = list(arrays) + list(keeps)
            early = list(arrays) + list(sends)
            if norms is not None:
                first, self.second, self.rows = reduce_x_proj, reduce_z_proj, self.rows + norms.shape[2]
                self.late, early = self.late + [norms], early + [norms]
            (self.send,) = run(first, [sds((depth, self.rows, n))], at, *early, name="reduce_x_" + name)
            self.bit = 0

        def go(self):
            self.got = od.start(ln.across, self.send)
            return self

        def step(self):
            if self.bit == 0:
                outs = [sds((depth // 2, self.rows, self.n))] * 2
                self.keep, send = run(self.second, outs, at, *self.late, self.got, name="reduce_z_" + self.name)
                self.bit = 1
            elif self.keep.shape[0] > 1:
                outs = [sds((self.keep.shape[0] // 2, self.rows, self.n))] * 2
                self.keep, send = run(reduce_more, outs, at, self.keep, self.got, name="reduce_m_" + self.name)
                self.bit *= 2
            else:
                return False
            self.got = ln.along(send, self.bit)
            return True

    def finish(*sums):
        for one in sums:
            while one.keep.shape[0] > 1:
                one.step()
        ins = [a for one in sums for a in (one.keep, one.got)]
        (total,) = run(functools.partial(reduce_last, len(sums)), [sds((sums[0].rows, sum(one.n for one in sums)))], at,
                       *ins, name="reduce_last")
        for bit in range(2, reps.bit_length() - 1):
            total = (total.astype(F32) + ln.rep_bit(total, 1 << bit).astype(F32)).astype(BF)
        ry = ln.y(total)
        return total, ry, ln.core(total), ln.core(ry)

    def back_half(index):
        return run(
            functools.partial(cross_back, index), [sds((vis, HALF)), sds((2, txt, HALF))],
            at, block_owner, visual_valid, queries, kv, d_mixed, logs,
            in_specs=[VM, VM, VM, PIN, VM, VM], scratch=[sds((vis, txt), F32)], name="cross_back", vmem=20)

    def weights_half(dq, dkv):
        return run(cross_weights, [sds((D, HALF))] * 3, at, text_normed, normed, dq, dkv, name="cross_weights")

    down = Sum("down", [gd_own, gd_came], D).go()
    d_carried, da_mine, da_send, g_self, sums3 = run(
        carry_back, [page, sds((vis, HALF)), sds((vis, HALF)), sds((D, D)), sds((2, D), F32)],
        at, d0, d1_came, carried, cotangent, attended, gains, w_self, name="carry_back")
    da_came = ln.y(da_send)
    up = Sum("up", [gu_own, gu_came], D)
    od.wait(da_came)
    down.step()
    up.go()
    ds0, ds1, gc_own, gc_oth = run(
        self_back, [page, sds((vis, D)), sds(grid4(w3)), sds(grid4(w3))],
        at, triple, da_mine, da_came, cot, cot_y, second, second_y, wc_own, wc_oth,
        scratch=[sds((2 * vis, 3 * HALF))], name="self_back")
    ds1_came = ln.y(ds1)
    gc_came = ln.core(gc_oth)
    down.step()
    up.step()
    d_joined, d_mixed, d_normed, b_keep, b_send, sums2 = run(
        gate_back, [page, sds((vis, D)), page, sds((2, shards, rows, D)), sds((2, shards, rows, D)), sds((2, D), F32)],
        at, d_carried, ds0, ds1_came, joined, normed, cross, gate, mixed, gains, w_gate, w_out, g_self, name="gate_back")
    b_came = ln.core(b_send)
    y1_came = od.start(ln.y, y1)
    dq_oth, dkv_oth = back_half(1)
    qkv = Sum("qkv", [gc_own, gc_came], w3).go()
    od.wait(y1_came)
    own_b, b_ys, b_yk = run(
        add_core_b, [sds(grid4(D)), sds((depth, rows, D)), sds((depth, rows, D))], at,
        b_keep.reshape((2,) + grid4(D)), b_came.reshape((2,) + grid4(D)), name="add_core_b")
    b_ys = ln.y(b_ys)
    od.wait(down.got)
    a_came = [ln.core(a) for a in weights_half(dq_oth, dkv_oth)]
    dq_own, dkv_own = back_half(0)
    up.step()
    gates = Sum("gate", [own_b], D, sends=[b_ys], keeps=[b_yk]).go()
    a_keep = weights_half(dq_own, dkv_own)
    qkv.step()
    own_a, a_y, own_q = run(
        add_core_a, [sds(grid4(HALF))] * 3, at,
        *[a.reshape(grid4(HALF)) for a in (*a_keep, *a_came)], name="add_core_a")
    a_y = ln.y(a_y)
    query = Sum("query", [own_q], HALF).go()
    row3 = pl.BlockSpec((2, tile, HALF), lambda i: (0, i, 0))
    grad_text, sums1 = run(
        text_back, [sds((txt, D), F32), sds((2, D), F32)],
        at, text, gains, w_kv, dkv_own, dkv_oth,
        grid=(5,), in_specs=[row_tile, whole((1, 4 * D)), whole((D, 2 * D)), row3, row3],
        out_specs=[row_tile, whole((2, D))], name="text_back", vmem=24)
    od.wait(up.got, gates.got)
    qkv.step()
    query.step()
    grad_visual, norms = run(
        visual_back, [page, sds((depth, 2, 8, HALF))],
        at, d_normed, dq_own, dq_oth, w_q, visual, d_joined, gains, sums1, sums2, sums3, name="visual_back")
    keyval = Sum("keyval", [own_a], HALF, sends=[a_y], keeps=[a_y], norms=norms).go()
    gates.late[1] = od.start(ln.y, b_yk)
    (layer_out,) = run(add_out, [sds((vis, D))], at, carried, y0, y1_came, name="add_out")
    query.step()
    keyval.step()
    first = finish(down, up, qkv)
    od.wait(query.got)
    keyval.step()
    gates.step()
    out = lambda r, n: sds((r, n), F32)
    last_a = finish(keyval, query)
    gates.step()
    g_qkv, g_up, g_down = run(
        finish_cd, [out(rows, 3 * D), out(rows, 4 * D), out(4 * rows, D)], at, *first, name="finish_cd")
    last_b = finish(gates)
    g_query, g_keyval, g_gains, g_biases = run(
        finish_ab, [out(rows, D), out(rows, 2 * D), sds((size,), F32), sds((size,), F32)], at, *last_a, name="finish_a")
    g_out, g_gate, g_self_out = run(
        finish_b, [out(rows, D), out(2 * rows, D), out(rows, D)], at, *last_b, name="finish_b")
    return (layer_out[None], grad_visual[None], grad_text[None], g_query, g_keyval, g_out, g_gate, g_qkv, g_self_out,
            g_up, g_down, g_gains, g_biases)


def solution(mesh):
    pages = P(("rep", "fsdp"), None, None)
    flags = P(("rep", "fsdp"), None)
    matrix = P("fsdp", None)
    vector = P("fsdp")
    in_specs = (pages, pages, flags, flags) + (matrix,) * 8 + (vector, vector, pages)
    out_specs = (pages, pages, pages) + (matrix,) * 8 + (vector, vector)
    reps, shards = mesh.shape["rep"], mesh.shape["fsdp"]

    def program(*args):
        return local(reps, shards, *args)

    return jax.shard_map(program, mesh=mesh, in_specs=in_specs, out_specs=out_specs, check_vma=False)
```

```python
import functools

import jax
import jax.numpy as jnp
from jax import lax
from jax.experimental import pallas as pl
from jax.experimental.pallas import tpu as pltpu
from jax.sharding import PartitionSpec as P

H = 12
HD = 64
D = H * HD
HALF = D // 2
QUART = D // 4
WIDE = -(-3 * QUART // 128) * 128
BF = jnp.bfloat16
F32 = jnp.float32

epsilon = 1e-05
filtered_logits = -1000000000.0
shared_sheet_reward = 6.0
SCALE = HD ** (-0.5)
VM = pl.BlockSpec()
SM = pl.BlockSpec(memory_space=pltpu.SMEM)
ANY = pl.BlockSpec(memory_space=pl.ANY)
PIN = pl.BlockSpec(memory_space=pltpu.VMEM)


def sds(shape, dtype=BF):
    return jax.ShapeDtypeStruct(tuple(shape), dtype)


def size_of(a):
    n = jnp.dtype(a.dtype).itemsize
    for d in a.shape:
        n *= d
    return n


class Order:
    def __init__(self):
        self.tokens = []

    def start(self, exchange, a, *args):
        a, *self.tokens = lax.optimization_barrier((a, *self.tokens))
        return exchange(a, *args)

    def wait(self, *arrays):
        self.tokens = self.tokens + list(arrays)

    def run(self, body, outs, where, *ins, name=None, scratch=(), grid=None, in_specs=None, out_specs=None, vmem=None, prefetch=False, far=False, cost=0):
        moved = sum(size_of(a) for a in ins) + sum(size_of(o) for o in outs)
        held = moved + sum(size_of(s) for s in scratch)
        limit = 66_000_000 if far else vmem << 20 if vmem else min(60 << 20, int(1.25 * held) + (10 << 20))
        ins_specs = ([VM] * len(ins) if in_specs is None else in_specs) + [ANY] * len(self.tokens)
        spec = dict(in_specs=([] if prefetch else [SM]) + ins_specs,
                    out_specs=([VM] * len(outs) if out_specs is None else out_specs) + [pl.BlockSpec((8, 128), lambda *_: (0, 0)) if grid else VM],
                    scratch_shapes=[pltpu.VMEM(s.shape, s.dtype) for s in scratch])
        if prefetch:
            spec = dict(grid_spec=pltpu.PrefetchScalarGridSpec(num_scalar_prefetch=1, grid=grid, **spec))
        elif grid is not None:
            spec["grid"] = grid
        kernel, count, late = body, len(ins), len(self.tokens)
        if far:
            spec["in_specs"] = [SM] + [pl.BlockSpec(memory_space=pltpu.HBM)] * count + [ANY] * late
            spec["scratch_shapes"] = [pltpu.VMEM(a.shape, a.dtype) for a in ins] + [pltpu.SemaphoreType.DMA((count,))]

            def kernel(at, *refs):
                held, sems = refs[-1 - count : -1], refs[-1]
                copies = [pltpu.make_async_copy(refs[i], held[i], sems.at[i]) for i in range(count)]
                for one in copies:
                    one.start()
                for one in copies:
                    one.wait()
                body(at, *held, *refs[count : -1 - count])

        ends = count + late + len(outs)

        def marked(at, *refs):
            refs[ends][...] = jnp.zeros((8, 128), F32)
            kernel(at, *refs[:count], *refs[count + late : ends], *refs[ends + 1 :])

        *got, mark = pl.pallas_call(
            marked,
            out_shape=list(outs) + [sds((8, 128), F32)],
            compiler_params=pltpu.CompilerParams(vmem_limit_bytes=limit),
            cost_estimate=pl.CostEstimate(flops=cost * 1_150_000_000, bytes_accessed=1024, transcendentals=0),
            name=name,
            **spec,
        )(where, *ins, *self.tokens)
        self.tokens = [mark]
        return got


T, C, X, Z = 0, 1, 2, 3


class Links:
    def __init__(self, reps, shards):
        self.reps, self.shards = reps, shards
        self.depth = shards // 2
        rank = lax.axis_index("rep")
        shard = lax.axis_index("fsdp")
        self.shard = shard
        self.at = jnp.stack([(rank // 2) % 2, rank % 2, shard % 2, shard // 2]).astype(jnp.int32)

    def core(self, a):
        return lax.ppermute(a, "rep", [(r, r ^ 1) for r in range(self.reps)])

    def y(self, a):
        return lax.ppermute(a, "rep", [(r, r ^ 2) for r in range(self.reps)])

    def rep_bit(self, a, bit):
        return lax.ppermute(a, "rep", [(r, r ^ bit) for r in range(self.reps)])

    def across(self, a):
        return lax.ppermute(a, "fsdp", [(s, s ^ 1) for s in range(self.shards)])

    def along(self, a, k):
        return lax.ppermute(a, "fsdp", [(s, s ^ (2 * k)) for s in range(self.shards)])


def mm(a, b):
    return jnp.dot(a, b, preferred_element_type=F32)


def nt(a, b):
    return lax.dot_general(a, b, (((1,), (1,)), ((), ())), preferred_element_type=F32)


def tn(a, b):
    return lax.dot_general(a, b, (((0,), (0,)), ((), ())), preferred_element_type=F32)


def stats(rows):
    mean = jnp.mean(rows, -1, keepdims=True)
    centred = rows - mean
    factor = lax.rsqrt(jnp.mean(centred * centred, -1, keepdims=True) + epsilon)
    return centred * factor, factor


def norm_back(grad, normal, factor, gain):
    scaled = grad * gain
    dx = scaled - jnp.mean(scaled, -1, keepdims=True) - normal * jnp.mean(scaled * normal, -1, keepdims=True)
    return dx * factor, jnp.sum(grad * normal, 0, keepdims=True), jnp.sum(grad, 0, keepdims=True)


def gain_of(ref, i):
    return ref[:, i * D : (i + 1) * D]


def half(i):
    return pl.ds(pl.multiple_of(i * HALF, 128), HALF)


def pair_masks(rows):
    lane = lax.broadcasted_iota(jnp.int32, (rows, 128), 1)
    return lane < HD


def two_heads(a):
    first = pair_masks(a.shape[0])
    zero = jnp.zeros_like(a)
    return jnp.concatenate([jnp.where(first, a, zero), jnp.where(first, zero, a)], 0)


def one_pair(a):
    n = a.shape[0] // 2
    return jnp.where(pair_masks(n), a[:n], a[n:])


def softmax(scores):
    peak = jnp.max(scores, -1, keepdims=True)
    expo = jnp.exp(scores - peak)
    total = jnp.sum(expo, -1, keepdims=True)
    return expo * (1.0 / total), peak + jnp.log(total)


def pack_a(at, query, keyval, gains, biases, part):
    rows, size = query.shape[0], gains.shape[0]
    part[:rows, :HALF] = keyval[:, pl.ds(pl.multiple_of(at[T] * D + at[C] * HALF, 128), HALF)]
    part[:rows, HALF:] = query[:, half(at[C])]
    part[rows:, :] = jnp.zeros((16, D), BF)
    g, b = gains[...].reshape(1, size), biases[...].reshape(1, size)
    g_hi, b_hi = g.astype(BF), b.astype(BF)
    g_lo, b_lo = (g - g_hi.astype(F32)).astype(BF), (b - b_hi.astype(F32)).astype(BF)
    row = lax.broadcasted_iota(jnp.int32, (16, size), 0)
    out = jnp.zeros((16, size), F32)
    for i, v in enumerate((g_hi, g_lo, b_hi, b_lo)):
        out = jnp.where(row == i, jnp.broadcast_to(v.astype(F32), (16, size)), out)
    part[rows:, HALF : HALF + size] = out.astype(BF)


def pack_rest(at, output, gate, qkv, self_out, up, down, cot, valid, part_b, part_c, part_d, page):
    rows = output.shape[0]
    n = cot.shape[0]
    page[:n] = cot[...]
    page[n:, :n] = jnp.broadcast_to(valid[...], (8, n)).astype(F32).astype(BF)
    page[n:, n:] = jnp.zeros((8, D - n), BF)
    shards = D // rows
    t0, c0 = at[T] == 0, at[C] == 0
    gate_c, out_c, self_c = gate[:, half(at[C])], output[:, half(at[C])], self_out[:, half(at[C])]
    part_b[:, :HALF] = jnp.where(t0, gate_c[:rows], gate_c[rows:])
    part_b[:, HALF:D] = jnp.where(t0, out_c, self_c)
    pieces = []
    for i in range(3):
        v = qkv[:, pl.ds(pl.multiple_of(i * D + at[T] * HALF, 128), HALF)]
        pieces.append(jnp.where(c0, v[:, :QUART], v[:, QUART:]))
    part_c[...] = jnp.concatenate(pieces + [jnp.zeros((rows, WIDE - 3 * QUART), BF)], 1)
    pieces = []
    for s in range(shards):
        v = [up[:, (s * 4 + g) * rows : (s * 4 + g + 1) * rows] for g in range(4)]
        pieces.append(jnp.where(t0, jnp.where(c0, v[0], v[1]), jnp.where(c0, v[2], v[3])))
    part_d[:, :D] = jnp.concatenate(pieces, 1)
    v = [down[g * rows : (g + 1) * rows, :] for g in range(4)]
    part_d[:, D:] = jnp.where(t0, jnp.where(c0, v[0], v[1]), jnp.where(c0, v[2], v[3]))


def column(at, *refs):
    for k, piece in enumerate(refs[:-1]):
        refs[-1][at[Z] ^ k] = piece[...]


def column_a(at, *refs):
    kv, qn = refs[-2:]
    rows = kv.shape[1]
    for k, piece in enumerate(refs[:-2]):
        kv[at[Z] ^ k] = piece[:rows, :HALF]
        qn[at[Z] ^ k] = piece[:, HALF:]


def column_halves(at, *refs):
    up, down = refs[-2:]
    for k, piece in enumerate(refs[:-2]):
        up[at[Z] ^ k] = piece[:, :D]
        down[at[Z] ^ k] = piece[:, D:]


def join_pieces(at, up, down, *refs):
    out = refs[-1]
    for z in range(up.shape[0]):
        out[z, at[X], :, :D] = up[z]
        out[z, at[X], :, D:] = down[z]
    for k, piece in enumerate(refs[:-1]):
        out[at[Z] ^ k, 1 - at[X]] = piece[...]


def join(at, mine, other, out):
    for src, side in ((mine, at[X]), (other, 1 - at[X])):
        for z in range(mine.shape[0]):
            out[z, side] = src[z]


def join_b(at, mine, other, y_mine, y_other, out):
    for i, pair in enumerate(((mine, other), (y_mine, y_other))):
        for src, side in zip(pair, (at[X], 1 - at[X])):
            for z in range(src.shape[0]):
                out[i, z, side] = src[z]


def join_a(at, kvm, kvo, kym, kyo, qm, qo, out, gains, biases):
    _three, depth, _two, rows, _n = out.shape
    size = 4 * D // (2 * depth)
    for i, pair in enumerate(((kvm, kvo), (kym, kyo), (qm, qo))):
        for src, side in zip(pair, (at[X], 1 - at[X])):
            for z in range(depth):
                out[i, z, side] = src[z, :rows]
    first = at[X] == 0
    for z in range(depth):
        a, b = qm[z, rows:, :size].astype(F32), qo[z, rows:, :size].astype(F32)
        for i, v in enumerate((jnp.where(first, a, b), jnp.where(first, b, a))):
            s = (z * 2 + i) * size
            gains[:, s : s + size] = v[0:1] + v[1:2]
            biases[:, s : s + size] = v[2:3] + v[3:4]


def place_b(at, own, came, cross_out, self_out, gate):
    t, c = at[T], at[C]
    for src, cc in ((own, c), (came, 1 - c)):
        for i in range(2):
            gate[:, t ^ i, :, half(cc)] = src[i, :, :, :HALF]
        cross_out[:, :, half(cc)] = src[t, :, :, HALF:]
        self_out[:, :, half(cc)] = src[1 - t, :, :, HALF:]


def normed_kernel(at, text, visual, gains, biases, text_normed, normed):
    normal, _f = stats(text[...].astype(F32))
    text_normed[...] = (normal * gain_of(gains, 1) + gain_of(biases, 1)).astype(BF)
    normal, _f = stats(visual[...].astype(F32))
    normed[...] = (normal * gain_of(gains, 0) + gain_of(biases, 0)).astype(BF)


def keyval_kernel(at, text_normed, normed, own, came, kv, w_kv, w_q, queries):
    t, c = at[T], at[C]

    @pl.when(pl.program_id(0) == 0)
    def _():
        for src, cc in ((own, c), (came, 1 - c)):
            for i in range(2):
                w_kv[:, pl.ds(pl.multiple_of((t ^ i) * D + cc * HALF, 128), HALF)] = src[i]
            w_q[:, half(cc)] = src[2]
        queries[...] = mm(normed[...], w_q[...]).astype(BF)

    kv[...] = mm(text_normed[...], w_kv[...]).astype(BF)


def cross_bias(owner, valid):
    n, m = valid.shape[1], owner.shape[1]
    parent = owner[...] == lax.broadcasted_iota(jnp.int32, (n, m), 0)
    ones = jnp.where(parent, 1.0, 0.0).astype(BF)
    real = jnp.broadcast_to(valid[...].astype(F32), (8, n)).astype(BF)
    present = mm(real, ones)[0:1] > 0.5
    return jnp.where(parent, shared_sheet_reward, 0.0) + jnp.where(present, 0.0, filtered_logits)


def lanes_at(i):
    return pl.ds(pl.multiple_of(i * 128, 128), 128)


def cross_fwd(at, owner, valid, q, kv, out, logs, bias):
    bias[...] = cross_bias(owner, valid)
    pairs = q.shape[1] // 128

    @pl.loop(0, pairs)
    def _(p):
        b = bias[...]
        k, v = kv[:, lanes_at(p)], kv[:, lanes_at(pairs + p)]
        scores = nt(two_heads(q[:, lanes_at(p)] * SCALE), k) + jnp.concatenate([b, b], 0)
        weight, log = softmax(scores)
        logs[p] = log
        out[:, lanes_at(p)] = one_pair(mm(weight.astype(BF), v)).astype(BF)


def gate_kernel(at, mixed, normed, visual, gains, biases, w_out, w_gate, cross, gate, joined, second):
    rows = mm(mixed[...], w_out[...]).astype(BF)
    cross[...] = rows
    g = jax.nn.sigmoid(mm(normed[...], w_gate[:D]) + mm(rows, w_gate[D:]))
    gate[...] = g
    j = visual[...].astype(F32) + g * rows.astype(F32)
    joined[...] = j
    normal, _f = stats(j)
    second[...] = (normal * gain_of(gains, 2) + gain_of(biases, 2)).astype(BF)


def head_order(at, a):
    return jnp.where(at[C] == 0, a, jnp.concatenate([a[:, QUART:], a[:, :QUART]], 1))


def self_bias(page):
    n = page.shape[0] - 8
    return jnp.where(page[n : n + 8, :n].astype(F32)[0:1] > 0.5, 0.0, filtered_logits)


def self_fwd(at, second0, second1, valid0, valid1, w_own, w_oth, triple, att0, att1):
    n = second0.shape[0]
    rows = jnp.concatenate([second0[...], second1[...]], 0)
    own, oth = [mm(rows, w[...]).astype(BF) for w in (w_own, w_oth)]
    for i in range(3):
        triple[:, i * HALF : (i + 1) * HALF] = jnp.concatenate(
            [own[:, i * QUART : (i + 1) * QUART], oth[:, i * QUART : (i + 1) * QUART]], 1)
    for page, (valid, att) in enumerate(((valid0, att0), (valid1, att1))):
        bias = self_bias(valid)
        r = slice(page * n, (page + 1) * n)
        outs = []
        for p in range(3):
            q, k, v = [triple[r, i * HALF + p * 128 : i * HALF + (p + 1) * 128] for i in range(3)]
            weight, _l = softmax(nt(two_heads(q), k) * SCALE + bias)
            outs.append(one_pair(mm(weight.astype(BF), v)).astype(BF))
        att[...] = head_order(at, jnp.concatenate(outs, 1))


def carry_kernel(at, mine, came, joined, gains, biases, w, attended, carried, third):
    attended[:, half(at[T])] = mine[...]
    attended[:, half(1 - at[T])] = came[...]
    c = joined[...] + mm(attended[...], w[...])
    carried[...] = c
    normal, _f = stats(c)
    third[...] = (normal * gain_of(gains, 3) + gain_of(biases, 3)).astype(BF)


def ffn_kernel(last, at, third0, third1, cot0, cot1, w, *refs):
    n = third0.shape[0]
    if last:
        y0i, y1i, d0i, d1i, y0, y1, d0, d1, g_up, g_down = refs
    else:
        y0, y1, d0, d1, g_up, g_down = refs
    rows = jnp.concatenate([third0[...], third1[...]], 0)
    cot = jnp.concatenate([cot0[:n], cot1[:n]], 0)
    up, down = w[:, :D], w[:, D:]
    v = mm(rows, up)
    k = (2.0 / 3.141592653589793) ** 0.5
    th = jnp.tanh(k * (v + 0.044715 * (v * v * v)))
    act = (0.5 * v * (1.0 + th)).astype(BF)
    slope = 0.5 * (1.0 + th) + 0.5 * v * (1.0 - th * th) * (k * (1.0 + 3.0 * 0.044715 * (v * v)))
    y = mm(act, down)
    g_down[...] = tn(act, cot).astype(BF)
    dl = (nt(cot, down) * slope).astype(BF)
    d = nt(dl, up)
    g_up[...] = tn(rows, dl).astype(BF)
    if last:
        y0[...] = y[:n] + y0i[...]
        y1[...] = (y[n:] + y1i[...]).astype(BF)
        d0[...] = d[:n] + d0i[...]
        d1[...] = (d[n:] + d1i[...]).astype(BF)
    else:
        y0[...], y1[...], d0[...], d1[...] = y[:n], y[n:], d[:n], d[n:]


def carry_back(at, d0, came, carried, cot, attended, gains, w, d_carried, mine, send, grad, sums):
    normal, factor = stats(carried[...])
    dx, gain, bias = norm_back(d0[...] + came[...].astype(F32), normal, factor, gain_of(gains, 3))
    dc = cot[...].astype(F32) + dx
    d_carried[...] = dc
    low = dc.astype(BF)
    da = nt(low, w[...]).astype(BF)
    t0 = at[T] == 0
    mine[...] = head_order(at, jnp.where(t0, da[:, :HALF], da[:, HALF:]))
    send[...] = head_order(at, jnp.where(t0, da[:, HALF:], da[:, :HALF]))
    grad[...] = tn(attended[...], low).astype(BF)
    sums[0:1], sums[1:2] = gain, bias


def self_back(at, triple, da0, da1, valid0, valid1, second0, second1, w_own, w_oth, d0, d1, g_own, g_oth, dt):
    n = second0.shape[0]

    @pl.loop(0, 3)
    def _(p):
        lanes = [pl.ds(pl.multiple_of(i * HALF + p * 128, 128), 128) for i in range(3)]
        for page, (valid, da) in enumerate(((valid0, da0), (valid1, da1))):
            bias = self_bias(valid)
            r = slice(page * n, (page + 1) * n)
            q, k, v = [triple[r, lane] for lane in lanes]
            qq = two_heads(q)
            dd = two_heads(da[:, lanes[0]])
            weight, _l = softmax(nt(qq, k) * SCALE + bias)
            dp = nt(dd, v)
            ds = (weight * (dp - jnp.sum(weight * dp, -1, keepdims=True))).astype(BF)
            grads = (one_pair(mm(ds, k)) * SCALE, tn(ds, qq) * SCALE, tn(weight.astype(BF), dd))
            for i in range(3):
                dt[r, lanes[i]] = grads[i].astype(BF)

    none = jnp.zeros((2 * n, WIDE - 3 * QUART), BF)
    own = jnp.concatenate([dt[:, i * HALF : i * HALF + QUART] for i in range(3)] + [none], 1)
    oth = jnp.concatenate([dt[:, i * HALF + QUART : (i + 1) * HALF] for i in range(3)] + [none], 1)
    rows = jnp.concatenate([second0[...], second1[...]], 0)
    g_own[...] = tn(rows, own).astype(BF).reshape(g_own.shape)
    g_oth[...] = tn(rows, oth).astype(BF).reshape(g_oth.shape)
    d = nt(own, w_own[...]) + nt(oth, w_oth[...])
    d0[...] = d[:n]
    d1[...] = d[n:].astype(BF)


def gate_back(at, d_carried, d0, came, joined, normed, cross, gate, mixed, gains, w_gate, w_out, g_self,
              d_joined, d_mixed, d_normed, keep, send, sums):
    t, c = at[T], at[C]
    rows = keep.shape[2]
    normal, factor = stats(joined[...])
    dx, gain, bias = norm_back(d0[...] + came[...].astype(F32), normal, factor, gain_of(gains, 2))
    dj = d_carried[...] + dx
    d_joined[...] = dj
    sums[0:1], sums[1:2] = gain, bias
    g = gate[...]
    dg = (dj * cross[...].astype(F32) * g * (1.0 - g)).astype(BF)
    d_normed[...] = nt(dg, w_gate[:D])
    dc = (dj * g + nt(dg, w_gate[D:])).astype(BF)
    d_mixed[...] = nt(dc, w_out[...]).astype(BF)
    g_gate = jnp.concatenate([tn(normed[...], dg).astype(BF), tn(cross[...], dg).astype(BF)], 0)
    g_gate = g_gate.reshape(D // rows, 2, rows, D)
    g_out = tn(mixed[...], dc).astype(BF).reshape(D // rows, rows, D)
    g_so = g_self[...].reshape(D // rows, rows, D)
    for tt in range(2):
        for cc in range(2):
            lanes = slice(cc * HALF, (cc + 1) * HALF)
            side = g_out if tt == 0 else g_so
            for out, same in ((keep, True), (send, False)):
                @pl.when((c == cc) == same)
                def _():
                    out[t ^ tt, :, :, :HALF] = g_gate[:, tt, :, lanes]
                    out[t ^ tt, :, :, HALF:] = side[:, :, lanes]


def cross_back(index, at, owner, valid, q, kv, dm, logs, dq, dkv, bias):
    bias[...] = cross_bias(owner, valid)
    pairs = q.shape[1] // 128
    first = (at[C] ^ index) * (pairs // 2)

    @pl.loop(0, pairs // 2)
    def _(i):
        p = first + i
        b = bias[...]
        k, v = kv[:, lanes_at(p)], kv[:, lanes_at(pairs + p)]
        qq, dd = two_heads(q[:, lanes_at(p)]), two_heads(dm[:, lanes_at(p)])
        scores = nt(qq * SCALE, k) + jnp.concatenate([b, b], 0)
        weight = jnp.exp(scores - logs[p])
        dp = nt(dd, v)
        ds = (weight * (dp - jnp.sum(weight * dp, -1, keepdims=True))).astype(BF)
        dq[:, lanes_at(i)] = (one_pair(mm(ds, k)) * SCALE).astype(BF)
        dkv[0, :, lanes_at(i)] = (tn(ds, qq) * SCALE).astype(BF)
        dkv[1, :, lanes_at(i)] = tn(weight.astype(BF), dd).astype(BF)


def cross_weights(at, text_normed, normed, dq, dkv, own, oth, q):
    t0 = at[T] == 0

    @pl.loop(0, 3)
    def _(j):
        lanes = pl.ds(pl.multiple_of(j * 256, 256), 256)
        x = text_normed[:, lanes]
        k, v = tn(x, dkv[0]).astype(BF), tn(x, dkv[1]).astype(BF)
        own[lanes] = jnp.where(t0, k, v)
        oth[lanes] = jnp.where(t0, v, k)
        q[lanes] = tn(normed[:, lanes], dq[...]).astype(BF)


def text_back(at, text, gains, w_kv, own, oth, grad, sums):
    c = at[C]
    d = nt(own[0], w_kv[:, half(c)])
    d = d + nt(oth[0], w_kv[:, half(1 - c)])
    d = d + nt(own[1], w_kv[:, pl.ds(pl.multiple_of(D + c * HALF, 128), HALF)])
    d = d + nt(oth[1], w_kv[:, pl.ds(pl.multiple_of(D + (1 - c) * HALF, 128), HALF)])
    normal, factor = stats(text[...].astype(F32))
    dx, gain, bias = norm_back(d, normal, factor, gain_of(gains, 1))
    grad[...] = dx

    @pl.when(pl.program_id(0) == 0)
    def _():
        sums[...] = jnp.zeros_like(sums)

    sums[0:1] += gain
    sums[1:2] += bias


def visual_back(at, d_normed, dq_own, dq_oth, w_q, visual, d_joined, gains, s1, s2, s3, grad, norms):
    c = at[C]
    depth = norms.shape[0]
    size = 4 * D // (2 * depth)
    d = d_normed[...] + nt(dq_own[...], w_q[:, half(c)]) + nt(dq_oth[...], w_q[:, half(1 - c)])
    normal, factor = stats(visual[...].astype(F32))
    dx, gain, bias = norm_back(d, normal, factor, gain_of(gains, 0))
    grad[...] = d_joined[...] + dx
    g = jnp.concatenate([gain, s1[0:1], s2[0:1], s3[0:1]], 1)
    b = jnp.concatenate([bias, s1[1:2], s2[1:2], s3[1:2]], 1)
    row = lax.broadcasted_iota(jnp.int32, (8, size), 0)
    norms[...] = jnp.zeros_like(norms)
    for s in range(2 * depth):
        lanes = slice(s * size, (s + 1) * size)
        v = jnp.where(row == 0, jnp.broadcast_to(g[:, lanes], (8, size)), jnp.broadcast_to(b[:, lanes], (8, size)))
        norms[s // 2, s % 2, :, :size] = jnp.where(row < 2, v, 0.0).astype(BF)


def finish_ab(at, r, ry, rc, ryc, g_query, g_keyval, gains, biases):
    t, c = at[T], at[C]
    rows, size = g_query.shape[0], gains.shape[0]
    for a, b, cc in ((r, ry, c), (rc, ryc, 1 - c)):
        g_keyval[:, pl.ds(pl.multiple_of(t * D + cc * HALF, 128), HALF)] = a[:rows, :HALF].astype(F32)
        g_keyval[:, pl.ds(pl.multiple_of((1 - t) * D + cc * HALF, 128), HALF)] = b[:rows, :HALF].astype(F32)
        g_query[:, half(cc)] = a[:rows, HALF:].astype(F32) + b[:rows, HALF:].astype(F32)
    norms = [a[rows:, :size].astype(F32) for a in (r, ry, rc, ryc)]
    norms = norms[0] + norms[1] + norms[2] + norms[3]
    gains[...] = norms[0:1].reshape(size)
    biases[...] = norms[1:2].reshape(size)


def in_order(at, groups, lanes):
    c0, t0 = at[C] == 0, at[T] == 0
    own, y, core, both = [r[:, lanes].astype(F32) for r in groups]
    a0, a1 = jnp.where(c0, own, core), jnp.where(c0, core, own)
    b0, b1 = jnp.where(c0, y, both), jnp.where(c0, both, y)
    return jnp.where(t0, a0, b0), jnp.where(t0, a1, b1), jnp.where(t0, b0, a0), jnp.where(t0, b1, a1)


def finish_cd(at, r, ry, rc, ryc, g_qkv, g_up, g_down):
    groups = (r, ry, rc, ryc)
    rows = g_qkv.shape[0]
    p = in_order(at, groups, slice(0, D))
    for i in range(4):
        g_down[i * rows : (i + 1) * rows] = p[i]
    for s in range(D // rows):
        p = in_order(at, groups, slice(D + s * rows, D + (s + 1) * rows))
        g_up[:, s * 4 * rows : (s + 1) * 4 * rows] = jnp.concatenate(p, 1)
    for i in range(3):
        p = in_order(at, groups, slice(2 * D + i * QUART, 2 * D + (i + 1) * QUART))
        g_qkv[:, i * D : (i + 1) * D] = jnp.concatenate(p, 1)


def finish_b(at, r, ry, rc, ryc, g_out, g_gate, g_self):
    groups = (r, ry, rc, ryc)
    rows = g_out.shape[0]
    p = in_order(at, groups, slice(0, HALF))
    for i in range(4):
        g_gate[(i // 2) * rows : (i // 2 + 1) * rows, (i % 2) * HALF : (i % 2 + 1) * HALF] = p[i]
    p = in_order(at, groups, slice(HALF, D))
    g_out[...] = jnp.concatenate(p[:2], 1)
    g_self[...] = jnp.concatenate(p[2:], 1)


def reduce_x(count, extra, lanes, at, *refs):
    out = refs[-1]
    m = extra[0] if extra else 0
    for z in range(out.shape[0]):
        out[z] = reduced(refs, count, m, lanes, z, 1 - at[X]).astype(BF)


def reduced(refs, count, m, lanes, z, side):
    acc = refs[0][z, side, :, lanes].astype(F32)
    for r in refs[1:count]:
        acc = acc + r[z, side, :, lanes].astype(F32)
    if m:
        y = refs[count]
        y = (y[z, side] if len(y.shape) == 4 else y[z]).astype(F32)
        acc = acc + y if y.shape == acc.shape else jnp.concatenate([acc[:, :m] + y, acc[:, m:]], 1)
    return acc


def reduce_z(count, extra, lanes, at, *refs):
    got, keep, send = refs[-3:]
    m = extra[0] if extra else 0
    for i in range(keep.shape[0]):
        for k, out in ((2 * i, keep), (2 * i + 1, send)):
            z = at[Z] ^ k
            out[i] = (reduced(refs, count, m, lanes, z, at[X]) + got[z].astype(F32)).astype(BF)


def reduce_x_proj(at, own, oth, norms, out):
    rows = own.shape[2]
    for z in range(out.shape[0]):
        out[z, :rows] = reduced((own, oth), 1, oth.shape[-1], slice(None), z, 1 - at[X]).astype(BF)
        out[z, rows:] = norms[z, 1 - at[X]]


def reduce_z_proj(at, own, oth, norms, got, keep, send):
    rows = own.shape[2]
    for i in range(keep.shape[0]):
        for k, out in ((2 * i, keep), (2 * i + 1, send)):
            z = at[Z] ^ k
            b = got[z].astype(F32)
            out[i, :rows] = (reduced((own, oth), 1, oth.shape[-1], slice(None), z, at[X]) + b[:rows]).astype(BF)
            out[i, rows:] = (norms[z, at[X]].astype(F32) + b[rows:]).astype(BF)


def reduce_more(at, keep, got, *outs):
    for i in range(keep.shape[0]):
        v = (keep[i].astype(F32) + got[i].astype(F32)).astype(BF)
        if len(outs) == 1:
            outs[0][...] = v
        else:
            outs[i % 2][i // 2] = v


def reduce_last(count, at, *refs):
    out = refs[-1]
    at_lane = 0
    for keep, got in zip(refs[0 : 2 * count : 2], refs[1 : 2 * count : 2]):
        rows, n = keep.shape[1:]
        out[:rows, at_lane : at_lane + n] = (keep[0].astype(F32) + got[0].astype(F32)).astype(BF)
        at_lane += n


def add_core_b(at, keep, came, own, oth_send, oth_keep):
    x = at[X]
    for z in range(own.shape[0]):
        for i in range(2):
            own[z, i] = (keep[0, z, i].astype(F32) + came[0, z, i].astype(F32)).astype(BF)
        oth_send[z] = (keep[1, z, 1 - x].astype(F32) + came[1, z, 1 - x].astype(F32)).astype(BF)
        oth_keep[z] = (keep[1, z, x].astype(F32) + came[1, z, x].astype(F32)).astype(BF)


def add_core_a(at, *refs):
    for keep, came, out in zip(refs[:3], refs[3:6], refs[6:]):
        out[...] = (keep[...].astype(F32) + came[...].astype(F32)).astype(BF)


def add_out(at, carried, y0, came, out):
    out[...] = (carried[...] + y0[...] + came[...].astype(F32)).astype(BF)


def local(reps, shards, visual, text, visual_valid, block_owner, cross_query, cross_keyval, cross_output, gate_weight,
          self_qkv, self_output, ffn_up, ffn_down, norm_gains, norm_biases, cotangent):
    ln = Links(reps, shards)
    at = ln.at
    od = Order()
    run = od.run
    visual, text, cotangent = visual[0], text[0], cotangent[0]
    rows, size = cross_query.shape[0], norm_gains.shape[0]
    vis, txt = visual.shape[0], text.shape[0]
    depth = shards // 2
    w3 = WIDE
    whole = lambda shape: pl.BlockSpec(shape, lambda *_: (0,) * len(shape))
    page = sds((vis, D), F32)
    grid4 = lambda n: (depth, 2, rows, n)

    def far_first(part):
        pieces = {0: part}
        for k in range(depth - 1, 0, -1):
            if k & (k - 1) == 0:
                pieces[k] = od.start(ln.along, part, k)
        return pieces

    def passed_on(pieces):
        for k in sorted(range(1, depth), key=lambda k: (bin(k).count("1"), -k)):
            if k not in pieces:
                od.wait(*[pieces[i] for i in sorted(pieces) if i])
                pieces[k] = od.start(ln.along, pieces[k & (k - 1)], k & -k)
        return [pieces[k] for k in range(depth)]

    (part_a,) = run(pack_a, [sds((rows + 16, D))], at, cross_query, cross_keyval, norm_gains, norm_biases, name="pack_a", far=True)
    pieces_a = far_first(part_a)
    part_b, part_c, part_d, cot = run(
        pack_rest, [sds((rows, D)), sds((rows, w3)), sds((rows, 2 * D)), sds((vis + 8, D))], at,
        cross_output, gate_weight, self_qkv, self_output, ffn_up, ffn_down, cotangent, visual_valid,
        name="pack_rest", far=True)
    d_xo, cot_y = ln.across(part_d), ln.y(cot)
    pieces_a = passed_on(pieces_a)
    od.wait(d_xo, cot_y)
    kv_m, qn_m = run(column_a, [sds((depth, rows, HALF)), sds((depth, rows + 16, HALF))], at, *pieces_a, name="column_a")
    kv_o, qn_o, kv_ym = ln.across(kv_m), ln.across(qn_m), ln.y(kv_m)
    pieces_b = passed_on(far_first(part_b))
    od.wait(kv_o)
    kv_yo = ln.y(kv_o)
    pieces_c = far_first(part_c)
    (b_m,) = run(column, [sds((depth, rows, D))], at, *pieces_b, name="column_b")
    joined_a, gains, biases = run(
        join_a, [sds((3,) + grid4(HALF)), sds((1, 4 * D), F32), sds((1, 4 * D), F32)],
        at, kv_m, kv_o, kv_ym, kv_yo, qn_m, qn_o, name="join_a")
    joined_a = joined_a.reshape(3, D, HALF)
    came_a = ln.core(joined_a)
    b_o, b_ym = od.start(ln.across, b_m), od.start(ln.y, b_m)
    tile = txt // 5
    row_tile = pl.BlockSpec((tile, D), lambda i: (i, 0))
    text_normed, normed = run(
        normed_kernel, [sds((txt, D)), sds((vis, D))], at, text, visual, gains, biases,
        grid=(5,), in_specs=[row_tile, whole((vis, D)), whole((1, 4 * D)), whole((1, 4 * D))],
        out_specs=[row_tile, whole((vis, D))], name="normed", vmem=12)
    pieces_c = passed_on(pieces_c)
    od.wait(came_a)
    pieces_d = far_first(part_d)

    kv, w_kv, w_q, queries = run(
        keyval_kernel, [sds((txt, 2 * D)), sds((D, 2 * D)), sds((D, D)), sds((vis, D))],
        at, text_normed, normed, joined_a, came_a,
        grid=(5,), in_specs=[row_tile, whole((vis, D)), whole((3, D, HALF)), whole((3, D, HALF))],
        out_specs=[pl.BlockSpec((tile, 2 * D), lambda i: (i, 0)), whole((D, 2 * D)), whole((D, D)), whole((vis, D))],
        name="keyval", vmem=30)
    (c_m,) = run(column, [sds((depth, rows, w3))], at, *pieces_c, name="column_c")
    od.wait(b_o, b_ym)
    c_o, b_yo = od.start(ln.across, c_m), od.start(ln.y, b_o)
    pairs = H // 2
    mixed, logs = run(
        cross_fwd, [sds((vis, D)), sds((pairs, 2 * vis, 1), F32)],
        at, block_owner, visual_valid, queries, kv,
        in_specs=[VM, VM, VM, PIN], scratch=[sds((vis, txt), F32)], name="cross_fwd", vmem=16, cost=6)
    od.wait(*[pieces_d[k] for k in sorted(pieces_d) if k])
    d_x = {0: d_xo}
    for k in sorted(pieces_d):
        if k:
            d_x[k] = od.start(ln.across, pieces_d[k])
    pieces_d = passed_on(pieces_d)
    (wc_own,) = run(join, [sds(grid4(w3))], at, c_m, c_o, name="join_c")
    wc_oth = ln.core(wc_own)
    (joined_b,) = run(join_b, [sds((2,) + grid4(D))], at, b_m, b_o, b_ym, b_yo, name="join_b")
    joined_b = joined_b.reshape(2, shards, rows, D)
    came_b = ln.core(joined_b)
    w_out, w_self, w_gate = run(
        place_b, [sds((shards, rows, D)), sds((shards, rows, D)), sds((shards, 2, rows, D))], at, joined_b, came_b, name="place_b")
    w_out, w_self, w_gate = w_out.reshape(D, D), w_self.reshape(D, D), w_gate.reshape(2 * D, D)
    od.wait(wc_oth)
    wc_own, wc_oth = wc_own.reshape(D, w3), wc_oth.reshape(D, w3)
    cross, gate, joined, second = run(
        gate_kernel, [sds((vis, D)), page, page, sds((vis, D))],
        at, mixed, normed, visual, gains, biases, w_out, w_gate, name="gate")
    second_y = ln.y(second)
    d_u, d_d = run(column_halves, [sds((depth, rows, D))] * 2, at, *pieces_d, name="column_d")
    d_cu, d_cd = ln.core(d_u), ln.core(d_d)
    od.wait(*[d_x[k] for k in d_x])
    triple, att_mine, att_send = run(
        self_fwd, [sds((2 * vis, 3 * HALF)), sds((vis, HALF)), sds((vis, HALF))],
        at, second, second_y, cot, cot_y, wc_own, wc_oth, name="self_fwd", cost=3)
    att_came = ln.y(att_send)
    d_cx = {k: od.start(ln.core, d_x[k]) for k in d_x}
    for k in range(depth):
        if k not in d_x:
            d_x[k] = od.start(ln.across, pieces_d[k])
    od.wait(d_cu, d_cd)
    attended, carried, third = run(
        carry_kernel, [sds((vis, D)), page, sds((vis, D))],
        at, att_mine, att_came, joined, gains, biases, w_self, name="carry", cost=3)
    third_y = ln.y(third)
    (wd_own,) = run(join_pieces, [sds(grid4(2 * D))], at, d_u, d_d, *[d_x[k] for k in range(depth)], name="join_d")
    od.wait(third_y)
    for k in range(depth):
        if k not in d_cx:
            d_cx[k] = od.start(ln.core, d_x[k])
    (wd_oth,) = run(join_pieces, [sds(grid4(2 * D))], at, d_cu, d_cd, *[d_cx[k] for k in range(depth)], name="join_d")
    wd_own, wd_oth = wd_own.reshape(D, 2 * D), wd_oth.reshape(D, 2 * D)

    y0, y1, d0, d1, gu_oth, gd_oth = run(
        functools.partial(ffn_kernel, False), [page] * 4 + [sds((D, D))] * 2,
        at, third, third_y, cot, cot_y, wd_oth, name="ffn_first")
    gd_came, gu_came = [ln.core(g).reshape(grid4(D)) for g in (gd_oth, gu_oth)]
    y0, y1, d0, d1, gu_own, gd_own = run(
        functools.partial(ffn_kernel, True), [page, sds((vis, D))] * 2 + [sds((D, D))] * 2,
        at, third, third_y, cot, cot_y, wd_own, y0, y1, d0, d1, name="ffn_second")
    gd_own, gu_own = gd_own.reshape(grid4(D)), gu_own.reshape(grid4(D))
    d1_came = ln.y(d1)

    class Sum:
        def __init__(self, name, arrays, n, lanes=slice(None), sends=(), keeps=(), norms=None):
            self.name, self.n, self.rows = name, n, arrays[0].shape[2]
            extra = [a.shape[-1] for a in keeps]
            first, self.second = [functools.partial(f, len(arrays), extra, lanes) for f in (reduce_x, reduce_z)]
            self.late = list(arrays) + list(keeps)
            early = list(arrays) + list(sends)
            if norms is not None:
                first, self.second, self.rows = reduce_x_proj, reduce_z_proj, self.rows + norms.shape[2]
                self.late, early = self.late + [norms], early + [norms]
            (self.send,) = run(first, [sds((depth, self.rows, n))], at, *early, name="reduce_x_" + name)
            self.bit = 0

        def go(self):
            self.got = od.start(ln.across, self.send)
            return self

        def step(self):
            if self.bit == 0:
                outs = [sds((depth // 2, self.rows, self.n))] * 2
                self.keep, send = run(self.second, outs, at, *self.late, self.got, name="reduce_z_" + self.name)
                self.bit = 1
            elif self.keep.shape[0] > 1:
                outs = [sds((self.keep.shape[0] // 2, self.rows, self.n))] * 2
                self.keep, send = run(reduce_more, outs, at, self.keep, self.got, name="reduce_m_" + self.name)
                self.bit *= 2
            else:
                return False
            self.got = ln.along(send, self.bit)
            return True

    def finish(*sums):
        for one in sums:
            while one.keep.shape[0] > 1:
                one.step()
        ins = [a for one in sums for a in (one.keep, one.got)]
        (total,) = run(functools.partial(reduce_last, len(sums)), [sds((sums[0].rows, sum(one.n for one in sums)))], at,
                       *ins, name="reduce_last")
        for bit in range(2, reps.bit_length() - 1):
            total = (total.astype(F32) + ln.rep_bit(total, 1 << bit).astype(F32)).astype(BF)
        ry = ln.y(total)
        return total, ry, ln.core(total), ln.core(ry)

    def back_half(index):
        return run(
            functools.partial(cross_back, index), [sds((vis, HALF)), sds((2, txt, HALF))],
            at, block_owner, visual_valid, queries, kv, d_mixed, logs,
            in_specs=[VM, VM, VM, PIN, VM, VM], scratch=[sds((vis, txt), F32)], name="cross_back", vmem=20)

    def weights_half(dq, dkv):
        return run(cross_weights, [sds((D, HALF))] * 3, at, text_normed, normed, dq, dkv, name="cross_weights")

    down = Sum("down", [gd_own, gd_came], D).go()
    d_carried, da_mine, da_send, g_self, sums3 = run(
        carry_back, [page, sds((vis, HALF)), sds((vis, HALF)), sds((D, D)), sds((2, D), F32)],
        at, d0, d1_came, carried, cotangent, attended, gains, w_self, name="carry_back")
    da_came = ln.y(da_send)
    up = Sum("up", [gu_own, gu_came], D)
    od.wait(da_came)
    down.step()
    up.go()
    ds0, ds1, gc_own, gc_oth = run(
        self_back, [page, sds((vis, D)), sds(grid4(w3)), sds(grid4(w3))],
        at, triple, da_mine, da_came, cot, cot_y, second, second_y, wc_own, wc_oth,
        scratch=[sds((2 * vis, 3 * HALF))], name="self_back")
    ds1_came = ln.y(ds1)
    gc_came = ln.core(gc_oth)
    down.step()
    up.step()
    d_joined, d_mixed, d_normed, b_keep, b_send, sums2 = run(
        gate_back, [page, sds((vis, D)), page, sds((2, shards, rows, D)), sds((2, shards, rows, D)), sds((2, D), F32)],
        at, d_carried, ds0, ds1_came, joined, normed, cross, gate, mixed, gains, w_gate, w_out, g_self, name="gate_back")
    b_came = ln.core(b_send)
    y1_came = od.start(ln.y, y1)
    dq_oth, dkv_oth = back_half(1)
    qkv = Sum("qkv", [gc_own, gc_came], w3).go()
    od.wait(y1_came)
    own_b, b_ys, b_yk = run(
        add_core_b, [sds(grid4(D)), sds((depth, rows, D)), sds((depth, rows, D))], at,
        b_keep.reshape((2,) + grid4(D)), b_came.reshape((2,) + grid4(D)), name="add_core_b")
    b_ys = ln.y(b_ys)
    od.wait(down.got)
    a_came = [ln.core(a) for a in weights_half(dq_oth, dkv_oth)]
    dq_own, dkv_own = back_half(0)
    up.step()
    gates = Sum("gate", [own_b], D, sends=[b_ys], keeps=[b_yk]).go()
    a_keep = weights_half(dq_own, dkv_own)
    qkv.step()
    own_a, a_y, own_q = run(
        add_core_a, [sds(grid4(HALF))] * 3, at,
        *[a.reshape(grid4(HALF)) for a in (*a_keep, *a_came)], name="add_core_a")
    a_y = ln.y(a_y)
    query = Sum("query", [own_q], HALF).go()
    row3 = pl.BlockSpec((2, tile, HALF), lambda i: (0, i, 0))
    grad_text, sums1 = run(
        text_back, [sds((txt, D), F32), sds((2, D), F32)],
        at, text, gains, w_kv, dkv_own, dkv_oth,
        grid=(5,), in_specs=[row_tile, whole((1, 4 * D)), whole((D, 2 * D)), row3, row3],
        out_specs=[row_tile, whole((2, D))], name="text_back", vmem=24)
    od.wait(up.got, gates.got)
    qkv.step()
    query.step()
    grad_visual, norms = run(
        visual_back, [page, sds((depth, 2, 8, HALF))],
        at, d_normed, dq_own, dq_oth, w_q, visual, d_joined, gains, sums1, sums2, sums3, name="visual_back")
    keyval = Sum("keyval", [own_a], HALF, sends=[a_y], keeps=[a_y], norms=norms).go()
    gates.late[1] = od.start(ln.y, b_yk)
    (layer_out,) = run(add_out, [sds((vis, D))], at, carried, y0, y1_came, name="add_out")
    query.step()
    keyval.step()
    first = finish(down, up, qkv)
    od.wait(query.got)
    keyval.step()
    gates.step()
    out = lambda r, n: sds((r, n), F32)
    last_a = finish(keyval, query)
    gates.step()
    g_qkv, g_up, g_down = run(
        finish_cd, [out(rows, 3 * D), out(rows, 4 * D), out(4 * rows, D)], at, *first, name="finish_cd")
    last_b = finish(gates)
    g_query, g_keyval, g_gains, g_biases = run(
        finish_ab, [out(rows, D), out(rows, 2 * D), sds((size,), F32), sds((size,), F32)], at, *last_a, name="finish_a")
    g_out, g_gate, g_self_out = run(
        finish_b, [out(rows, D), out(2 * rows, D), out(rows, D)], at, *last_b, name="finish_b")
    return (layer_out[None], grad_visual[None], grad_text[None], g_query, g_keyval, g_out, g_gate, g_qkv, g_self_out,
            g_up, g_down, g_gains, g_biases)


def solution(mesh):
    pages = P(("rep", "fsdp"), None, None)
    flags = P(("rep", "fsdp"), None)
    matrix = P("fsdp", None)
    vector = P("fsdp")
    in_specs = (pages, pages, flags, flags) + (matrix,) * 8 + (vector, vector, pages)
    out_specs = (pages, pages, pages) + (matrix,) * 8 + (vector, vector)
    reps, shards = mesh.shape["rep"], mesh.shape["fsdp"]

    def program(*args):
        return local(reps, shards, *args)

    return jax.shard_map(program, mesh=mesh, in_specs=in_specs, out_specs=out_specs, check_vma=False)
```
